32 devices in a mesh: groups: 2 (over x), seq: 8 (over z, y), heads: 2 (over core).
Axes of the slice: x: 2, y: 2, z: 4, core: 2. Of those that a mesh axis runs over, the one named last changes fastest.
Arguments:
- x_in: bfloat16 [2048, 8192], P(('groups', 'seq'), 'heads'), parts along dimension 0, may hold values from -6 to 6
- z_in: bfloat16 [2048, 8192], P(('groups', 'seq'), 'heads'), parts along dimension 0, may hold values from -6 to 6
- bc_in: bfloat16 [2048, 2, 512], P(('groups', 'seq'), None, 'heads'), parts along dimension 0, may hold values from -1.25 to 1.25
- conv_x_weight: bfloat16 [4, 8192], P(None, 'heads'), may hold values from -3 to 3
- conv_x_bias: float32 [8192], P('heads'), may hold values from -3 to 3
- conv_bc_weight: bfloat16 [4, 2, 512], P(None, None, 'heads'), may hold values from -3 to 3
- conv_bc_bias: float32 [2, 512], P(None, 'heads'), may hold values from -0.625 to 0.625
- dt_raw: bfloat16 [2048, 128], P(('groups', 'seq'), 'heads'), parts along dimension 0, may hold values from -3 to 3
- dt_bias: float32 [128], P('heads'), may hold values from -1 to 0.5
- decay: float32 [128], P('heads'), may hold values from 1.953125e-05 to 0.05
- skip_d: float32 [128], P('heads'), may hold values from 0.5 to 1.5
- norm_gain: float32 [8192], P('heads'), may hold values from 0.1 to 1.9
- lengths: int32 [16], P('groups'), parts along dimension 0, may hold values from 1 to 512, 1024 in all
Outputs:
- mixed: bfloat16 [2048, 8192], P(('groups', 'seq'), 'heads'), parts along dimension 0
The draws below stay inside these ranges and needn't reach their ends.
There are 2 independent parts, one for each index of `groups`. The reference program is written for one: setup_inputs(seed, part) draws one part's arguments, and reference() takes and returns one part's arrays. A program takes and returns all parts, laid end to end along the dimension named above; an argument that names none is the same for every part. Nothing has to cross between parts.
Inputs may be any that keep to these rules, and one draw needn't show every extreme that they name: `lengths`: 8 token counts that sum to 1024; the longest rollout has exactly 512 tokens.
All inputs are finite; a program needn't handle non-finite values.
Results may differ from the reference program's by a relative error of at most 0.0098.
Values may be sent and summed in bfloat16 or wider, within the bound.
No kernel may reach another device: no remote copies, remote signals or barrier semaphores. Data moves between devices by JAX's collectives and lax.ppermute only.
A program may use at most 192 MiB of HBM per device.

```python
import math
import jax
import jax.numpy as jnp
import numpy as np
from jax import lax

HEADS = 128
HEAD_DIM = 64
STATE = 128
GROUPS = 4
KW = 4
BLOCK = 128
NSEG = 8
LENGTH = 1024
CHAN = 8192


def levels(rng, shape, shards, least, high):
    def one(dim, blocks):
        draws = jax.random.uniform(jax.random.fold_in(jax.random.fold_in(rng, 6), dim), (blocks,), jnp.float32, least / len(shards), high / len(shards))
        return jnp.repeat(jnp.exp(draws), shape[dim] // blocks).reshape((-1,) + (1,) * (len(shape) - dim - 1))

    factor_of = one(*shards[0])
    for cut in shards[1:]:
        factor_of = factor_of * one(*cut)
    return factor_of


def profile(number_of, total, bound, lean):
    portions = [(1 << 20) // math.isqrt(grade ** lean) + 1 for grade in range(2, number_of + 1)]
    rest, holding = total - bound - (number_of - 1), [1] * (number_of - 1)
    while rest > 0:
        movable = [i for i in range(number_of - 1) if holding[i] < bound]
        whole, budget = sum([portions[i] for i in movable]), rest
        for i in movable:
            addition = min(bound - holding[i], max(1, budget * portions[i] // whole), rest)
            holding[i] = holding[i] + addition
            rest = rest - addition
    return np.array([bound] + holding)


def ragged(key, count, total, bound, slope):
    if count == 2:
        one = jax.random.randint(key, (), max(1, total - bound), min(bound, total - 1) + 1)
        return jnp.stack([one, total - one])
    sizes = jnp.asarray(profile(count, total, bound, slope), jnp.int32)
    pairs = (count - 1) // 2
    donor, receiver = sizes[1:1 + 2 * pairs:2], sizes[2:2 + 2 * pairs:2]
    room = jnp.minimum(donor - 1, bound - receiver)
    shifted = jax.random.randint(jax.random.fold_in(key, 1), (pairs,), 0, 1 << 20) % (room + 1)
    sizes = sizes.at[1:1 + 2 * pairs:2].set(donor - shifted).at[2:2 + 2 * pairs:2].set(receiver + shifted)
    return sizes[jax.random.permutation(jax.random.fold_in(key, 2), count)]


def bell_draw(rng, shape, spread, bound, cuts=(), held_as=jnp.bfloat16):
    result = jax.random.normal(rng, shape, jnp.float32) * spread
    if len(cuts) > 0:
        result = levels(rng, shape, cuts, -0.22, 0.18) * result
    return jnp.clip(result, min=-bound, max=bound).astype(held_as)


def setup_inputs(seed: int = 0, part: int = 0) -> dict:
    arg_keys = jax.random.split(jax.random.key(seed), 14)
    part_splits = jax.random.split(jax.random.fold_in(arg_keys[13], part), 14)
    x_in = bell_draw(part_splits[0], (LENGTH, CHAN), 1.0, 6.0, ((0, 8), (1, 2)))
    z_in = bell_draw(part_splits[1], (LENGTH, CHAN), 1.0, 6.0, ((0, 8), (1, 2)))
    bc_in = bell_draw(part_splits[2], (LENGTH, 2, GROUPS * STATE), 0.2, 1.25, ((0, 8), (2, 2)))
    conv_x_weight = bell_draw(arg_keys[3], (KW, CHAN), KW ** -0.5, 3.0, ((1, 2),))
    conv_x_bias = bell_draw(arg_keys[4], (CHAN,), 0.5, 3.0, ((0, 2),), jnp.float32)
    conv_bc_weight = bell_draw(arg_keys[5], (KW, 2, GROUPS * STATE), KW ** -0.5, 3.0, ((2, 2),))
    conv_bc_bias = bell_draw(arg_keys[6], (2, GROUPS * STATE), 0.1, 0.625, ((1, 2),), jnp.float32)
    dt_raw = bell_draw(part_splits[7], (LENGTH, HEADS), 0.5, 3.0, ((0, 8), (1, 2)))
    dt_bias = jnp.clip(-1.0 + 1.5 * jax.random.uniform(arg_keys[8], (HEADS,), jnp.float32) ** levels(arg_keys[8], (HEADS,), ((0, 2),), -0.2, 0.2), -1.0, 0.5)
    decay = jnp.clip(jnp.exp(math.log(0.05) - 7.8477626 * jax.random.uniform(arg_keys[9], (HEADS,), jnp.float32) ** levels(arg_keys[9], (HEADS,), ((0, 2),), -0.2, 0.2)), 1.9531249563442543e-05, 0.05)
    skip_d = jnp.clip(0.5 + 1.0 * jax.random.uniform(arg_keys[10], (HEADS,), jnp.float32) ** levels(arg_keys[10], (HEADS,), ((0, 2),), -0.2, 0.2), 0.5, 1.5)
    norm_gain = jnp.clip(1.0 + 0.18 * jax.random.normal(arg_keys[11], (CHAN,), jnp.float32), 0.1, 1.9)
    lengths = ragged(part_splits[12], NSEG, LENGTH, LENGTH // 2, 2).astype(jnp.int32)
    return dict(x_in=x_in, z_in=z_in, bc_in=bc_in, conv_x_weight=conv_x_weight, conv_x_bias=conv_x_bias, conv_bc_weight=conv_bc_weight, conv_bc_bias=conv_bc_bias, dt_raw=dt_raw, dt_bias=dt_bias, decay=decay, skip_d=skip_d, norm_gain=norm_gain, lengths=lengths)


def seg_ids(ends, pos):
    count = lax.optimization_barrier(jnp.sum((ends[None, :] <= pos[:, None]).astype(jnp.int32), axis=1))
    return jnp.where(pos >= 0, count, -1).astype(jnp.int32)

def conv_act(extended, weight, bias, keep):
    rows = keep.shape[1]
    total = bias.astype(jnp.float32)
    for k in range(weight.shape[0]):
        piece = extended[k:k + rows].astype(jnp.float32) * weight[k].astype(jnp.float32)
        flag = keep[k].reshape((rows,) + (1,) * (extended.ndim - 1))
        total = total + jnp.where(flag, piece, 0.0)
    return jax.nn.silu(total).astype(jnp.bfloat16)

def contract(form, left, right):
    return jnp.einsum(form, left.astype(jnp.float32), right.astype(jnp.float32), precision=lax.Precision.HIGHEST)

def block_terms(xs, rates, decay, bmat, cmat, seg, prev_seg, block):
    count, heads, hdim = xs.shape
    groups, state = (bmat.shape[1], bmat.shape[2])
    per = heads // groups
    blocks = count // block
    xb = xs.reshape(blocks, block, groups, per, hdim)
    rate_b = rates.reshape(blocks, block, groups, per)
    cum = jnp.cumsum(-rate_b * decay.reshape(groups, per), axis=1)
    segb = seg.reshape(blocks, block)
    bb = bmat.reshape(blocks, block, groups, state)
    cb = cmat.reshape(blocks, block, groups, state)
    scores = contract('btgn,bsgn->bgts', cb, bb)
    order = jnp.arange(block)
    mask = (segb[:, :, None] == segb[:, None, :]) & (order[:, None] >= order[None, :])
    cum_t = jnp.transpose(cum, (0, 2, 3, 1))
    diff = cum_t[..., :, None] - cum_t[..., None, :]
    mask5 = mask[:, None, None]
    decays = jnp.where(mask5, jnp.exp(jnp.where(mask5, diff, 0.0)), 0.0)
    rate_t = jnp.transpose(rate_b, (0, 2, 3, 1))
    weights = (decays * scores[:, :, None] * rate_t[..., None, :]).astype(jnp.bfloat16)
    inner = contract('bgkts,bsgkp->btgkp', weights, xb)
    last = cum[:, -1]
    same_end = segb == segb[:, -1:]
    to_end = jnp.where(same_end[:, :, None, None], jnp.exp(last[:, None] - cum), 0.0) * rate_b
    scaled = (to_end[..., None] * xb.astype(jnp.float32)).astype(jnp.bfloat16)
    states = contract('bsgn,bsgkp->bgknp', bb, scaled)
    live = segb == prev_seg[:, None]
    carry = jnp.where(live[:, -1][:, None, None], jnp.exp(last), 0.0)
    entry = jnp.where(live[:, :, None, None], jnp.exp(cum), 0.0)
    return (inner, states, carry, entry, cb, xb)

def combine(earlier, later):
    return (earlier[0] * later[0], later[0][..., None, None] * earlier[1] + later[1])

def prefix_blocks(carry, states):
    return lax.associative_scan(combine, (carry, states), axis=0)

def finish(pieces, prefix, skip, start):
    inner, states, carry, entry, cb, xb = pieces
    blocks, block, groups, per, hdim = xb.shape
    lead_g = jnp.concatenate([jnp.ones_like(prefix[0][:1]), prefix[0][:-1]], axis=0)
    lead_s = jnp.concatenate([jnp.zeros_like(prefix[1][:1]), prefix[1][:-1]], axis=0)
    entering = (lead_s + lead_g[..., None, None] * start[None]).astype(jnp.bfloat16)
    outer = contract('btgn,bgknp->btgkp', cb, entering) * entry[..., None]
    total = inner + outer + skip.reshape(groups, per)[:, :, None] * xb.astype(jnp.float32)
    return total.reshape(blocks * block, groups * per, hdim).astype(jnp.bfloat16)

def gated_norm(y, gate, gain, gsize):
    rows, width = y.shape
    mixed = y.astype(jnp.float32) * jax.nn.silu(gate.astype(jnp.float32))
    grouped = mixed.reshape(rows, width // gsize, gsize)
    meansq = lax.optimization_barrier(jnp.mean(grouped * grouped, axis=-1, keepdims=True))
    normed = (grouped * lax.rsqrt(meansq + 1e-05)).reshape(rows, width)
    return (normed * gain).astype(jnp.bfloat16)

def reference(x_in, z_in, bc_in, conv_x_weight, conv_x_bias, conv_bc_weight, conv_bc_bias, dt_raw, dt_bias, decay, skip_d, norm_gain, lengths):
    length = x_in.shape[0]
    per = HEADS // GROUPS
    ends = jnp.cumsum(lengths).astype(jnp.int32)
    position = jnp.arange(length, dtype=jnp.int32)
    own = seg_ids(ends, position)
    width = conv_x_weight.shape[0]
    keep = jnp.stack([seg_ids(ends, position - (width - 1) + k) == own for k in range(width)])
    x_ext = jnp.concatenate([jnp.zeros((width - 1,) + x_in.shape[1:], x_in.dtype), x_in], axis=0)
    bc_ext = jnp.concatenate([jnp.zeros((width - 1,) + bc_in.shape[1:], bc_in.dtype), bc_in], axis=0)
    xc = conv_act(x_ext, conv_x_weight, conv_x_bias, keep)
    bcc = conv_act(bc_ext, conv_bc_weight, conv_bc_bias, keep)
    rates = jax.nn.softplus(dt_raw.astype(jnp.float32) + dt_bias)
    prev_seg = seg_ids(ends, jnp.arange(length // BLOCK, dtype=jnp.int32) * BLOCK - 1)
    xh = xc.reshape(length, GROUPS, per, HEAD_DIM)
    bm = bcc[:, 0].reshape(length, GROUPS, STATE)
    cm = bcc[:, 1].reshape(length, GROUPS, STATE)
    rate_g = rates.reshape(length, GROUPS, per)
    decay_g = decay.reshape(GROUPS, per)
    skip_g = skip_d.reshape(GROUPS, per)

    def one_group(index):
        xs = lax.dynamic_index_in_dim(xh, index, 1, keepdims=False)
        rs = lax.dynamic_index_in_dim(rate_g, index, 1, keepdims=False)
        bsel = lax.dynamic_index_in_dim(bm, index, 1, keepdims=True)
        csel = lax.dynamic_index_in_dim(cm, index, 1, keepdims=True)
        dsel = lax.dynamic_index_in_dim(decay_g, index, 0, keepdims=False)
        ksel = lax.dynamic_index_in_dim(skip_g, index, 0, keepdims=False)
        pieces = block_terms(xs, rs, dsel, bsel, csel, own, prev_seg, BLOCK)
        prefix = prefix_blocks(pieces[2], pieces[1])
        start = jnp.zeros((1, per, STATE, HEAD_DIM), jnp.float32)
        return finish(pieces, prefix, ksel, start)
    outs = lax.map(one_group, jnp.arange(GROUPS, dtype=jnp.int32))
    y = jnp.transpose(outs, (1, 0, 2, 3)).reshape(length, HEADS * HEAD_DIM)
    return gated_norm(y, z_in, norm_gain, HEADS * HEAD_DIM // GROUPS)
```

```python
import functools

import jax
import jax.numpy as jnp
from jax import lax
from jax.experimental import pallas as pl
from jax.experimental.pallas import tpu as pltpu
from jax.sharding import PartitionSpec as P

HEAD_DIM = 64
STATE = 128
BLOCK = 128
QUAD = 4
HALO = 16
EXTRA = 16
F32 = jnp.float32
BF16 = jnp.bfloat16


def mm(left, right):
    return jnp.dot(left, right, preferred_element_type=F32)


def ends_of(lens_ref):
    total = 0
    ends = []
    for i in range(lens_ref.shape[0]):
        total = total + lens_ref[i]
        ends.append(total)
    return ends


def seg_of(pos, ends):
    count = 0
    for end in ends:
        count = count + jnp.where(end <= pos, 1, 0)
    return jnp.where(pos >= 0, count, -1)


def tokens(start, shape, dim):
    return start + lax.broadcasted_iota(jnp.int32, shape, dim)


def shift_matrix(start, ends, taps):
    shape = (BLOCK, HALO + BLOCK)
    row = lax.broadcasted_iota(jnp.int32, shape, 0)
    col = lax.broadcasted_iota(jnp.int32, shape, 1)
    same = seg_of(start + row, ends) == seg_of(start - HALO + col, ends)
    parts = []
    for k in range(taps - 1):
        parts.append(jnp.where((col == row + (HALO - taps + 1 + k)) & same, 1.0, 0.0))
    return jnp.concatenate(parts, axis=0).astype(BF16)


def conv_half(shift, halo, block, weight, bias):
    taps = weight.shape[0]
    half = weight.astype(F32) * 0.5
    moved = mm(shift, jnp.concatenate([halo, block], axis=0))
    total = bias * 0.5 + block.astype(F32) * half[taps - 1 : taps]
    for k in range(taps - 1):
        total = total + moved[k * BLOCK : (k + 1) * BLOCK] * half[k : k + 1]
    return total


def silu_of_half(half):
    return half + half * jnp.tanh(half)


def rates_of(dt_ref, dtb_ref, dec_ref):
    raw = jnp.transpose(dt_ref[...].astype(F32)) + dtb_ref[...]
    rate = jnp.maximum(raw, 0.0) + jnp.log1p(jnp.exp(-jnp.abs(raw)))
    shape = (BLOCK, BLOCK)
    lower = lax.broadcasted_iota(jnp.int32, shape, 0) >= lax.broadcasted_iota(jnp.int32, shape, 1)
    cum = jnp.dot(
        jnp.where(lower, 1.0, 0.0),
        -rate * dec_ref[...],
        precision=lax.Precision.HIGHEST,
        preferred_element_type=F32,
    )
    return rate, cum


def head_map(heads, first, width):
    shape = (heads, width)
    row = lax.broadcasted_iota(jnp.int32, shape, 0)
    col = lax.broadcasted_iota(jnp.int32, shape, 1)
    return jnp.where(row == first + col // HEAD_DIM, 1.0, 0.0).astype(BF16)


def pair_of(value):
    high = value.astype(BF16)
    low = (value - high.astype(F32)).astype(BF16)
    return high, low


def spread(value, onehot2):
    high, low = pair_of(value)
    return mm(jnp.concatenate([high, low], axis=1), onehot2)


def state_kernel(k, info, lens, x, halo, b_in, halo_b, wx, bx, wb, bb, dt, dtb, dec, msg, xc_out):
    start = info[0] * BLOCK
    quarter = info[1] ^ k
    width = x.shape[1]
    heads = dt.shape[0]
    ends = ends_of(lens)
    shift = shift_matrix(start, ends, wx.shape[0])
    xc = silu_of_half(conv_half(shift, halo[...], x[...], wx[...], bx[...])).astype(BF16)
    xc_out[...] = xc
    bmat = silu_of_half(conv_half(shift, halo_b[...], b_in[...], wb[...], bb[...]))
    bmat_t = jnp.transpose(bmat).astype(BF16)
    rate, cum = rates_of(dt, dtb, dec)
    last = cum[BLOCK - 1 : BLOCK]
    seg_last = seg_of(start + BLOCK - 1, ends)
    same = seg_of(tokens(start, (BLOCK, heads), 0), ends) == seg_last
    factor = jnp.where(same, jnp.exp(last - cum), 0.0) * rate
    onehot = head_map(heads, quarter * (width // HEAD_DIM), width)
    scaled = (xc.astype(F32) * spread(factor, jnp.concatenate([onehot, onehot], axis=0))).astype(BF16)
    msg[0:STATE, :] = mm(bmat_t, scaled).astype(BF16)
    live = seg_last == seg_of(start - 1, ends)
    carry = jnp.where(live, jnp.exp(last), 0.0)
    high, low = pair_of(carry)
    row = lax.broadcasted_iota(jnp.int32, (EXTRA, heads), 0)
    rows = jnp.where(row == 0, high.astype(F32), jnp.where(row == 1, low.astype(F32), 0.0))
    msg[STATE : STATE + EXTRA, :] = mm(rows.astype(BF16), onehot).astype(BF16)


def carry_of(msg):
    return msg[STATE : STATE + 1, :].astype(F32) + msg[STATE + 1 : STATE + 2, :].astype(F32)


def fold_kernel(info, m0, m1, m2, m3, total, decay):
    msgs = (m0, m1, m2, m3)
    for mine in range(QUAD):

        @pl.when(info[1] == mine)
        def _():
            block = [msgs[mine ^ b] for b in range(QUAD)]
            state = block[0][0:STATE, :].astype(F32)
            through = carry_of(block[0])
            for b in range(1, QUAD):
                carry = carry_of(block[b])
                state = block[b][0:STATE, :].astype(F32) + carry * state
                through = through * carry
            total[...] = state.astype(BF16)
            decay[...] = jnp.broadcast_to(through, decay.shape)


def enter_kernel(info, start, m0, m1, m2, m3, o0, o1, o2, o3):
    msgs = (m0, m1, m2, m3)
    outs = (o0, o1, o2, o3)
    for mine in range(QUAD):

        @pl.when(info[1] == mine)
        def _():
            outs[mine][...] = start[...]
            state = start[...].astype(F32)
            for b in range(1, QUAD):
                prev = msgs[mine ^ (b - 1)]
                state = prev[0:STATE, :].astype(F32) + carry_of(prev) * state
                outs[mine ^ b][...] = state.astype(BF16)


def inner_kernel(
    k, info, lens, xc, z, b_in, c_in, halo_b, halo_c, wb, wc, bb, bc, dt, dtb, dec, skip, near, gain, c_out
):
    start = info[0] * BLOCK
    quarter = info[1] ^ k
    width = xc.shape[1]
    heads = dt.shape[0]
    ends = ends_of(lens)
    shift = shift_matrix(start, ends, wb.shape[0])
    bmat = silu_of_half(conv_half(shift, halo_b[...], b_in[...], wb[...], bb[...])).astype(BF16)
    cmat = silu_of_half(conv_half(shift, halo_c[...], c_in[...], wc[...], bc[...])).astype(BF16)
    c_out[...] = cmat
    rate, cum = rates_of(dt, dtb, dec)
    shape = (BLOCK, BLOCK)
    row = lax.broadcasted_iota(jnp.int32, shape, 0)
    col = lax.broadcasted_iota(jnp.int32, shape, 1)
    mask = (row >= col) & (seg_of(start + row, ends) == seg_of(start + col, ends))
    scores = lax.dot_general(cmat, bmat, (((1,), (1,)), ((), ())), preferred_element_type=F32)
    scores = jnp.where(mask, scores, 0.0).astype(BF16)
    onehot = head_map(heads, quarter * (width // HEAD_DIM), width)
    onehot2 = jnp.concatenate([onehot, onehot], axis=0)
    xf = xc[...].astype(F32)
    scaled = (xf * spread(rate * jnp.exp(-cum), onehot2)).astype(BF16)
    grown = jnp.exp(cum)
    grown_c = spread(grown, onehot2)
    skip_c = spread(jnp.broadcast_to(skip[...], (8, heads)), onehot2)[0:1]
    zf = z[...].astype(F32) * 0.5
    gate = silu_of_half(zf)
    near[...] = (mm(scores, scaled) * grown_c + skip_c * xf) * gate
    live = seg_of(tokens(start, (BLOCK, width), 0), ends) == seg_of(start - 1, ends)
    gain[...] = jnp.where(live, grown_c * gate, 0.0)


def finish_kernel(k, info, near0, near1, gain0, gain1, e0, e1, cmat, scale, *rest):
    out = rest[-1]
    width = near0.shape[1]
    c = cmat[...]
    first = near0[...] + gain0[...] * mm(c, e0[...])
    second = near1[...] + gain1[...] * mm(c, e1[...])
    square = jnp.sum(first * first, axis=1, keepdims=True) + jnp.sum(second * second, axis=1, keepdims=True)
    inv = lax.rsqrt(square * (1.0 / (2 * width)) + 1e-05)
    low = ((info[1] ^ k) & 1) == 0
    for mine in range(2):

        @pl.when(low == (mine == 0))
        def _():
            a = slice(mine * width, (mine + 1) * width)
            b = slice((1 - mine) * width, (2 - mine) * width)
            out[:, a] = (first * inv * scale[:, a]).astype(BF16)
            out[:, b] = (second * inv * scale[:, b]).astype(BF16)


def call(kernel, scalars, grid_in, outs, specs_in, specs_out, args, flops, aliases=None, limit=None):
    nbytes = 4 << 20
    return pl.pallas_call(
        kernel,
        grid_spec=pltpu.PrefetchScalarGridSpec(
            num_scalar_prefetch=len(scalars), grid=grid_in, in_specs=specs_in, out_specs=specs_out
        ),
        out_shape=outs,
        input_output_aliases=aliases or {},
        cost_estimate=pl.CostEstimate(flops=flops, bytes_accessed=nbytes, transcendentals=0),
        compiler_params=pltpu.CompilerParams(vmem_limit_bytes=limit or (32 << 20)),
    )(*scalars, *args)


def shards(
    x_in,
    z_in,
    bc_in,
    conv_x_weight,
    conv_x_bias,
    conv_bc_weight,
    conv_bc_bias,
    dt_raw,
    dt_bias,
    decay,
    skip_d,
    norm_gain,
    lengths,
):
    rows, chan = x_in.shape
    heads = dt_raw.shape[1]
    peers = lax.axis_size("seq")
    shard = lax.axis_index("seq").astype(jnp.int32)
    taps = conv_x_weight.shape[0]
    width = chan // QUAD
    groups = bc_in.shape[2] // STATE
    per_group = QUAD // groups
    bcw = bc_in.shape[2]
    reach = peers // 2 // QUAD

    bc2 = bc_in.reshape(rows, 2 * bcw)
    wbc = conv_bc_weight.reshape(taps, 2 * bcw)
    bbc = conv_bc_bias.reshape(1, 2 * bcw)
    bx = conv_x_bias.reshape(1, chan)
    gain = norm_gain.reshape(1, chan)
    dt_t = dt_raw.T
    dtb = dt_bias.reshape(1, heads)
    dec = decay.reshape(1, heads)
    skip = skip_d.reshape(1, heads)
    info = jnp.stack([shard, shard % QUAD])

    edge = jnp.concatenate([x_in[rows - HALO :], bc2[rows - HALO :]], axis=1)
    edge = lax.ppermute(edge, "seq", [(i, (i + 1) % peers) for i in range(peers)])
    scalars = (info, lengths)

    def spec(shape, col):
        return pl.BlockSpec(shape, lambda i, info, *_: (0, col(info)))

    def whole(shape):
        return pl.BlockSpec(shape, lambda i, *_: (0, 0))

    def at(k):
        return lambda info: info[1] ^ k

    def group_at(k, base):
        return lambda info: base + (info[1] ^ k) // per_group

    rate_specs = [whole((heads, rows)), whole((1, heads)), whole((1, heads))]
    rate_args = [dt_t, dtb, dec]
    xw = width // STATE * QUAD

    def state(k):
        return call(
            functools.partial(state_kernel, k),
            scalars,
            (1,),
            [jax.ShapeDtypeStruct((STATE + EXTRA, width), BF16), jax.ShapeDtypeStruct((rows, width), BF16)],
            [
                spec((rows, width), at(k)),
                spec((HALO, width), at(k)),
                spec((rows, STATE), group_at(k, 0)),
                spec((HALO, STATE), group_at(k, xw)),
                spec((taps, width), at(k)),
                spec((1, width), at(k)),
                spec((taps, STATE), group_at(k, 0)),
                spec((1, STATE), group_at(k, 0)),
                *rate_specs,
            ],
            [whole((STATE + EXTRA, width)), whole((rows, width))],
            [x_in, edge, bc2, edge, conv_x_weight, bx, wbc, bbc, *rate_args],
            400_000_000,
        )

    def inner(k, xc):
        return call(
            functools.partial(inner_kernel, k),
            scalars,
            (1,),
            [
                jax.ShapeDtypeStruct((rows, width), F32),
                jax.ShapeDtypeStruct((rows, width), F32),
                jax.ShapeDtypeStruct((rows, STATE), BF16),
            ],
            [
                whole((rows, width)),
                spec((rows, width), at(k)),
                spec((rows, STATE), group_at(k, 0)),
                spec((rows, STATE), group_at(k, groups)),
                spec((HALO, STATE), group_at(k, xw)),
                spec((HALO, STATE), group_at(k, xw + groups)),
                spec((taps, STATE), group_at(k, 0)),
                spec((taps, STATE), group_at(k, groups)),
                spec((1, STATE), group_at(k, 0)),
                spec((1, STATE), group_at(k, groups)),
                *rate_specs,
                whole((1, heads)),
            ],
            [whole((rows, width)), whole((rows, width)), whole((rows, STATE))],
            [xc, z_in, bc2, bc2, edge, edge, wbc, wbc, bbc, bbc, *rate_args, skip],
            400_000_000,
        )

    def swap(value, k):
        return lax.ppermute(value, "seq", [(i, i ^ k) for i in range(peers)])

    def ahead(value):
        return lax.ppermute(value, "seq", [(i, (i + QUAD) % peers) for i in range(peers)])

    msgs, xcs = [None] * QUAD, [None] * QUAD
    for k in (3, 2, 1, 0):
        msgs[k], xcs[k] = state(k)
        if k:
            msgs[k] = swap(msgs[k], k)

    locals_ = [inner(k, xcs[k]) for k in range(QUAD)]

    msg_spec = whole((STATE + EXTRA, width))
    state_spec = whole((STATE, width))
    total, through = call(
        fold_kernel,
        (info,),
        (1,),
        [jax.ShapeDtypeStruct((STATE, width), BF16), jax.ShapeDtypeStruct((8, width), F32)],
        [msg_spec] * QUAD,
        [state_spec, whole((8, width))],
        msgs,
        1_000_000,
    )
    entering = ahead(total)
    for _ in range(reach - 1):
        entering = ahead((total.astype(F32) + through[0:1] * entering.astype(F32)).astype(BF16))
    enter = call(
        enter_kernel,
        (info,),
        (1,),
        [jax.ShapeDtypeStruct((STATE, width), BF16)] * QUAD,
        [state_spec] + [msg_spec] * QUAD,
        [state_spec] * QUAD,
        [entering, *msgs],
        1_000_000,
    )
    enter = [enter[0]] + [swap(enter[k], k) for k in range(1, QUAD)]

    out = None
    for p in range(groups):
        k = 2 * p
        args = [
            locals_[k][0], locals_[k + 1][0], locals_[k][1], locals_[k + 1][1], enter[k], enter[k + 1],
            locals_[k][2], gain,
        ]
        specs = [whole((rows, width))] * 4 + [state_spec] * 2
        specs += [whole((rows, STATE)), spec((1, 2 * width), group_at(k, 0))]
        aliases = {}
        if out is not None:
            aliases = {1 + len(args): 0}
            args.append(out)
            specs.append(pl.BlockSpec(memory_space=pl.ANY))
        out = call(
            functools.partial(finish_kernel, k),
            (info,),
            (1,),
            jax.ShapeDtypeStruct((rows, chan), BF16),
            specs,
            spec((rows, 2 * width), group_at(k, 0)),
            args,
            200_000_000,
            aliases,
        )
    return out


def solution(mesh):
    return jax.shard_map(
        shards,
        mesh=mesh,
        in_specs=(
            P(("groups", "seq"), "heads"),
            P(("groups", "seq"), "heads"),
            P(("groups", "seq"), None, "heads"),
            P(None, "heads"),
            P("heads"),
            P(None, None, "heads"),
            P(None, "heads"),
            P(("groups", "seq"), "heads"),
            P("heads"),
            P("heads"),
            P("heads"),
            P("heads"),
            P("groups"),
        ),
        out_specs=P(("groups", "seq"), "heads"),
        check_vma=False,
    )
```

```python
import functools

import jax
import jax.numpy as jnp
from jax import lax
from jax.experimental import pallas as pl
from jax.experimental.pallas import tpu as pltpu
from jax.sharding import PartitionSpec as P

HEAD_DIM = 64
STATE = 128
BLOCK = 128
QUAD = 4
HALO = 16
EXTRA = 16
F32 = jnp.float32
BF16 = jnp.bfloat16


def mm(left, right):
    return jnp.dot(left, right, preferred_element_type=F32)


def ends_of(lens_ref):
    total = 0
    ends = []
    for i in range(lens_ref.shape[0]):
        total = total + lens_ref[i]
        ends.append(total)
    return ends


def seg_of(pos, ends):
    count = 0
    for end in ends:
        count = count + jnp.where(end <= pos, 1, 0)
    return jnp.where(pos >= 0, count, -1)


def tokens(start, shape, dim):
    return start + lax.broadcasted_iota(jnp.int32, shape, dim)


def shift_matrix(start, ends, rows, before, taps):
    shape = (rows, before + rows)
    row = lax.broadcasted_iota(jnp.int32, shape, 0)
    col = lax.broadcasted_iota(jnp.int32, shape, 1)
    same = seg_of(start + row, ends) == seg_of(start - before + col, ends)
    parts = []
    for k in range(taps - 1):
        parts.append(jnp.where((col == row + (before - taps + 1 + k)) & same, 1.0, 0.0))
    return jnp.concatenate(parts, axis=0).astype(BF16)


def conv_half(shift, extended, block, weight, bias):
    rows = block.shape[0]
    taps = weight.shape[0]
    half = weight.astype(F32) * 0.5
    moved = mm(shift, extended)
    total = bias * 0.5 + block.astype(F32) * half[taps - 1 : taps]
    for k in range(taps - 1):
        total = total + moved[k * rows : (k + 1) * rows] * half[k : k + 1]
    return total


def silu_of_half(half):
    return half + half * jnp.tanh(half)


def rates_of(dt_ref, dtb_ref, dec_ref):
    raw = jnp.transpose(dt_ref[...].astype(F32)) + dtb_ref[...]
    rate = jnp.maximum(raw, 0.0) + jnp.log1p(jnp.exp(-jnp.abs(raw)))
    shape = (BLOCK, BLOCK)
    lower = lax.broadcasted_iota(jnp.int32, shape, 0) >= lax.broadcasted_iota(jnp.int32, shape, 1)
    cum = jnp.dot(
        jnp.where(lower, 1.0, 0.0),
        -rate * dec_ref[...],
        precision=lax.Precision.HIGHEST,
        preferred_element_type=F32,
    )
    return rate, cum


def head_map(heads, first, width):
    shape = (heads, width)
    row = lax.broadcasted_iota(jnp.int32, shape, 0)
    col = lax.broadcasted_iota(jnp.int32, shape, 1)
    return jnp.where(row == first + col // HEAD_DIM, 1.0, 0.0).astype(BF16)


def pair_of(value):
    high = value.astype(BF16)
    low = (value - high.astype(F32)).astype(BF16)
    return jnp.concatenate([high, low], axis=1)


def twice(onehot):
    return jnp.concatenate([onehot, onehot], axis=0)


def early_kernel(info, lens, x, bc, wx, bx, wbc, bbc, dt, dtb, dec, xc_out, part, first, carries, factors):
    start = info[0] * BLOCK
    heads = dt.shape[0]
    chan = x.shape[1]
    inner = bc.shape[1] // 2
    groups = inner // STATE
    ends = ends_of(lens)
    shift = shift_matrix(start, ends, BLOCK, 0, wx.shape[0])
    b_in = bc[:, 0:inner]
    bmat = silu_of_half(conv_half(shift, b_in, b_in, wbc[:, 0:inner], bbc[:, 0:inner]))
    bmat = jnp.where(tokens(0, bmat.shape, 0) >= HALO, bmat, 0.0)
    bmat_t = jnp.transpose(bmat).astype(BF16)
    rate, cum = rates_of(dt, dtb, dec)
    last = cum[BLOCK - 1 : BLOCK]
    seg_last = seg_of(start + BLOCK - 1, ends)
    same = seg_of(tokens(start, (BLOCK, heads), 0), ends) == seg_last
    factor = pair_of(jnp.where(same, jnp.exp(last - cum), 0.0) * rate)
    factors[:, 0 : 2 * heads] = pair_of(rate * jnp.exp(-cum))
    factors[:, 2 * heads : 4 * heads] = pair_of(jnp.exp(cum))
    live = seg_last == seg_of(start - 1, ends)
    carry = pair_of(jnp.where(live, jnp.exp(last), 0.0)).astype(F32)
    row = lax.broadcasted_iota(jnp.int32, (EXTRA, heads), 0)
    rows = jnp.where(row == 0, carry[:, 0:heads], jnp.where(row == 1, carry[:, heads:], 0.0)).astype(BF16)
    step = 1024
    for at in range(0, chan, step):
        lane = slice(at, at + step)
        g = at // (chan // groups)
        xs = x[:, lane]
        xc = silu_of_half(conv_half(shift, xs, xs, wx[:, lane], bx[:, lane])).astype(BF16)
        xc_out[:, lane] = xc
        onehot = head_map(heads, at // HEAD_DIM, step)
        spread = mm(factor, twice(onehot))
        first[:, lane] = spread[0:HALO]
        carries[:, lane] = mm(rows, onehot).astype(BF16)
        part[:, lane] = mm(bmat_t[g * STATE : (g + 1) * STATE], (xc.astype(F32) * spread).astype(BF16))


def late_kernel(g, info, lens, x, bc, halo, wx, bx, wbc, bbc, part, first, carries, m0, m1, m2, m3, xc_out):
    start = info[0] * BLOCK
    mine = info[1]
    chan = x.shape[1]
    groups = bc.shape[1] // 2 // STATE
    wide = chan // groups
    width = wide // QUAD
    ends = ends_of(lens)
    shift = shift_matrix(start, ends, HALO, HALO, wx.shape[0])
    lane = slice(g * STATE, (g + 1) * STATE)
    top = bc[0:HALO, lane]
    ext = jnp.concatenate([halo[:, chan + g * STATE : chan + (g + 1) * STATE], top], axis=0)
    bmat = silu_of_half(conv_half(shift, ext, top, wbc[:, lane], bbc[:, lane])).astype(BF16)
    for k, msg in enumerate((m0, m1, m2, m3)):
        inside = pl.multiple_of((mine ^ k) * width, width)
        at = pl.ds(pl.multiple_of(g * wide + inside, width), width)
        top = x[0:HALO, at]
        ext = jnp.concatenate([halo[:, at], top], axis=0)
        xc = silu_of_half(conv_half(shift, ext, top, wx[:, at], bx[:, at])).astype(BF16)
        xc_out[:, pl.ds(inside, width)] = xc
        scaled = (xc.astype(F32) * first[:, at]).astype(BF16)
        add = lax.dot_general(bmat, scaled, (((0,), (0,)), ((), ())), preferred_element_type=F32)
        msg[0:STATE, :] = (part[:, at] + add).astype(BF16)
        msg[STATE : STATE + EXTRA, :] = carries[:, at]


def carry_of(msg):
    return msg[STATE : STATE + 1, :].astype(F32) + msg[STATE + 1 : STATE + 2, :].astype(F32)


def fold_kernel(info, m0, m1, m2, m3, total, decay):
    msgs = (m0, m1, m2, m3)
    for mine in range(QUAD):

        @pl.when(info[1] == mine)
        def _():
            block = [msgs[mine ^ b] for b in range(QUAD)]
            state = block[0][0:STATE, :].astype(F32)
            through = carry_of(block[0])
            for b in range(1, QUAD):
                carry = carry_of(block[b])
                state = block[b][0:STATE, :].astype(F32) + carry * state
                through = through * carry
            total[...] = state.astype(BF16)
            decay[...] = jnp.broadcast_to(through, decay.shape)


def enter_kernel(info, start, m0, m1, m2, m3, o0, o1, o2, o3):
    msgs = (m0, m1, m2, m3)
    outs = (o0, o1, o2, o3)
    for mine in range(QUAD):

        @pl.when(info[1] == mine)
        def _():
            outs[mine][...] = start[...]
            state = start[...].astype(F32)
            for b in range(1, QUAD):
                prev = msgs[mine ^ (b - 1)]
                state = prev[0:STATE, :].astype(F32) + carry_of(prev) * state
                outs[mine ^ b][...] = state.astype(BF16)


def inner_kernel(g, info, lens, xc_in, xc_top, z, bc, halo, wbc, bbc, factors, skip, near, gain, c_out):
    start = info[0] * BLOCK
    chan = xc_in.shape[1]
    inner = bc.shape[1] // 2
    groups = inner // STATE
    wide = chan // groups
    heads = skip.shape[1]
    ends = ends_of(lens)
    shift = shift_matrix(start, ends, BLOCK, HALO, wbc.shape[0])

    def conv(base):
        lane = slice(base, base + STATE)
        block = bc[:, lane]
        ext = jnp.concatenate([halo[:, chan + base : chan + base + STATE], block], axis=0)
        return silu_of_half(conv_half(shift, ext, block, wbc[:, lane], bbc[:, lane])).astype(BF16)

    bmat = conv(g * STATE)
    cmat = conv(inner + g * STATE)
    c_out[...] = cmat
    shape = (BLOCK, BLOCK)
    row = lax.broadcasted_iota(jnp.int32, shape, 0)
    col = lax.broadcasted_iota(jnp.int32, shape, 1)
    mask = (row >= col) & (seg_of(start + row, ends) == seg_of(start + col, ends))
    scores = lax.dot_general(cmat, bmat, (((1,), (1,)), ((), ())), preferred_element_type=F32)
    scores = jnp.where(mask, scores, 0.0).astype(BF16)
    skips = pair_of(jnp.broadcast_to(skip[...], (8, heads)))
    step = 1024
    live = seg_of(tokens(start, (BLOCK, step), 0), ends) == seg_of(start - 1, ends)
    for at in range(0, wide, step):
        lane = slice(at, at + step)
        deep = slice(g * wide + at, g * wide + at + step)
        onehot2 = twice(head_map(heads, (g * wide + at) // HEAD_DIM, step))
        xf = jnp.concatenate([xc_top[:, lane], xc_in[HALO:, deep]], axis=0).astype(F32)
        scaled = (xf * mm(factors[:, 0 : 2 * heads], onehot2)).astype(BF16)
        grown = mm(factors[:, 2 * heads : 4 * heads], onehot2)
        skip_c = mm(skips, onehot2)[0:1]
        gate = silu_of_half(z[:, deep].astype(F32) * 0.5)
        near[:, lane] = (mm(scores, scaled) * grown + skip_c * xf) * gate
        gain[:, lane] = jnp.where(live, grown * gate, 0.0)


def finish_kernel(g, info, near, gain, e0, e1, e2, e3, cmat, scale, *rest):
    out, held, sem = rest[-3:]
    mine = info[1]
    wide = near.shape[1]
    width = wide // QUAD
    c = cmat[...]
    values = []
    square = 0.0
    for k, e in enumerate((e0, e1, e2, e3)):
        at = pl.ds(pl.multiple_of((mine ^ k) * width, width), width)
        value = near[:, at] + gain[:, at] * mm(c, e[...])
        square = square + jnp.sum(value * value, axis=1, keepdims=True)
        values.append((at, value))
    inv = lax.rsqrt(square * (1.0 / wide) + 1e-05)
    for k, (at, value) in enumerate(values):
        deep = pl.ds(pl.multiple_of(g * wide + (mine ^ k) * width, width), width)
        held[:, at] = (value * inv * scale[:, deep]).astype(BF16)
    copy = pltpu.make_async_copy(held, out.at[:, g * wide : (g + 1) * wide], sem)
    copy.start()
    copy.wait()


SMEM = pl.BlockSpec(memory_space=pltpu.SMEM)
VMEM = pl.BlockSpec(memory_space=pltpu.VMEM)
ANY = pl.BlockSpec(memory_space=pl.ANY)


def call(kernel, scalars, args, outs, flops, **more):
    return pl.pallas_call(
        kernel,
        in_specs=[SMEM] * len(scalars) + more.pop("specs", [VMEM] * len(args)),
        out_specs=more.pop("out_specs", [VMEM] * len(outs)),
        out_shape=[jax.ShapeDtypeStruct(*out) for out in outs],
        cost_estimate=pl.CostEstimate(flops=flops, bytes_accessed=4 << 20, transcendentals=0),
        compiler_params=pltpu.CompilerParams(vmem_limit_bytes=32 << 20),
        **more,
    )(*scalars, *args)


def tie(first, second):
    return lax.optimization_barrier((first, second))


def shards(
    x_in,
    z_in,
    bc_in,
    conv_x_weight,
    conv_x_bias,
    conv_bc_weight,
    conv_bc_bias,
    dt_raw,
    dt_bias,
    decay,
    skip_d,
    norm_gain,
    lengths,
):
    rows, chan = x_in.shape
    heads = dt_raw.shape[1]
    peers = lax.axis_size("seq")
    shard = lax.axis_index("seq").astype(jnp.int32)
    taps = conv_x_weight.shape[0]
    bcw = bc_in.shape[2]
    groups = bcw // STATE
    wide = chan // groups
    width = wide // QUAD
    reach = peers // 2 // QUAD

    bc = bc_in.reshape(rows, 2 * bcw)
    wbc = conv_bc_weight.reshape(taps, 2 * bcw)
    bbc = conv_bc_bias.reshape(1, 2 * bcw)
    bx = conv_x_bias.reshape(1, chan)
    scale = norm_gain.reshape(1, chan)
    info = jnp.stack([shard, shard % QUAD])
    both = (info, lengths)

    halo = jnp.concatenate([x_in[rows - HALO :], bc[rows - HALO :]], axis=1)
    halo = lax.ppermute(halo, "seq", [(i, (i + 1) % peers) for i in range(peers)])

    def swap(values):
        routes = [[(i, i ^ k) for i in range(peers)] for k in range(QUAD)]
        swapped = {k: lax.ppermute(values[k], "seq", routes[k]) for k in (3, 1, 2)}
        return [values[0], swapped[1], swapped[2], swapped[3]]

    def ahead(value):
        return lax.ppermute(value, "seq", [(i, (i + QUAD) % peers) for i in range(peers)])

    convs = [conv_x_weight, bx, wbc, bbc]
    xc, part, first, carries, factors = call(
        early_kernel,
        both,
        [x_in, bc, *convs, dt_raw.T, dt_bias.reshape(1, heads), decay.reshape(1, heads)],
        [
            ((rows, chan), BF16),
            ((STATE, chan), F32),
            ((HALO, chan), F32),
            ((EXTRA, chan), BF16),
            ((rows, 4 * heads), BF16),
        ],
        600_000_000,
    )
    msgs, tops = [], []
    for g in range(groups):
        *sent, top = call(
            functools.partial(late_kernel, g),
            both,
            [x_in, bc, halo, *convs, part, first, carries],
            [((STATE + EXTRA, width), BF16)] * QUAD + [((HALO, wide), BF16)],
            20_000_000,
        )
        msgs.append(swap(sent))
        tops.append(top)

    local = []
    for g in range(groups):
        args = [xc, tops[g], z_in, bc, halo, wbc, bbc, factors, skip_d.reshape(1, heads)]
        outs = [((rows, wide), F32), ((rows, wide), F32), ((rows, STATE), BF16)]
        local.append(list(call(functools.partial(inner_kernel, g), both, args, outs, 300_000_000)))
        msgs[g][0], local[g][0] = tie(msgs[g][0], local[g][0])

    entering = []
    for g in range(groups):
        total, through = call(
            fold_kernel, (info,), msgs[g], [((STATE, width), BF16), ((8, width), F32)], 1_000_000
        )
        state = ahead(total)
        for _ in range(reach - 1):
            state = ahead((total.astype(F32) + through[0:1] * state.astype(F32)).astype(BF16))
        entering.append(state)

    blocks = []
    for g in range(groups):
        outs = [((STATE, width), BF16)] * QUAD
        blocks.append(swap(call(enter_kernel, (info,), [entering[g], *msgs[g]], outs, 1_000_000)))

    out = None
    for g in range(groups):
        near, gain, cmat = local[g]
        args = [near, gain, *blocks[g], cmat, scale]
        specs = [VMEM] * len(args)
        aliases = {}
        if out is not None:
            aliases = {1 + len(args): 0}
            args.append(out)
            specs.append(ANY)
        (out,) = call(
            functools.partial(finish_kernel, g),
            (info,),
            args,
            [((rows, chan), BF16)],
            100_000_000,
            specs=specs,
            out_specs=[ANY],
            scratch_shapes=[pltpu.VMEM((rows, wide), BF16), pltpu.SemaphoreType.DMA],
            input_output_aliases=aliases,
        )
    return out


def solution(mesh):
    return jax.shard_map(
        shards,
        mesh=mesh,
        in_specs=(
            P(("groups", "seq"), "heads"),
            P(("groups", "seq"), "heads"),
            P(("groups", "seq"), None, "heads"),
            P(None, "heads"),
            P("heads"),
            P(None, None, "heads"),
            P(None, "heads"),
            P(("groups", "seq"), "heads"),
            P("heads"),
            P("heads"),
            P("heads"),
            P("heads"),
            P("groups"),
        ),
        out_specs=P(("groups", "seq"), "heads"),
        check_vma=False,
    )
```

```python
import functools

import jax
import jax.numpy as jnp
from jax import lax
from jax.experimental import pallas as pl
from jax.experimental.pallas import tpu as pltpu
from jax.sharding import PartitionSpec as P

HEAD_DIM = 64
STATE = 128
BLOCK = 128
QUAD = 4
HALO = 16
EXTRA = 16
F32 = jnp.float32
BF16 = jnp.bfloat16


def mm(left, right):
    return jnp.dot(left, right, preferred_element_type=F32)


def ends_of(lens_ref):
    total = 0
    ends = []
    for i in range(lens_ref.shape[0]):
        total = total + lens_ref[i]
        ends.append(total)
    return ends


def seg_of(pos, ends):
    count = 0
    for end in ends:
        count = count + jnp.where(end <= pos, 1, 0)
    return jnp.where(pos >= 0, count, -1)


def tokens(start, shape, dim):
    return start + lax.broadcasted_iota(jnp.int32, shape, dim)


def shift_matrix(start, ends, rows, before, taps):
    shape = (rows, before + rows)
    row = lax.broadcasted_iota(jnp.int32, shape, 0)
    col = lax.broadcasted_iota(jnp.int32, shape, 1)
    same = seg_of(start + row, ends) == seg_of(start - before + col, ends)
    parts = []
    for k in range(taps - 1):
        parts.append(jnp.where((col == row + (before - taps + 1 + k)) & same, 1.0, 0.0))
    return jnp.concatenate(parts, axis=0).astype(BF16)


def conv_half(shift, extended, block, weight, bias):
    rows = block.shape[0]
    taps = weight.shape[0]
    half = weight.astype(F32) * 0.5
    moved = mm(shift, extended)
    total = bias * 0.5 + block.astype(F32) * half[taps - 1 : taps]
    for k in range(taps - 1):
        total = total + moved[k * rows : (k + 1) * rows] * half[k : k + 1]
    return total


def silu_of_half(half):
    return half + half * jnp.tanh(half)


def rates_of(dt_ref, dtb_ref, dec_ref):
    raw = jnp.transpose(dt_ref[...].astype(F32)) + dtb_ref[...]
    rate = jnp.maximum(raw, 0.0) + jnp.log1p(jnp.exp(-jnp.abs(raw)))
    shape = (BLOCK, BLOCK)
    lower = lax.broadcasted_iota(jnp.int32, shape, 0) >= lax.broadcasted_iota(jnp.int32, shape, 1)
    cum = jnp.dot(
        jnp.where(lower, 1.0, 0.0),
        -rate * dec_ref[...],
        precision=lax.Precision.HIGHEST,
        preferred_element_type=F32,
    )
    return rate, cum


def head_map(heads, first, width):
    shape = (heads, width)
    row = lax.broadcasted_iota(jnp.int32, shape, 0)
    col = lax.broadcasted_iota(jnp.int32, shape, 1)
    return jnp.where(row == first + col // HEAD_DIM, 1.0, 0.0).astype(BF16)


def pair_of(value):
    high = value.astype(BF16)
    low = (value - high.astype(F32)).astype(BF16)
    return jnp.concatenate([high, low], axis=1)


def twice(onehot):
    return jnp.concatenate([onehot, onehot], axis=0)


def edge_kernel(x, bc, out, held, sems):
    rows, chan = x.shape
    inner = bc.shape[2]
    copies = [
        pltpu.make_async_copy(bc.at[rows - HALO : rows], held, sems.at[0]),
        pltpu.make_async_copy(x.at[rows - HALO : rows, :], out.at[:, 0:chan], sems.at[1]),
    ]
    for copy in copies:
        copy.start()
    copies[0].wait()
    value = held[...].astype(F32)
    for i in range(2):
        out[:, chan + i * inner : chan + (i + 1) * inner] = value[:, i, :].astype(BF16)
    copies[1].wait()


def early_kernel(
    info, lens_in, x_in, wx_in, bx_in, dt_in, dtb_in, dec_in, wbc_in, bbc_in, skip_in,
    xc_out, scaled, top, first, carries, factors, shift, mask, wx, bx, wbc, bbc, skip,
    lens, x, dt, dtb, dec, sems,
):
    heads, rows = dt.shape
    chan = x.shape[1]
    step = 1024
    small = [
        (lens_in, lens), (dt_in, dt), (dtb_in, dtb), (dec_in, dec), (wx_in, wx), (bx_in, bx), (wbc_in, wbc),
        (bbc_in, bbc), (skip_in, skip),
    ]
    copies = [pltpu.make_async_copy(s, d, sems.at[i]) for i, (s, d) in enumerate(small)]
    blocks = [
        pltpu.make_async_copy(x_in.at[:, at : at + step], x.at[:, at : at + step], sems.at[len(small) + i])
        for i, at in enumerate(range(0, chan, step))
    ]
    for copy in copies + blocks:
        copy.start()
    for copy in copies:
        copy.wait()
    start = info[0] * BLOCK
    ends = ends_of(lens)
    moves = shift_matrix(start, ends, BLOCK, HALO, wx.shape[0])
    shift[...] = moves
    moves = shift_matrix(start, ends, BLOCK, 0, wx.shape[0])
    shape = (BLOCK, BLOCK)
    row = lax.broadcasted_iota(jnp.int32, shape, 0)
    col = lax.broadcasted_iota(jnp.int32, shape, 1)
    seg_row = seg_of(start + row, ends)
    mask[...] = jnp.where((row >= col) & (seg_row == seg_of(start + col, ends)), 1.0, 0.0)
    rate, cum = rates_of(dt, dtb, dec)
    last = cum[BLOCK - 1 : BLOCK]
    seg_last = seg_of(start + BLOCK - 1, ends)
    seg_head = seg_row[:, 0:heads]
    factor = pair_of(jnp.where(seg_head == seg_last, jnp.exp(last - cum), 0.0) * rate)
    grown = jnp.exp(cum)
    before = seg_of(start - 1, ends)
    factors[:, 0 : 2 * heads] = pair_of(rate * jnp.exp(-cum))
    factors[:, 2 * heads : 4 * heads] = pair_of(grown)
    factors[:, 4 * heads : 6 * heads] = pair_of(jnp.where(seg_head == before, grown, 0.0))
    carry = pair_of(jnp.where(seg_last == before, jnp.exp(last), 0.0)).astype(F32)
    row = lax.broadcasted_iota(jnp.int32, (EXTRA, heads), 0)
    rows = jnp.where(row == 0, carry[:, 0:heads], jnp.where(row == 1, carry[:, heads:], 0.0)).astype(BF16)
    for i, at in enumerate(range(0, chan, step)):
        lane = slice(at, at + step)
        onehot = head_map(heads, at // HEAD_DIM, step)
        spread = mm(factor, twice(onehot))
        first[:, lane] = spread[0:HALO]
        carries[:, lane] = mm(rows, onehot).astype(BF16)
        blocks[i].wait()
        xs = x[:, lane]
        top[:, lane] = xs[0:HALO]
        xc = silu_of_half(conv_half(moves, xs, xs, wx[:, lane], bx[:, lane])).astype(BF16)
        xc_out[:, lane] = xc
        scaled[:, lane] = (xc.astype(F32) * spread).astype(BF16)


def bc_conv(which, g, shift, halo, bc, wbc, bbc):
    taps, _, inner = wbc.shape
    chan = halo.shape[1] - 2 * inner
    base = which * inner + g * STATE
    lane = slice(g * STATE, (g + 1) * STATE)
    block = bc[:, base : base + STATE]
    ext = jnp.concatenate([halo[:, chan + base : chan + base + STATE], block], axis=0)
    weight = jnp.concatenate([wbc[k].astype(F32)[which : which + 1, lane] for k in range(taps)], axis=0)
    return silu_of_half(conv_half(shift[...], ext, block, weight, bbc[which : which + 1, lane]))


def late_kernel(g, info, top, bc, halo, wx, bx, wbc, bbc, shift, scaled, first, carries, m0, m1, m2, m3, xc_out, b_out, held):
    mine = info[1]
    wide, width = xc_out.shape[1], m0.shape[1]
    taps = wx.shape[0]
    deep = slice(g * wide, (g + 1) * wide)
    bmat = bc_conv(0, g, shift, halo, bc, wbc, bbc)
    b_out[...] = bmat.astype(BF16)
    moves = jnp.concatenate([shift[k * BLOCK : k * BLOCK + HALO, 0 : 2 * HALO] for k in range(taps - 1)], axis=0)
    ext = jnp.concatenate([halo[:, deep], top[:, deep]], axis=0)
    xc = silu_of_half(conv_half(moves, ext, top[:, deep], wx[:, deep], bx[:, deep])).astype(BF16)
    xc_out[...] = xc
    head = (xc.astype(F32) * first[:, deep]).astype(BF16)
    operand = jnp.concatenate([head, scaled[HALO:, deep]], axis=0)
    held[0:STATE, :] = mm(jnp.transpose(bmat).astype(BF16), operand).astype(BF16)
    held[STATE : STATE + EXTRA, :] = carries[:, deep]
    for k, msg in enumerate((m0, m1, m2, m3)):
        msg[...] = held[:, pl.ds(pl.multiple_of((mine ^ k) * width, width), width)]


def carry_of(msg):
    return msg[STATE : STATE + 1, :].astype(F32) + msg[STATE + 1 : STATE + 2, :].astype(F32)


def fold_kernel(info, m0, m1, m2, m3, total, *decay):
    msgs = (m0, m1, m2, m3)
    for mine in range(QUAD):

        @pl.when(info[1] == mine)
        def _():
            block = [msgs[mine ^ b] for b in range(QUAD)]
            state = block[0][0:STATE, :].astype(F32)
            through = carry_of(block[0])
            for b in range(1, QUAD):
                carry = carry_of(block[b])
                state = block[b][0:STATE, :].astype(F32) + carry * state
                through = through * carry
            total[...] = state.astype(BF16)
            for out in decay:
                out[...] = jnp.broadcast_to(through, out.shape)


def enter_kernel(info, start, m0, m1, m2, m3, o0, o1, o2, o3):
    msgs = (m0, m1, m2, m3)
    outs = (o0, o1, o2, o3)
    for mine in range(QUAD):

        @pl.when(info[1] == mine)
        def _():
            outs[mine][...] = start[...]
            state = start[...].astype(F32)
            for b in range(1, QUAD):
                prev = msgs[mine ^ (b - 1)]
                state = prev[0:STATE, :].astype(F32) + carry_of(prev) * state
                outs[mine ^ b][...] = state.astype(BF16)


def inner_kernel(
    g, xc_in, xc_top, z_in, bc, bmat, halo, wbc, bbc, shift, mask, factors, skip, near, gain, c_out, z, sem
):
    wide = xc_top.shape[1]
    copy = pltpu.make_async_copy(z_in.at[:, g * wide : (g + 1) * wide], z, sem)
    copy.start()
    heads = skip.shape[1]
    cmat = bc_conv(1, g, shift, halo, bc, wbc, bbc).astype(BF16)
    c_out[...] = cmat
    scores = lax.dot_general(cmat, bmat[...], (((1,), (1,)), ((), ())), preferred_element_type=F32)
    scores = (scores * mask[...]).astype(BF16)
    skips = pair_of(jnp.broadcast_to(skip[...], (8, heads)))
    step = 1024
    copy.wait()
    for at in range(0, wide, step):
        lane = slice(at, at + step)
        deep = slice(g * wide + at, g * wide + at + step)
        onehot2 = twice(head_map(heads, (g * wide + at) // HEAD_DIM, step))
        xf = jnp.concatenate([xc_top[:, lane], xc_in[HALO:, deep]], axis=0).astype(F32)
        scaled = (xf * mm(factors[:, 0 : 2 * heads], onehot2)).astype(BF16)
        grown = mm(factors[:, 2 * heads : 4 * heads], onehot2)
        skip_c = mm(skips, onehot2)[0:1]
        gate = silu_of_half(z[:, lane].astype(F32) * 0.5)
        near[:, lane] = (mm(scores, scaled) * grown + skip_c * xf) * gate
        gain[:, lane] = mm(factors[:, 4 * heads : 6 * heads], onehot2) * gate


def finish_kernel(g, info, near, gain, e0, e1, e2, e3, cmat, scale_in, *rest):
    out, held, scale, sems = rest[-4:]
    mine = info[1]
    rows, wide = near.shape
    width = wide // QUAD
    steps = sems.shape[0] - 1
    part = rows // steps
    fetch = pltpu.make_async_copy(scale_in.at[:, g * wide : (g + 1) * wide], scale, sems.at[steps])
    fetch.start()
    copies = []
    for i in range(steps):
        these = slice(i * part, (i + 1) * part)
        c = cmat[these, :]
        values = []
        square = 0.0
        for k, e in enumerate((e0, e1, e2, e3)):
            at = pl.ds(pl.multiple_of((mine ^ k) * width, width), width)
            value = near[these, at] + gain[these, at] * mm(c, e[...])
            square = square + jnp.sum(value * value, axis=1, keepdims=True)
            values.append((at, value))
        inv = lax.rsqrt(square * (1.0 / wide) + 1e-05)
        if i == 0:
            fetch.wait()
        for at, value in values:
            held[these, at] = (value * inv * scale[:, at]).astype(BF16)
        copy = pltpu.make_async_copy(held.at[these, :], out.at[these, g * wide : (g + 1) * wide], sems.at[i])
        copy.start()
        copies.append(copy)
    for copy in copies:
        copy.wait()


SMEM = pl.BlockSpec(memory_space=pltpu.SMEM)
VMEM = pl.BlockSpec(memory_space=pltpu.VMEM)
ANY = pl.BlockSpec(memory_space=pl.ANY)
HBM = pl.BlockSpec(memory_space=pltpu.HBM)


def call(kernel, scalars, args, outs, flops, limit=32 << 20, **more):
    pinned = more.get("specs", ())
    args = [
        pltpu.with_memory_space_constraint(arg, pltpu.HBM) if i < len(pinned) and pinned[i] is HBM else arg
        for i, arg in enumerate(args)
    ]
    return pl.pallas_call(
        kernel,
        in_specs=[SMEM] * len(scalars) + more.pop("specs", [VMEM] * len(args)),
        out_specs=more.pop("out_specs", [VMEM] * len(outs)),
        out_shape=[jax.ShapeDtypeStruct(*out) for out in outs],
        cost_estimate=pl.CostEstimate(flops=flops, bytes_accessed=4 << 20, transcendentals=0),
        compiler_params=pltpu.CompilerParams(vmem_limit_bytes=limit),
        **more,
    )(*scalars, *args)


def tie(first, second):
    return lax.optimization_barrier((first, second))


def shards(
    x_in,
    z_in,
    bc_in,
    conv_x_weight,
    conv_x_bias,
    conv_bc_weight,
    conv_bc_bias,
    dt_raw,
    dt_bias,
    decay,
    skip_d,
    norm_gain,
    lengths,
):
    rows, chan = x_in.shape
    heads = dt_raw.shape[1]
    peers = lax.axis_size("seq")
    shard = lax.axis_index("seq").astype(jnp.int32)
    taps = conv_x_weight.shape[0]
    bcw = bc_in.shape[2]
    groups = bcw // STATE
    wide = chan // groups
    width = wide // QUAD
    reach = peers // 2 // QUAD

    bx = conv_x_bias.reshape(1, chan)
    scale = norm_gain.reshape(1, chan)
    info = jnp.stack([shard, shard % QUAD])

    (edge,) = call(
        edge_kernel,
        [],
        [x_in, bc_in],
        [((HALO, chan + 2 * bcw), BF16)],
        1_000_000,
        specs=[HBM] * 2,
        scratch_shapes=[pltpu.VMEM((HALO, 2, bcw), BF16), pltpu.SemaphoreType.DMA((2,))],
    )
    halo = lax.ppermute(edge, "seq", [(i, (i + 1) % peers) for i in range(peers)])
    bc = bc_in.reshape(rows, 2 * bcw)

    def swap(values):
        routes = [[(i, i ^ k) for i in range(peers)] for k in range(QUAD)]
        swapped = {k: lax.ppermute(values[k], "seq", routes[k]) for k in (3, 1, 2)}
        return [values[0], swapped[1], swapped[2], swapped[3]]

    def ahead(value):
        return lax.ppermute(value, "seq", [(i, (i + QUAD) % peers) for i in range(peers)])

    early_args = [
        lengths, x_in, conv_x_weight, bx, dt_raw.T, dt_bias.reshape(1, heads), decay.reshape(1, heads),
        conv_bc_weight, conv_bc_bias, skip_d.reshape(1, heads),
    ]
    xc, scaled, top, first, carries, factors, shift, mask, wx, bx, wbc, bbc, skip = call(
        early_kernel,
        [info],
        early_args,
        [
            ((rows, chan), BF16),
            ((rows, chan), BF16),
            ((HALO, chan), BF16),
            ((HALO, chan), F32),
            ((EXTRA, chan), BF16),
            ((rows, 6 * heads), BF16),
            (((taps - 1) * BLOCK, HALO + BLOCK), BF16),
            ((BLOCK, BLOCK), F32),
            ((taps, chan), BF16),
            ((1, chan), F32),
            ((taps, 2, bcw), BF16),
            ((2, bcw), F32),
            ((1, heads), F32),
        ],
        600_000_000,
        specs=[HBM] * len(early_args),
        scratch_shapes=[
            pltpu.SMEM(lengths.shape, jnp.int32),
            pltpu.VMEM((rows, chan), BF16),
            pltpu.VMEM((heads, rows), BF16),
            pltpu.VMEM((1, heads), F32),
            pltpu.VMEM((1, heads), F32),
            pltpu.SemaphoreType.DMA((13,)),
        ],
    )
    msgs, tops, bmats = [], [], []
    for g in range(groups):
        *sent, xc_top, bmat = call(
            functools.partial(late_kernel, g),
            [info],
            [top, bc, halo, wx, bx, wbc, bbc, shift, scaled, first, carries],
            [((STATE + EXTRA, width), BF16)] * QUAD + [((HALO, wide), BF16), ((rows, STATE), BF16)],
            100_000_000,
            scratch_shapes=[pltpu.VMEM((STATE + EXTRA, wide), BF16)],
        )
        msgs.append(swap(sent))
        tops.append(xc_top)
        bmats.append(bmat)

    local = []
    for g in range(groups):
        args = [xc, tops[g], z_in, bc, bmats[g], halo, wbc, bbc, shift, mask, factors, skip]
        outs = [((rows, wide), F32), ((rows, wide), F32), ((rows, STATE), BF16)]
        near = call(
            functools.partial(inner_kernel, g),
            [],
            args,
            outs,
            300_000_000,
            specs=[HBM if arg is z_in else VMEM for arg in args],
            scratch_shapes=[pltpu.VMEM((rows, wide), BF16), pltpu.SemaphoreType.DMA],
        )
        local.append(list(near))
        msgs[g][0], local[g][0] = tie(msgs[g][0], local[g][0])

    entering = []
    for g in range(groups):
        outs = [((STATE, width), BF16)] + [((8, width), F32)] * (reach > 1)
        total, *through = call(fold_kernel, (info,), msgs[g], outs, 1_000_000)
        state = ahead(total)
        for _ in range(reach - 1):
            state = ahead((total.astype(F32) + through[0][0:1] * state.astype(F32)).astype(BF16))
        entering.append(state)

    blocks = []
    for g in range(groups):
        outs = [((STATE, width), BF16)] * QUAD
        blocks.append(swap(call(enter_kernel, (info,), [entering[g], *msgs[g]], outs, 1_000_000)))

    out = None
    for g in range(groups):
        near, gain, cmat = local[g]
        args = [near, gain, *blocks[g], cmat, scale]
        specs = [VMEM] * (len(args) - 1) + [HBM]
        aliases = {}
        if out is not None:
            aliases = {1 + len(args): 0}
            args.append(out)
            specs.append(ANY)
        (out,) = call(
            functools.partial(finish_kernel, g),
            (info,),
            args,
            [((rows, chan), BF16)],
            100_000_000,
            specs=specs,
            out_specs=[ANY],
            scratch_shapes=[
                pltpu.VMEM((rows, wide), BF16),
                pltpu.VMEM((1, wide), F32),
                pltpu.SemaphoreType.DMA((3,)),
            ],
            input_output_aliases=aliases,
        )
    return out


def solution(mesh):
    return jax.shard_map(
        shards,
        mesh=mesh,
        in_specs=(
            P(("groups", "seq"), "heads"),
            P(("groups", "seq"), "heads"),
            P(("groups", "seq"), None, "heads"),
            P(None, "heads"),
            P("heads"),
            P(None, None, "heads"),
            P(None, "heads"),
            P(("groups", "seq"), "heads"),
            P("heads"),
            P("heads"),
            P("heads"),
            P("heads"),
            P("groups"),
        ),
        out_specs=P(("groups", "seq"), "heads"),
        check_vma=False,
    )
```

```python
import functools

import jax
import jax.numpy as jnp
from jax import lax
from jax.experimental import pallas as pl
from jax.experimental.pallas import tpu as pltpu
from jax.sharding import PartitionSpec as P

HEAD_DIM = 64
STATE = 128
BLOCK = 128
QUAD = 4
HALO = 8
EXTRA = 8
FIRST = 16
F32 = jnp.float32
BF16 = jnp.bfloat16


def mm(left, right):
    return jnp.dot(left, right, preferred_element_type=F32)


def ends_of(lens_ref):
    total = 0
    ends = []
    for i in range(lens_ref.shape[0]):
        total = total + lens_ref[i]
        ends.append(total)
    return ends


def seg_of(pos, ends):
    count = 0
    for end in ends:
        count = count + jnp.where(end <= pos, 1, 0)
    return jnp.where(pos >= 0, count, -1)


def tokens(start, shape, dim):
    return start + lax.broadcasted_iota(jnp.int32, shape, dim)


def shift_matrix(start, ends, rows, before, taps):
    shape = (rows, before + rows)
    row = lax.broadcasted_iota(jnp.int32, shape, 0)
    col = lax.broadcasted_iota(jnp.int32, shape, 1)
    same = seg_of(start + row, ends) == seg_of(start - before + col, ends)
    parts = []
    for k in range(taps - 1):
        parts.append(jnp.where((col == row + (before - taps + 1 + k)) & same, 1.0, 0.0))
    return jnp.concatenate(parts, axis=0).astype(BF16)


def conv_half(shift, extended, block, weight, bias):
    rows = block.shape[0]
    taps = weight.shape[0]
    half = weight.astype(F32) * 0.5
    moved = mm(shift, extended)
    total = bias * 0.5 + block.astype(F32) * half[taps - 1 : taps]
    for k in range(taps - 1):
        total = total + moved[k * rows : (k + 1) * rows] * half[k : k + 1]
    return total


def silu_of_half(half):
    return half + half * jnp.tanh(half)


def rates_of(dt_ref, dtb_ref, dec_ref):
    raw = jnp.transpose(dt_ref[...].astype(F32)) + dtb_ref[...]
    rate = jnp.maximum(raw, 0.0) + jnp.log1p(jnp.exp(-jnp.abs(raw)))
    shape = (BLOCK, BLOCK)
    lower = lax.broadcasted_iota(jnp.int32, shape, 0) >= lax.broadcasted_iota(jnp.int32, shape, 1)
    cum = jnp.dot(
        jnp.where(lower, 1.0, 0.0),
        -rate * dec_ref[...],
        precision=lax.Precision.HIGHEST,
        preferred_element_type=F32,
    )
    return rate, cum


def head_map(heads, first, width):
    shape = (heads, width)
    row = lax.broadcasted_iota(jnp.int32, shape, 0)
    col = lax.broadcasted_iota(jnp.int32, shape, 1)
    return jnp.where(row == first + col // HEAD_DIM, 1.0, 0.0).astype(BF16)


def pair_of(value):
    high = value.astype(BF16)
    low = (value - high.astype(F32)).astype(BF16)
    return jnp.concatenate([high, low], axis=1)


def twice(onehot):
    return jnp.concatenate([onehot, onehot], axis=0)


def edge_kernel(x, bc, out, held, sems):
    rows, chan = x.shape
    inner = bc.shape[2]
    copies = [
        pltpu.make_async_copy(bc.at[rows - HALO : rows], held, sems.at[0]),
        pltpu.make_async_copy(x.at[rows - HALO : rows, :], out.at[:, 0:chan], sems.at[1]),
    ]
    for copy in copies:
        copy.start()
    copies[0].wait()
    value = held[...].astype(F32)
    for i in range(2):
        out[:, chan + i * inner : chan + (i + 1) * inner] = value[:, i, :].astype(BF16)
    copies[1].wait()


def early_kernel(
    info, lens_in, x_in, wx_in, bx_in, dt_in, dtb_in, dec_in, wbc_in, bbc_in, skip_in, scale_in,
    xc_out, scaled, top, first, carries, factors, shift, mask, wx, bx, wbc, bbc, skip, scale,
    lens, x, dt, dtb, dec, sems,
):
    heads, rows = dt.shape
    chan = x.shape[1]
    step = 1024
    small = [
        (lens_in, lens), (dt_in, dt), (dtb_in, dtb), (dec_in, dec), (wx_in, wx), (bx_in, bx), (wbc_in, wbc),
        (bbc_in, bbc), (skip_in, skip), (scale_in, scale),
    ]
    copies = [pltpu.make_async_copy(s, d, sems.at[i]) for i, (s, d) in enumerate(small)]
    blocks = [
        pltpu.make_async_copy(x_in.at[:, at : at + step], x.at[:, at : at + step], sems.at[len(small) + i])
        for i, at in enumerate(range(0, chan, step))
    ]
    for copy in copies + blocks:
        copy.start()
    for copy in copies:
        copy.wait()
    start = info[0] * BLOCK
    ends = ends_of(lens)
    moves = shift_matrix(start, ends, BLOCK, HALO, wx.shape[0])
    shift[...] = moves
    moves = shift_matrix(start, ends, BLOCK, 0, wx.shape[0])
    shape = (BLOCK, BLOCK)
    row = lax.broadcasted_iota(jnp.int32, shape, 0)
    col = lax.broadcasted_iota(jnp.int32, shape, 1)
    seg_row = seg_of(start + row, ends)
    mask[...] = jnp.where((row >= col) & (seg_row == seg_of(start + col, ends)), 1.0, 0.0)
    rate, cum = rates_of(dt, dtb, dec)
    last = cum[BLOCK - 1 : BLOCK]
    seg_last = seg_of(start + BLOCK - 1, ends)
    seg_head = seg_row[:, 0:heads]
    factor = pair_of(jnp.where(seg_head == seg_last, jnp.exp(last - cum), 0.0) * rate)
    grown = jnp.exp(cum)
    before = seg_of(start - 1, ends)
    factors[:, 0 : 2 * heads] = pair_of(rate * jnp.exp(-cum))
    factors[:, 2 * heads : 4 * heads] = pair_of(grown)
    factors[:, 4 * heads : 6 * heads] = pair_of(jnp.where(seg_head == before, grown, 0.0))
    carry = pair_of(jnp.where(seg_last == before, jnp.exp(last), 0.0)).astype(F32)
    row = lax.broadcasted_iota(jnp.int32, (EXTRA, heads), 0)
    rows = jnp.where(row == 0, carry[:, 0:heads], jnp.where(row == 1, carry[:, heads:], 0.0)).astype(BF16)
    for i, at in enumerate(range(0, chan, step)):
        lane = slice(at, at + step)
        onehot = head_map(heads, at // HEAD_DIM, step)
        spread = mm(factor, twice(onehot))
        first[:, lane] = spread[0:FIRST]
        carries[:, lane] = mm(rows, onehot).astype(BF16)
        blocks[i].wait()
        xs = x[:, lane]
        top[:, lane] = xs[0:FIRST]
        xc = silu_of_half(conv_half(moves, xs, xs, wx[:, lane], bx[:, lane])).astype(BF16)
        xc_out[:, lane] = xc
        scaled[:, lane] = (xc.astype(F32) * spread).astype(BF16)


def joined(above, below):
    return jnp.concatenate([above.astype(F32), below.astype(F32)], axis=0).astype(BF16)


def bc_conv(which, g, shift, halo, bc, wbc, bbc):
    taps, _, inner = wbc.shape
    chan = halo.shape[1] - 2 * inner
    base = which * inner + g * STATE
    lane = slice(g * STATE, (g + 1) * STATE)
    block = bc[:, base : base + STATE]
    ext = joined(halo[:, chan + base : chan + base + STATE], block)
    weight = jnp.concatenate([wbc[k].astype(F32)[which : which + 1, lane] for k in range(taps)], axis=0)
    return silu_of_half(conv_half(shift[...], ext, block, weight, bbc[which : which + 1, lane]))


def late_kernel(g, info, top, bc, halo, wx, bx, wbc, bbc, shift, scaled, first, carries, m0, m1, m2, m3, xc_out, b_out, held):
    mine = info[1]
    wide, width = xc_out.shape[1], m0.shape[1]
    taps = wx.shape[0]
    deep = slice(g * wide, (g + 1) * wide)
    bmat = bc_conv(0, g, shift, halo, bc, wbc, bbc)
    b_out[...] = bmat.astype(BF16)
    cols = slice(0, HALO + FIRST)
    moves = jnp.concatenate([shift[k * BLOCK : k * BLOCK + FIRST, cols] for k in range(taps - 1)], axis=0)
    ext = joined(halo[:, deep], top[:, deep])
    xc = silu_of_half(conv_half(moves, ext, top[:, deep], wx[:, deep], bx[:, deep])).astype(BF16)
    xc_out[...] = xc
    head = (xc.astype(F32) * first[:, deep]).astype(BF16)
    operand = jnp.concatenate([head, scaled[FIRST:, deep]], axis=0)
    held[0:STATE, :] = mm(jnp.transpose(bmat).astype(BF16), operand).astype(BF16)
    held[STATE : STATE + EXTRA, :] = carries[:, deep]
    for k, msg in enumerate((m0, m1, m2, m3)):
        msg[...] = held[:, pl.ds(pl.multiple_of((mine ^ k) * width, width), width)]


def carry_of(msg):
    return msg[STATE : STATE + 1, :].astype(F32) + msg[STATE + 1 : STATE + 2, :].astype(F32)


def fold_kernel(info, m0, m1, m2, m3, total, *decay):
    msgs = (m0, m1, m2, m3)
    for mine in range(QUAD):

        @pl.when(info[1] == mine)
        def _():
            block = [msgs[mine ^ b] for b in range(QUAD)]
            state = block[0][0:STATE, :].astype(F32)
            through = carry_of(block[0])
            for b in range(1, QUAD):
                carry = carry_of(block[b])
                state = block[b][0:STATE, :].astype(F32) + carry * state
                through = through * carry
            total[...] = state.astype(BF16)
            for out in decay:
                out[...] = jnp.broadcast_to(through, out.shape)


def enter_kernel(info, start, m0, m1, m2, m3, o0, o1, o2, o3):
    msgs = (m0, m1, m2, m3)
    outs = (o0, o1, o2, o3)
    for mine in range(QUAD):

        @pl.when(info[1] == mine)
        def _():
            outs[mine][...] = start[...]
            state = start[...].astype(F32)
            for b in range(1, QUAD):
                prev = msgs[mine ^ (b - 1)]
                state = prev[0:STATE, :].astype(F32) + carry_of(prev) * state
                outs[mine ^ b][...] = state.astype(BF16)


def inner_kernel(
    g, xc_in, xc_top, z_in, bc, bmat, halo, wbc, bbc, shift, mask, factors, skip, near, gain, c_out, z, sem
):
    wide = xc_top.shape[1]
    copy = pltpu.make_async_copy(z_in.at[:, g * wide : (g + 1) * wide], z, sem)
    copy.start()
    heads = skip.shape[1]
    cmat = bc_conv(1, g, shift, halo, bc, wbc, bbc).astype(BF16)
    c_out[...] = cmat
    scores = lax.dot_general(cmat, bmat[...], (((1,), (1,)), ((), ())), preferred_element_type=F32)
    scores = (scores * mask[...]).astype(BF16)
    skips = pair_of(jnp.broadcast_to(skip[...], (8, heads)))
    step = 1024
    copy.wait()
    for at in range(0, wide, step):
        lane = slice(at, at + step)
        deep = slice(g * wide + at, g * wide + at + step)
        onehot2 = twice(head_map(heads, (g * wide + at) // HEAD_DIM, step))
        xf = jnp.concatenate([xc_top[:, lane], xc_in[FIRST:, deep]], axis=0).astype(F32)
        scaled = (xf * mm(factors[:, 0 : 2 * heads], onehot2)).astype(BF16)
        grown = mm(factors[:, 2 * heads : 4 * heads], onehot2)
        skip_c = mm(skips, onehot2)[0:1]
        gate = silu_of_half(z[:, lane].astype(F32) * 0.5)
        near[:, lane] = (mm(scores, scaled) * grown + skip_c * xf) * gate
        gain[:, lane] = mm(factors[:, 4 * heads : 6 * heads], onehot2) * gate


def finish_kernel(g, info, near, gain, e0, e1, e2, e3, cmat, scale, *rest):
    out, ready, held, sems = rest[-4:]
    mine = info[1]
    rows, wide = near.shape
    width = wide // QUAD
    steps = sems.shape[0]
    part = rows // steps
    square = [0.0] * steps
    ats = [pl.ds(pl.multiple_of((mine ^ k) * width, width), width) for k in range(QUAD)]
    c = cmat[...]
    for at, e in zip(ats, (e0, e1, e2, e3)):
        far = mm(c, e[...])
        for i in range(steps):
            these = slice(i * part, (i + 1) * part)
            value = near[these, at] + gain[these, at] * far[these]
            square[i] = square[i] + jnp.sum(value * value, axis=1, keepdims=True)
            held[these, at] = value
    copies = []
    for i in range(steps):
        these = slice(i * part, (i + 1) * part)
        inv = lax.rsqrt(square[i] * (1.0 / wide) + 1e-05)
        ready[these, :] = (held[these, :] * inv * scale[:, g * wide : (g + 1) * wide]).astype(BF16)
        copy = pltpu.make_async_copy(ready.at[these, :], out.at[these, g * wide : (g + 1) * wide], sems.at[i])
        copy.start()
        copies.append(copy)
    for copy in copies:
        copy.wait()


SMEM = pl.BlockSpec(memory_space=pltpu.SMEM)
VMEM = pl.BlockSpec(memory_space=pltpu.VMEM)
ANY = pl.BlockSpec(memory_space=pl.ANY)
HBM = pl.BlockSpec(memory_space=pltpu.HBM)


def call(kernel, scalars, args, outs, flops, limit=32 << 20, **more):
    pinned = more.get("specs", ())
    args = [
        pltpu.with_memory_space_constraint(arg, pltpu.HBM) if i < len(pinned) and pinned[i] is HBM else arg
        for i, arg in enumerate(args)
    ]
    return pl.pallas_call(
        kernel,
        in_specs=[SMEM] * len(scalars) + more.pop("specs", [VMEM] * len(args)),
        out_specs=more.pop("out_specs", [VMEM] * len(outs)),
        out_shape=[jax.ShapeDtypeStruct(*out) for out in outs],
        cost_estimate=pl.CostEstimate(flops=flops, bytes_accessed=4 << 20, transcendentals=0),
        compiler_params=pltpu.CompilerParams(vmem_limit_bytes=limit),
        **more,
    )(*scalars, *args)


def tie(first, second):
    return lax.optimization_barrier((first, second))


def shards(
    x_in,
    z_in,
    bc_in,
    conv_x_weight,
    conv_x_bias,
    conv_bc_weight,
    conv_bc_bias,
    dt_raw,
    dt_bias,
    decay,
    skip_d,
    norm_gain,
    lengths,
):
    rows, chan = x_in.shape
    heads = dt_raw.shape[1]
    peers = lax.axis_size("seq")
    shard = lax.axis_index("seq").astype(jnp.int32)
    taps = conv_x_weight.shape[0]
    bcw = bc_in.shape[2]
    groups = bcw // STATE
    wide = chan // groups
    width = wide // QUAD
    reach = peers // 2 // QUAD

    bx = conv_x_bias.reshape(1, chan)
    scale = norm_gain.reshape(1, chan)
    info = jnp.stack([shard, shard % QUAD])

    (edge,) = call(
        edge_kernel,
        [],
        [x_in, bc_in],
        [((HALO, chan + 2 * bcw), BF16)],
        1_000_000,
        specs=[HBM] * 2,
        scratch_shapes=[pltpu.VMEM((HALO, 2, bcw), BF16), pltpu.SemaphoreType.DMA((2,))],
    )
    halo = lax.ppermute(edge, "seq", [(i, (i + 1) % peers) for i in range(peers)])
    bc = bc_in.reshape(rows, 2 * bcw)

    def swap(values):
        routes = [[(i, i ^ k) for i in range(peers)] for k in range(QUAD)]
        swapped = {k: lax.ppermute(values[k], "seq", routes[k]) for k in (3, 1, 2)}
        return [values[0], swapped[1], swapped[2], swapped[3]]

    def ahead(value):
        return lax.ppermute(value, "seq", [(i, (i + QUAD) % peers) for i in range(peers)])

    early_args = [
        lengths, x_in, conv_x_weight, bx, dt_raw.T, dt_bias.reshape(1, heads), decay.reshape(1, heads),
        conv_bc_weight, conv_bc_bias, skip_d.reshape(1, heads), scale,
    ]
    xc, scaled, top, first, carries, factors, shift, mask, wx, bx, wbc, bbc, skip, scale = call(
        early_kernel,
        [info],
        early_args,
        [
            ((rows, chan), BF16),
            ((rows, chan), BF16),
            ((FIRST, chan), BF16),
            ((FIRST, chan), F32),
            ((EXTRA, chan), BF16),
            ((rows, 6 * heads), BF16),
            (((taps - 1) * BLOCK, HALO + BLOCK), BF16),
            ((BLOCK, BLOCK), F32),
            ((taps, chan), BF16),
            ((1, chan), F32),
            ((taps, 2, bcw), BF16),
            ((2, bcw), F32),
            ((1, heads), F32),
            ((1, chan), F32),
        ],
        600_000_000,
        specs=[HBM] * len(early_args),
        scratch_shapes=[
            pltpu.SMEM(lengths.shape, jnp.int32),
            pltpu.VMEM((rows, chan), BF16),
            pltpu.VMEM((heads, rows), BF16),
            pltpu.VMEM((1, heads), F32),
            pltpu.VMEM((1, heads), F32),
            pltpu.SemaphoreType.DMA((14,)),
        ],
    )
    msgs, tops, bmats = [], [], []
    for g in range(groups):
        *sent, xc_top, bmat = call(
            functools.partial(late_kernel, g),
            [info],
            [top, bc, halo, wx, bx, wbc, bbc, shift, scaled, first, carries],
            [((STATE + EXTRA, width), BF16)] * QUAD + [((FIRST, wide), BF16), ((rows, STATE), BF16)],
            100_000_000,
            scratch_shapes=[pltpu.VMEM((STATE + EXTRA, wide), BF16)],
        )
        msgs.append(swap(sent))
        tops.append(xc_top)
        bmats.append(bmat)

    local = []
    for g in range(groups):
        args = [xc, tops[g], z_in, bc, bmats[g], halo, wbc, bbc, shift, mask, factors, skip]
        outs = [((rows, wide), F32), ((rows, wide), F32), ((rows, STATE), BF16)]
        near = call(
            functools.partial(inner_kernel, g),
            [],
            args,
            outs,
            300_000_000,
            specs=[HBM if arg is z_in else VMEM for arg in args],
            scratch_shapes=[pltpu.VMEM((rows, wide), BF16), pltpu.SemaphoreType.DMA],
        )
        local.append(list(near))
        msgs[g][0], local[g][0] = tie(msgs[g][0], local[g][0])

    entering = []
    for g in range(groups):
        outs = [((STATE, width), BF16)] + [((8, width), F32)] * (reach > 1)
        total, *through = call(fold_kernel, (info,), msgs[g], outs, 1_000_000)
        state = ahead(total)
        for _ in range(reach - 1):
            state = ahead((total.astype(F32) + through[0][0:1] * state.astype(F32)).astype(BF16))
        entering.append(state)

    blocks = []
    for g in range(groups):
        outs = [((STATE, width), BF16)] * QUAD
        blocks.append(swap(call(enter_kernel, (info,), [entering[g], *msgs[g]], outs, 1_000_000)))

    out = None
    for g in range(groups):
        near, gain, cmat = local[g]
        args = [near, gain, *blocks[g], cmat, scale]
        specs = [VMEM] * len(args)
        aliases = {}
        if out is not None:
            aliases = {1 + len(args): 0}
            args.append(out)
            specs.append(ANY)
        (out,) = call(
            functools.partial(finish_kernel, g),
            (info,),
            args,
            [((rows, chan), BF16)],
            100_000_000,
            specs=specs,
            out_specs=[ANY],
            scratch_shapes=[
                pltpu.VMEM((rows, wide), BF16),
                pltpu.VMEM((rows, wide), F32),
                pltpu.SemaphoreType.DMA((4,)),
            ],
            input_output_aliases=aliases,
        )
    return out


def solution(mesh):
    return jax.shard_map(
        shards,
        mesh=mesh,
        in_specs=(
            P(("groups", "seq"), "heads"),
            P(("groups", "seq"), "heads"),
            P(("groups", "seq"), None, "heads"),
            P(None, "heads"),
            P("heads"),
            P(None, None, "heads"),
            P(None, "heads"),
            P(("groups", "seq"), "heads"),
            P("heads"),
            P("heads"),
            P("heads"),
            P("heads"),
            P("groups"),
        ),
        out_specs=P(("groups", "seq"), "heads"),
        check_vma=False,
    )
```

```python
import functools

import jax
import jax.numpy as jnp
from jax import lax
from jax.experimental import pallas as pl
from jax.experimental.pallas import tpu as pltpu
from jax.sharding import PartitionSpec as P

HEAD_DIM = 64
STATE = 128
BLOCK = 128
QUAD = 4
HALO = 8
EXTRA = 8
FIRST = 16
F32 = jnp.float32
BF16 = jnp.bfloat16


def mm(left, right):
    return jnp.dot(left, right, preferred_element_type=F32)


def ends_of(lens_ref):
    total = 0
    ends = []
    for i in range(lens_ref.shape[0]):
        total = total + lens_ref[i]
        ends.append(total)
    return ends


def seg_of(pos, ends):
    count = 0
    for end in ends:
        count = count + jnp.where(end <= pos, 1, 0)
    return jnp.where(pos >= 0, count, -1)


def tokens(start, shape, dim):
    return start + lax.broadcasted_iota(jnp.int32, shape, dim)


def shift_matrix(start, ends, rows, before, taps):
    shape = (rows, before + rows)
    row = lax.broadcasted_iota(jnp.int32, shape, 0)
    col = lax.broadcasted_iota(jnp.int32, shape, 1)
    same = seg_of(start + row, ends) == seg_of(start - before + col, ends)
    parts = []
    for k in range(taps - 1):
        parts.append(jnp.where((col == row + (before - taps + 1 + k)) & same, 1.0, 0.0))
    return jnp.concatenate(parts, axis=0).astype(BF16)


def conv_half(shift, extended, block, weight, bias):
    rows = block.shape[0]
    taps = weight.shape[0]
    half = weight.astype(F32) * 0.5
    moved = mm(shift, extended)
    total = bias * 0.5 + block.astype(F32) * half[taps - 1 : taps]
    for k in range(taps - 1):
        total = total + moved[k * rows : (k + 1) * rows] * half[k : k + 1]
    return total


def silu_of_half(half):
    return half + half * jnp.tanh(half)


def rates_of(dt_ref, dtb_ref, dec_ref):
    raw = jnp.transpose(dt_ref[...].astype(F32)) + dtb_ref[...]
    rate = jnp.maximum(raw, 0.0) + jnp.log1p(jnp.exp(-jnp.abs(raw)))
    shape = (BLOCK, BLOCK)
    lower = lax.broadcasted_iota(jnp.int32, shape, 0) >= lax.broadcasted_iota(jnp.int32, shape, 1)
    cum = jnp.dot(
        jnp.where(lower, 1.0, 0.0),
        -rate * dec_ref[...],
        precision=lax.Precision.HIGHEST,
        preferred_element_type=F32,
    )
    return rate, cum


def head_map(heads, first, width):
    shape = (heads, width)
    row = lax.broadcasted_iota(jnp.int32, shape, 0)
    col = lax.broadcasted_iota(jnp.int32, shape, 1)
    return jnp.where(row == first + col // HEAD_DIM, 1.0, 0.0).astype(BF16)


def pair_of(value):
    high = value.astype(BF16)
    low = (value - high.astype(F32)).astype(BF16)
    return jnp.concatenate([high, low], axis=1)


def twice(onehot):
    return jnp.concatenate([onehot, onehot], axis=0)


def edge_kernel(x, bc, out, held, sems):
    rows, chan = x.shape
    inner = bc.shape[2]
    copies = [
        pltpu.make_async_copy(bc.at[rows - HALO : rows], held, sems.at[0]),
        pltpu.make_async_copy(x.at[rows - HALO : rows, :], out.at[:, 0:chan], sems.at[1]),
    ]
    for copy in copies:
        copy.start()
    copies[0].wait()
    value = held[...].astype(F32)
    for i in range(2):
        out[:, chan + i * inner : chan + (i + 1) * inner] = value[:, i, :].astype(BF16)
    copies[1].wait()


def early_kernel(
    info, lens_in, x_in, wx_in, bx_in, dt_in, dtb_in, dec_in, wbc_in, bbc_in, skip_in, scale_in,
    xc_out, scaled, top, first, carries, factors, shift, mask, wx, bx, wbc, bbc, skip, scale,
    lens, x, dt, dtb, dec, sems,
):
    heads, rows = dt.shape
    chan = x.shape[1]
    step = 1024
    small = [
        (lens_in, lens), (dt_in, dt), (dtb_in, dtb), (dec_in, dec), (wx_in, wx), (bx_in, bx), (wbc_in, wbc),
        (bbc_in, bbc), (skip_in, skip), (scale_in, scale),
    ]
    copies = [pltpu.make_async_copy(s, d, sems.at[i]) for i, (s, d) in enumerate(small)]
    blocks = [
        pltpu.make_async_copy(x_in.at[:, at : at + step], x.at[:, at : at + step], sems.at[len(small) + i])
        for i, at in enumerate(range(0, chan, step))
    ]
    for copy in copies + blocks:
        copy.start()
    for copy in copies:
        copy.wait()
    start = info[0] * BLOCK
    ends = ends_of(lens)
    moves = shift_matrix(start, ends, BLOCK, HALO, wx.shape[0])
    shift[...] = moves
    moves = shift_matrix(start, ends, BLOCK, 0, wx.shape[0])
    shape = (BLOCK, BLOCK)
    row = lax.broadcasted_iota(jnp.int32, shape, 0)
    col = lax.broadcasted_iota(jnp.int32, shape, 1)
    seg_row = seg_of(start + row, ends)
    mask[...] = jnp.where((row >= col) & (seg_row == seg_of(start + col, ends)), 1.0, 0.0)
    rate, cum = rates_of(dt, dtb, dec)
    last = cum[BLOCK - 1 : BLOCK]
    seg_last = seg_of(start + BLOCK - 1, ends)
    seg_head = seg_row[:, 0:heads]
    factor = pair_of(jnp.where(seg_head == seg_last, jnp.exp(last - cum), 0.0) * rate)
    grown = jnp.exp(cum)
    before = seg_of(start - 1, ends)
    factors[:, 0 : 2 * heads] = pair_of(rate * jnp.exp(-cum))
    factors[:, 2 * heads : 4 * heads] = pair_of(grown)
    factors[:, 4 * heads : 6 * heads] = pair_of(jnp.where(seg_head == before, grown, 0.0))
    carry = pair_of(jnp.where(seg_last == before, jnp.exp(last), 0.0)).astype(F32)
    row = lax.broadcasted_iota(jnp.int32, (EXTRA, heads), 0)
    rows = jnp.where(row == 0, carry[:, 0:heads], jnp.where(row == 1, carry[:, heads:], 0.0)).astype(BF16)
    for i, at in enumerate(range(0, chan, step)):
        lane = slice(at, at + step)
        onehot = head_map(heads, at // HEAD_DIM, step)
        spread = mm(factor, twice(onehot))
        first[:, lane] = spread[0:FIRST]
        carries[:, lane] = mm(rows, onehot).astype(BF16)
        blocks[i].wait()
        xs = x[:, lane]
        top[:, lane] = xs[0:FIRST]
        xc = silu_of_half(conv_half(moves, xs, xs, wx[:, lane], bx[:, lane])).astype(BF16)
        xc_out[:, lane] = xc
        scaled[:, lane] = (xc.astype(F32) * spread).astype(BF16)


def joined(above, below):
    return jnp.concatenate([above.astype(F32), below.astype(F32)], axis=0).astype(BF16)


def bc_conv(which, g, shift, halo, bc, wbc, bbc):
    taps, _, inner = wbc.shape
    chan = halo.shape[1] - 2 * inner
    base = which * inner + g * STATE
    lane = slice(g * STATE, (g + 1) * STATE)
    block = bc[:, base : base + STATE]
    ext = joined(halo[:, chan + base : chan + base + STATE], block)
    weight = jnp.concatenate([wbc[k].astype(F32)[which : which + 1, lane] for k in range(taps)], axis=0)
    return silu_of_half(conv_half(shift[...], ext, block, weight, bbc[which : which + 1, lane]))


def late_kernel(g, info, top, bc, halo, wx, bx, wbc, bbc, shift, scaled, first, carries, m0, m1, m2, m3, xc_out, b_out, held):
    mine = info[2]
    wide, width = xc_out.shape[1], m0.shape[1]
    taps = wx.shape[0]
    deep = slice(g * wide, (g + 1) * wide)
    bmat = bc_conv(0, g, shift, halo, bc, wbc, bbc)
    b_out[...] = bmat.astype(BF16)
    cols = slice(0, HALO + FIRST)
    moves = jnp.concatenate([shift[k * BLOCK : k * BLOCK + FIRST, cols] for k in range(taps - 1)], axis=0)
    ext = joined(halo[:, deep], top[:, deep])
    xc = silu_of_half(conv_half(moves, ext, top[:, deep], wx[:, deep], bx[:, deep])).astype(BF16)
    xc_out[...] = xc
    head = (xc.astype(F32) * first[:, deep]).astype(BF16)
    operand = jnp.concatenate([head, scaled[FIRST:, deep]], axis=0)
    held[0:STATE, :] = mm(jnp.transpose(bmat).astype(BF16), operand).astype(BF16)
    held[STATE : STATE + EXTRA, :] = carries[:, deep]
    for k, msg in enumerate((m0, m1, m2, m3)):
        msg[...] = held[:, pl.ds(pl.multiple_of((mine ^ k) * width, width), width)]


def carry_of(msg):
    return msg[STATE : STATE + 1, :].astype(F32) + msg[STATE + 1 : STATE + 2, :].astype(F32)


def fold_kernel(info, m0, m1, m2, m3, total, *decay):
    msgs = (m0, m1, m2, m3)
    for mine in range(QUAD):

        @pl.when(info[1] == mine)
        def _():
            block = [msgs[mine ^ b] for b in range(QUAD)]
            state = block[0][0:STATE, :].astype(F32)
            through = carry_of(block[0])
            for b in range(1, QUAD):
                carry = carry_of(block[b])
                state = block[b][0:STATE, :].astype(F32) + carry * state
                through = through * carry
            total[...] = state.astype(BF16)
            for out in decay:
                out[...] = jnp.broadcast_to(through, out.shape)


def enter_kernel(info, start, m0, m1, m2, m3, o0, o1, o2, o3):
    msgs = (m0, m1, m2, m3)
    outs = (o0, o1, o2, o3)
    for mine in range(QUAD):

        @pl.when(info[1] == mine)
        def _():
            outs[mine][...] = start[...]
            state = start[...].astype(F32)
            for b in range(1, QUAD):
                prev = msgs[mine ^ (b - 1)]
                state = prev[0:STATE, :].astype(F32) + carry_of(prev) * state
                outs[mine ^ b][...] = state.astype(BF16)


def inner_kernel(
    g, xc_in, xc_top, z_in, bc, bmat, halo, wbc, bbc, shift, mask, factors, skip, near, gain, c_out, z, sem
):
    wide = xc_top.shape[1]
    copy = pltpu.make_async_copy(z_in.at[:, g * wide : (g + 1) * wide], z, sem)
    copy.start()
    heads = skip.shape[1]
    cmat = bc_conv(1, g, shift, halo, bc, wbc, bbc).astype(BF16)
    c_out[...] = cmat
    scores = lax.dot_general(cmat, bmat[...], (((1,), (1,)), ((), ())), preferred_element_type=F32)
    scores = (scores * mask[...]).astype(BF16)
    skips = pair_of(jnp.broadcast_to(skip[...], (8, heads)))
    step = 1024
    copy.wait()
    for at in range(0, wide, step):
        lane = slice(at, at + step)
        deep = slice(g * wide + at, g * wide + at + step)
        onehot2 = twice(head_map(heads, (g * wide + at) // HEAD_DIM, step))
        xf = jnp.concatenate([xc_top[:, lane], xc_in[FIRST:, deep]], axis=0).astype(F32)
        scaled = (xf * mm(factors[:, 0 : 2 * heads], onehot2)).astype(BF16)
        grown = mm(factors[:, 2 * heads : 4 * heads], onehot2)
        skip_c = mm(skips, onehot2)[0:1]
        gate = silu_of_half(z[:, lane].astype(F32) * 0.5)
        near[:, lane] = (mm(scores, scaled) * grown + skip_c * xf) * gate
        gain[:, lane] = mm(factors[:, 4 * heads : 6 * heads], onehot2) * gate


def finish_kernel(g, info, near, gain, e0, e1, e2, e3, cmat, scale, *rest):
    out, ready, held, sems = rest[-4:]
    mine = info[2]
    rows, wide = near.shape
    width = wide // QUAD
    steps = sems.shape[0]
    part = rows // steps
    square = [0.0] * steps
    ats = [pl.ds(pl.multiple_of((mine ^ k) * width, width), width) for k in range(QUAD)]
    c = cmat[...]
    for at, e in zip(ats, (e0, e1, e2, e3)):
        far = mm(c, e[...])
        for i in range(steps):
            these = slice(i * part, (i + 1) * part)
            value = near[these, at] + gain[these, at] * far[these]
            square[i] = square[i] + jnp.sum(value * value, axis=1, keepdims=True)
            held[these, at] = value
    copies = []
    for i in range(steps):
        these = slice(i * part, (i + 1) * part)
        inv = lax.rsqrt(square[i] * (1.0 / wide) + 1e-05)
        ready[these, :] = (held[these, :] * inv * scale[:, g * wide : (g + 1) * wide]).astype(BF16)
        copy = pltpu.make_async_copy(ready.at[these, :], out.at[these, g * wide : (g + 1) * wide], sems.at[i])
        copy.start()
        copies.append(copy)
    for copy in copies:
        copy.wait()


SMEM = pl.BlockSpec(memory_space=pltpu.SMEM)
VMEM = pl.BlockSpec(memory_space=pltpu.VMEM)
ANY = pl.BlockSpec(memory_space=pl.ANY)
HBM = pl.BlockSpec(memory_space=pltpu.HBM)


def call(kernel, scalars, args, outs, flops, limit=32 << 20, **more):
    pinned = more.get("specs", ())
    args = [
        pltpu.with_memory_space_constraint(arg, pltpu.HBM) if i < len(pinned) and pinned[i] is HBM else arg
        for i, arg in enumerate(args)
    ]
    return pl.pallas_call(
        kernel,
        in_specs=[SMEM] * len(scalars) + more.pop("specs", [VMEM] * len(args)),
        out_specs=more.pop("out_specs", [VMEM] * len(outs)),
        out_shape=[jax.ShapeDtypeStruct(*out) for out in outs],
        cost_estimate=pl.CostEstimate(flops=flops, bytes_accessed=4 << 20, transcendentals=0),
        compiler_params=pltpu.CompilerParams(vmem_limit_bytes=limit),
        **more,
    )(*scalars, *args)


def tie(first, second):
    return lax.optimization_barrier((first, second))


def shards(
    x_in,
    z_in,
    bc_in,
    conv_x_weight,
    conv_x_bias,
    conv_bc_weight,
    conv_bc_bias,
    dt_raw,
    dt_bias,
    decay,
    skip_d,
    norm_gain,
    lengths,
):
    rows, chan = x_in.shape
    heads = dt_raw.shape[1]
    peers = lax.axis_size("seq")
    shard = lax.axis_index("seq").astype(jnp.int32)
    taps = conv_x_weight.shape[0]
    bcw = bc_in.shape[2]
    groups = bcw // STATE
    wide = chan // groups
    width = wide // QUAD
    reach = peers // 2 // QUAD

    bx = conv_x_bias.reshape(1, chan)
    scale = norm_gain.reshape(1, chan)
    owner = (shard % QUAD) ^ (shard // QUAD % 2 * 2)
    info = jnp.stack([shard, shard % QUAD, owner])

    (edge,) = call(
        edge_kernel,
        [],
        [x_in, bc_in],
        [((HALO, chan + 2 * bcw), BF16)],
        1_000_000,
        specs=[HBM] * 2,
        scratch_shapes=[pltpu.VMEM((HALO, 2, bcw), BF16), pltpu.SemaphoreType.DMA((2,))],
    )
    halo = lax.ppermute(edge, "seq", [(i, (i + 1) % peers) for i in range(peers)])
    bc = bc_in.reshape(rows, 2 * bcw)

    def swap(values):
        routes = [[(i, i ^ k) for i in range(peers)] for k in range(QUAD)]
        swapped = {k: lax.ppermute(values[k], "seq", routes[k]) for k in (3, 1, 2)}
        return [values[0], swapped[1], swapped[2], swapped[3]]

    def ahead(value):
        return lax.ppermute(value, "seq", [(i, (i + QUAD) % peers ^ 2) for i in range(peers)])

    early_args = [
        lengths, x_in, conv_x_weight, bx, dt_raw.T, dt_bias.reshape(1, heads), decay.reshape(1, heads),
        conv_bc_weight, conv_bc_bias, skip_d.reshape(1, heads), scale,
    ]
    xc, scaled, top, first, carries, factors, shift, mask, wx, bx, wbc, bbc, skip, scale = call(
        early_kernel,
        [info],
        early_args,
        [
            ((rows, chan), BF16),
            ((rows, chan), BF16),
            ((FIRST, chan), BF16),
            ((FIRST, chan), F32),
            ((EXTRA, chan), BF16),
            ((rows, 6 * heads), BF16),
            (((taps - 1) * BLOCK, HALO + BLOCK), BF16),
            ((BLOCK, BLOCK), F32),
            ((taps, chan), BF16),
            ((1, chan), F32),
            ((taps, 2, bcw), BF16),
            ((2, bcw), F32),
            ((1, heads), F32),
            ((1, chan), F32),
        ],
        600_000_000,
        specs=[HBM] * len(early_args),
        scratch_shapes=[
            pltpu.SMEM(lengths.shape, jnp.int32),
            pltpu.VMEM((rows, chan), BF16),
            pltpu.VMEM((heads, rows), BF16),
            pltpu.VMEM((1, heads), F32),
            pltpu.VMEM((1, heads), F32),
            pltpu.SemaphoreType.DMA((14,)),
        ],
    )
    msgs, tops, bmats = [], [], []
    for g in range(groups):
        *sent, xc_top, bmat = call(
            functools.partial(late_kernel, g),
            [info],
            [top, bc, halo, wx, bx, wbc, bbc, shift, scaled, first, carries],
            [((STATE + EXTRA, width), BF16)] * QUAD + [((FIRST, wide), BF16), ((rows, STATE), BF16)],
            100_000_000,
            scratch_shapes=[pltpu.VMEM((STATE + EXTRA, wide), BF16)],
        )
        msgs.append(swap(sent))
        tops.append(xc_top)
        bmats.append(bmat)

    local = []
    for g in range(groups):
        args = [xc, tops[g], z_in, bc, bmats[g], halo, wbc, bbc, shift, mask, factors, skip]
        outs = [((rows, wide), F32), ((rows, wide), F32), ((rows, STATE), BF16)]
        near = call(
            functools.partial(inner_kernel, g),
            [],
            args,
            outs,
            300_000_000,
            specs=[HBM if arg is z_in else VMEM for arg in args],
            scratch_shapes=[pltpu.VMEM((rows, wide), BF16), pltpu.SemaphoreType.DMA],
        )
        local.append(list(near))
        msgs[g][0], local[g][0] = tie(msgs[g][0], local[g][0])

    entering = []
    for g in range(groups):
        outs = [((STATE, width), BF16)] + [((8, width), F32)] * (reach > 1)
        total, *through = call(fold_kernel, (info,), msgs[g], outs, 1_000_000)
        state = ahead(total)
        for _ in range(reach - 1):
            state = ahead((total.astype(F32) + through[0][0:1] * state.astype(F32)).astype(BF16))
        entering.append(state)

    blocks = []
    for g in range(groups):
        outs = [((STATE, width), BF16)] * QUAD
        blocks.append(swap(call(enter_kernel, (info,), [entering[g], *msgs[g]], outs, 1_000_000)))

    out = None
    for g in range(groups):
        near, gain, cmat = local[g]
        args = [near, gain, *blocks[g], cmat, scale]
        specs = [VMEM] * len(args)
        aliases = {}
        if out is not None:
            aliases = {1 + len(args): 0}
            args.append(out)
            specs.append(ANY)
        (out,) = call(
            functools.partial(finish_kernel, g),
            (info,),
            args,
            [((rows, chan), BF16)],
            100_000_000,
            specs=specs,
            out_specs=[ANY],
            scratch_shapes=[
                pltpu.VMEM((rows, wide), BF16),
                pltpu.VMEM((rows, wide), F32),
                pltpu.SemaphoreType.DMA((4,)),
            ],
            input_output_aliases=aliases,
        )
    return out


def solution(mesh):
    return jax.shard_map(
        shards,
        mesh=mesh,
        in_specs=(
            P(("groups", "seq"), "heads"),
            P(("groups", "seq"), "heads"),
            P(("groups", "seq"), None, "heads"),
            P(None, "heads"),
            P("heads"),
            P(None, None, "heads"),
            P(None, "heads"),
            P(("groups", "seq"), "heads"),
            P("heads"),
            P("heads"),
            P("heads"),
            P("heads"),
            P("groups"),
        ),
        out_specs=P(("groups", "seq"), "heads"),
        check_vma=False,
    )
```

```python
import functools

import jax
import jax.numpy as jnp
from jax import lax
from jax.experimental import pallas as pl
from jax.experimental.pallas import tpu as pltpu
from jax.sharding import PartitionSpec as P

HEAD_DIM = 64
STATE = 128
BLOCK = 128
QUAD = 4
HALO = 8
TILE = 8
EXTRA = 16
FIRST = 16
F32 = jnp.float32
BF16 = jnp.bfloat16


def mm(left, right):
    return jnp.dot(left, right, preferred_element_type=F32)


def ends_of(lens_ref):
    total = 0
    ends = []
    for i in range(lens_ref.shape[0]):
        total = total + lens_ref[i]
        ends.append(total)
    return ends


def seg_of(pos, ends):
    count = 0
    for end in ends:
        count = count + jnp.where(end <= pos, 1, 0)
    return jnp.where(pos >= 0, count, -1)


def tokens(start, shape, dim):
    return start + lax.broadcasted_iota(jnp.int32, shape, dim)


def shift_matrix(start, ends, rows, before, taps):
    shape = (rows, before + rows)
    row = lax.broadcasted_iota(jnp.int32, shape, 0)
    col = lax.broadcasted_iota(jnp.int32, shape, 1)
    same = seg_of(start + row, ends) == seg_of(start - before + col, ends)
    parts = []
    for k in range(taps - 1):
        parts.append(jnp.where((col == row + (before - taps + 1 + k)) & same, 1.0, 0.0))
    return jnp.concatenate(parts, axis=0).astype(BF16)


def conv_half(shift, extended, block, weight, bias):
    rows = block.shape[0]
    taps = weight.shape[0]
    half = weight.astype(F32) * 0.5
    moved = mm(shift, extended)
    total = bias * 0.5 + block.astype(F32) * half[taps - 1 : taps]
    for k in range(taps - 1):
        total = total + moved[k * rows : (k + 1) * rows] * half[k : k + 1]
    return total


def silu_of_half(half):
    return half + half * jnp.tanh(half)


def rates_of(dt_ref, dtb_ref, dec_ref):
    raw = jnp.transpose(dt_ref[...].astype(F32)) + dtb_ref[...]
    rate = jnp.maximum(raw, 0.0) + jnp.log1p(jnp.exp(-jnp.abs(raw)))
    shape = (BLOCK, BLOCK)
    lower = lax.broadcasted_iota(jnp.int32, shape, 0) >= lax.broadcasted_iota(jnp.int32, shape, 1)
    cum = jnp.dot(
        jnp.where(lower, 1.0, 0.0),
        -rate * dec_ref[...],
        precision=lax.Precision.HIGHEST,
        preferred_element_type=F32,
    )
    return rate, cum


def head_map(heads, first, width):
    shape = (heads, width)
    row = lax.broadcasted_iota(jnp.int32, shape, 0)
    col = lax.broadcasted_iota(jnp.int32, shape, 1)
    return jnp.where(row == first + col // HEAD_DIM, 1.0, 0.0).astype(BF16)


def pair_of(value):
    high = value.astype(BF16)
    low = (value - high.astype(F32)).astype(BF16)
    return jnp.concatenate([high, low], axis=1)


def twice(onehot):
    return jnp.concatenate([onehot, onehot], axis=0)


def next_matrix(start, ends, taps):
    shape = (TILE, BLOCK)
    row = lax.broadcasted_iota(jnp.int32, shape, 0)
    col = lax.broadcasted_iota(jnp.int32, shape, 1)
    same = seg_of(start + BLOCK + row, ends) == seg_of(start + col, ends)
    parts = []
    for k in range(taps - 1):
        parts.append(jnp.where((col == row + (BLOCK - taps + 1 + k)) & same, 1.0, 0.0))
    return jnp.concatenate(parts, axis=0).astype(BF16)


def conv_both(moves, block, weight, bias):
    taps = weight.shape[0]
    half = weight.astype(F32) * 0.5
    moved = mm(moves, block)
    total = bias * 0.5 + block.astype(F32) * half[taps - 1 : taps]
    after = 0.0
    base = (taps - 1) * BLOCK
    for k in range(taps - 1):
        total = total + moved[k * BLOCK : (k + 1) * BLOCK] * half[k : k + 1]
        after = after + moved[base + k * TILE : base + (k + 1) * TILE] * half[k : k + 1]
    return total, after


def bc_weight(which, lane, wbc):
    return jnp.concatenate([wbc[k].astype(F32)[which : which + 1, lane] for k in range(wbc.shape[0])], axis=0)


def send_states(g, mine, x, bc, wx, bx, wbc, bbc, moves, factor, carry, xc_out, msgs, held):
    taps = wx.shape[0]
    chan = x.shape[1]
    wide = xc_out.shape[1]
    heads = carry.shape[1] // 2
    width = wide // QUAD
    lane = slice(g * STATE, (g + 1) * STATE)
    btotal, bafter = conv_both(moves[...], bc[:, lane], bc_weight(0, lane, wbc), bbc[0:1, lane])
    bmat = silu_of_half(btotal)
    bmat = jnp.where(tokens(0, bmat.shape, 0) >= taps - 1, bmat, 0.0)
    bmat_t = jnp.transpose(bmat).astype(BF16)
    bparts = jnp.concatenate([btotal[0:TILE], bafter] + [jnp.zeros_like(bafter)] * (width // STATE - 2), axis=1)
    bparts = pltpu.roll(bparts, taps - 1, 0)
    step = 1024
    for at in range(0, wide, step):
        here = slice(at, at + step)
        deep = slice(g * wide + at, g * wide + at + step)
        onehot2 = twice(head_map(heads, (g * wide + at) // HEAD_DIM, step))
        total, after = conv_both(moves[...], x[:, deep], wx[:, deep], bx[:, deep])
        xc = silu_of_half(total).astype(BF16)
        xc_out[:, here] = xc
        spread = mm(factor[...], onehot2)
        held[0:STATE, here] = mm(bmat_t, (xc.astype(F32) * spread).astype(BF16)).astype(BF16)
        row = lax.broadcasted_iota(jnp.int32, (TILE, step), 0)
        passed = mm(carry[...], onehot2[0 : 2 * heads])
        high = passed.astype(BF16).astype(F32)
        upper = jnp.where(row < 2 + taps - 1, pltpu.roll(total[0:TILE], 2, 0), pltpu.roll(after, 1 + taps, 0))
        upper = jnp.where(row == 0, high, jnp.where(row == 1, passed - high, upper))
        lower = jnp.where(row < taps - 1, spread[0:TILE], jnp.concatenate([bparts] * (step // width), axis=1))
        held[STATE : STATE + EXTRA, here] = jnp.concatenate([upper, lower], axis=0).astype(BF16)
    for k, msg in enumerate(msgs):
        msg[...] = held[:, pl.ds(pl.multiple_of((mine ^ k) * width, width), width)]


def first_kernel(
    info, lens_in, x_in, bc_in, wx_in, bx_in, dt_in, dtb_in, dec_in, wbc_in, bbc_in, skip_in, scale_in,
    x, bc, moves, shift, mask, factors, factor, carry, wx, bx, wbc, bbc, skip, scale, xc_out, m0, m1, m2, m3,
    lens, raw, dt, dtb, dec, held, sems,
):
    heads = dt.shape[0]
    wide = xc_out.shape[1]
    inner = bc.shape[1] // 2
    pairs = [
        (lens_in, lens), (dt_in, dt), (dtb_in, dtb), (dec_in, dec), (bc_in, raw), (wx_in, wx), (bx_in, bx),
        (wbc_in, wbc), (bbc_in, bbc), (x_in.at[:, 0:wide], x.at[:, 0:wide]), (x_in.at[:, wide:], x.at[:, wide:]),
        (skip_in, skip), (scale_in, scale),
    ]
    copies = [pltpu.make_async_copy(src, dst, sems.at[i]) for i, (src, dst) in enumerate(pairs)]
    for copy in copies:
        copy.start()
    for copy in copies[0:4]:
        copy.wait()
    start = info[0] * BLOCK
    taps = wx.shape[0]
    ends = ends_of(lens)
    moves[0 : (taps - 1) * BLOCK, :] = shift_matrix(start, ends, BLOCK, 0, taps)
    moves[(taps - 1) * BLOCK :, :] = next_matrix(start, ends, taps)
    shift[...] = shift_matrix(start, ends, BLOCK, HALO, taps)
    shape = (BLOCK, BLOCK)
    row = lax.broadcasted_iota(jnp.int32, shape, 0)
    col = lax.broadcasted_iota(jnp.int32, shape, 1)
    seg_row = seg_of(start + row, ends)
    mask[...] = jnp.where((row >= col) & (seg_row == seg_of(start + col, ends)), 1.0, 0.0)
    rate, cum = rates_of(dt, dtb, dec)
    last = cum[BLOCK - 1 : BLOCK]
    seg_last = seg_of(start + BLOCK - 1, ends)
    seg_head = seg_row[:, 0:heads]
    factor[...] = pair_of(jnp.where(seg_head == seg_last, jnp.exp(last - cum), 0.0) * rate)
    grown = jnp.exp(cum)
    before = seg_of(start - 1, ends)
    factors[:, 0 : 2 * heads] = pair_of(rate * jnp.exp(-cum))
    factors[:, 2 * heads : 4 * heads] = pair_of(grown)
    factors[:, 4 * heads : 6 * heads] = pair_of(jnp.where(seg_head == before, grown, 0.0))
    passed = jnp.where(seg_last == before, jnp.exp(last), 0.0)
    carry[...] = pair_of(jnp.broadcast_to(passed, (TILE, heads)))
    for copy in copies[4:9]:
        copy.wait()
    value = raw[...].astype(F32)
    for i in range(2):
        bc[:, i * inner : (i + 1) * inner] = value[:, i, :].astype(BF16)
    copies[9].wait()
    send_states(0, info[2], x, bc, wx, bx, wbc, bbc, moves, factor, carry, xc_out, (m0, m1, m2, m3), held)
    for copy in copies[10:]:
        copy.wait()


def other_kernel(g, info, x, bc, wx, bx, wbc, bbc, moves, factor, carry, xc_out, edge, m0, m1, m2, m3, held):
    send_states(g, info[2], x, bc, wx, bx, wbc, bbc, moves, factor, carry, xc_out, (m0, m1, m2, m3), held)
    rows, chan = x.shape
    edge[:, 0:chan] = x[rows - HALO : rows, :]
    edge[:, chan:] = bc[rows - HALO : rows, :]


def extra_of(msg):
    value = msg[STATE : STATE + EXTRA, :].astype(F32)
    return value[0:TILE], value[TILE:EXTRA]


def top_state(taps, here, prior):
    upper, lower = here
    total = pltpu.roll(upper, TILE - 2, 0)
    btotal = pltpu.roll(lower[:, 0:STATE], TILE - taps + 1, 0)
    if prior is not None:
        total = total + pltpu.roll(prior[0], TILE - 1 - taps, 0)
        btotal = btotal + pltpu.roll(prior[1][:, STATE : 2 * STATE], TILE - taps + 1, 0)
    xc = silu_of_half(total).astype(BF16).astype(F32)
    scaled = jnp.where(tokens(0, xc.shape, 0) < taps - 1, xc * lower, 0.0)
    bmat = jnp.where(tokens(0, btotal.shape, 0) < taps - 1, silu_of_half(btotal), 0.0)
    scaled = jnp.concatenate([scaled, jnp.zeros_like(scaled)], axis=0).astype(BF16)
    bmat = jnp.concatenate([bmat, jnp.zeros_like(bmat)], axis=0).astype(BF16)
    return lax.dot_general(bmat, scaled, (((0,), (0,)), ((), ())), preferred_element_type=F32)


def carry_row(extra):
    return extra[0][0:1] + extra[0][1:2]


def fold_kernel(taps, more, info, *refs):
    msgs, rest = refs[0:QUAD], refs[QUAD:]
    total, fixed = rest[more], rest[more + 1]
    for mine in range(QUAD):

        @pl.when(info[1] == mine)
        def _():
            block = [msgs[mine ^ b] for b in range(QUAD)]
            extra = [extra_of(msg) for msg in block]
            prior = extra_of(rest[0]) if more else None
            state = block[0][0:STATE, :].astype(F32) + top_state(taps, extra[0], prior)
            through = carry_row(extra[0])
            for b in range(1, QUAD):
                own = block[b][0:STATE, :].astype(F32) + top_state(taps, extra[b], extra[b - 1])
                if b < QUAD - 1:
                    fixed[(b - 1) * STATE : b * STATE, :] = own.astype(BF16)
                state = own + carry_row(extra[b]) * state
                through = through * carry_row(extra[b])
            total[0:STATE, :] = state.astype(BF16)
            total[STATE : STATE + EXTRA, :] = block[QUAD - 1][STATE : STATE + EXTRA, :]
            for out in rest[more + 2 :]:
                out[...] = jnp.broadcast_to(through, out.shape)


def enter_kernel(taps, info, start, fixed, m0, m1, m2, m3, o0, o1, o2, o3):
    msgs = (m0, m1, m2, m3)
    outs = (o0, o1, o2, o3)
    prior = extra_of(start)
    for mine in range(QUAD):

        @pl.when(info[1] == mine)
        def _():
            outs[mine][...] = start[0:STATE, :]
            head = extra_of(msgs[mine])
            state = msgs[mine][0:STATE, :].astype(F32) + top_state(taps, head, prior)
            state = state + carry_row(head) * start[0:STATE, :].astype(F32)
            outs[mine ^ 1][...] = state.astype(BF16)
            for b in range(2, QUAD):
                own = fixed[(b - 2) * STATE : (b - 1) * STATE, :].astype(F32)
                state = own + carry_row(extra_of(msgs[mine ^ (b - 1)])) * state
                outs[mine ^ b][...] = state.astype(BF16)


def joined(above, below):
    return jnp.concatenate([above.astype(F32), below.astype(F32)], axis=0).astype(BF16)


def bc_conv(which, g, shift, halo, bc, wbc, bbc):
    inner = wbc.shape[2]
    chan = halo.shape[1] - 2 * inner
    base = which * inner + g * STATE
    lane = slice(g * STATE, (g + 1) * STATE)
    block = bc[:, base : base + STATE]
    ext = joined(halo[:, chan + base : chan + base + STATE], block)
    half = conv_half(shift[...], ext, block, bc_weight(which, lane, wbc), bbc[which : which + 1, lane])
    return silu_of_half(half).astype(BF16)


def inner_kernel(
    g, xc_in, x, z_in, bc, halo, wx, bx, wbc, bbc, shift, mask, factors, skip, near, gain, c_out, z, sem
):
    wide = xc_in.shape[1]
    copy = pltpu.make_async_copy(z_in.at[:, g * wide : (g + 1) * wide], z, sem)
    copy.start()
    heads = skip.shape[1]
    taps = wx.shape[0]
    cmat = bc_conv(1, g, shift, halo, bc, wbc, bbc)
    c_out[...] = cmat
    bmat = bc_conv(0, g, shift, halo, bc, wbc, bbc)
    scores = lax.dot_general(cmat, bmat, (((1,), (1,)), ((), ())), preferred_element_type=F32)
    scores = (scores * mask[...]).astype(BF16)
    skips = pair_of(jnp.broadcast_to(skip[...], (8, heads)))
    cols = slice(0, HALO + FIRST)
    moves = jnp.concatenate([shift[k * BLOCK : k * BLOCK + FIRST, cols] for k in range(taps - 1)], axis=0)
    step = 1024
    copy.wait()
    for at in range(0, wide, step):
        lane = slice(at, at + step)
        deep = slice(g * wide + at, g * wide + at + step)
        onehot2 = twice(head_map(heads, (g * wide + at) // HEAD_DIM, step))
        top = x[0:FIRST, deep]
        xc_top = silu_of_half(conv_half(moves, joined(halo[:, deep], top), top, wx[:, deep], bx[:, deep]))
        xf = jnp.concatenate([xc_top.astype(BF16), xc_in[FIRST:, lane]], axis=0).astype(F32)
        scaled = (xf * mm(factors[:, 0 : 2 * heads], onehot2)).astype(BF16)
        grown = mm(factors[:, 2 * heads : 4 * heads], onehot2)
        skip_c = mm(skips, onehot2)[0:1]
        gate = silu_of_half(z[:, lane].astype(F32) * 0.5)
        near[:, lane] = (mm(scores, scaled) * grown + skip_c * xf) * gate
        gain[:, lane] = mm(factors[:, 4 * heads : 6 * heads], onehot2) * gate


def finish_kernel(g, info, near, gain, e0, e1, e2, e3, cmat, scale, *rest):
    out, ready, held, sems = rest[-4:]
    mine = info[2]
    rows, wide = near.shape
    width = wide // QUAD
    steps = sems.shape[0]
    part = rows // steps
    square = [0.0] * steps
    ats = [pl.ds(pl.multiple_of((mine ^ k) * width, width), width) for k in range(QUAD)]
    c = cmat[...]
    for at, e in zip(ats, (e0, e1, e2, e3)):
        far = mm(c, e[...])
        for i in range(steps):
            these = slice(i * part, (i + 1) * part)
            value = near[these, at] + gain[these, at] * far[these]
            square[i] = square[i] + jnp.sum(value * value, axis=1, keepdims=True)
            held[these, at] = value
    copies = []
    for i in range(steps):
        these = slice(i * part, (i + 1) * part)
        inv = lax.rsqrt(square[i] * (1.0 / wide) + 1e-05)
        ready[these, :] = (held[these, :] * inv * scale[:, g * wide : (g + 1) * wide]).astype(BF16)
        copy = pltpu.make_async_copy(ready.at[these, :], out.at[these, g * wide : (g + 1) * wide], sems.at[i])
        copy.start()
        copies.append(copy)
    for copy in copies:
        copy.wait()


SMEM = pl.BlockSpec(memory_space=pltpu.SMEM)
VMEM = pl.BlockSpec(memory_space=pltpu.VMEM)
ANY = pl.BlockSpec(memory_space=pl.ANY)
HBM = pl.BlockSpec(memory_space=pltpu.HBM)


def call(kernel, scalars, args, outs, flops, limit=32 << 20, **more):
    pinned = more.get("specs", ())
    args = [
        pltpu.with_memory_space_constraint(arg, pltpu.HBM) if i < len(pinned) and pinned[i] is HBM else arg
        for i, arg in enumerate(args)
    ]
    return pl.pallas_call(
        kernel,
        in_specs=[SMEM] * len(scalars) + more.pop("specs", [VMEM] * len(args)),
        out_specs=more.pop("out_specs", [VMEM] * len(outs)),
        out_shape=[jax.ShapeDtypeStruct(*out) for out in outs],
        cost_estimate=pl.CostEstimate(flops=flops, bytes_accessed=4 << 20, transcendentals=0),
        compiler_params=pltpu.CompilerParams(vmem_limit_bytes=limit),
        **more,
    )(*scalars, *args)


def tie(first, second):
    return lax.optimization_barrier((first, second))


def shards(
    x_in,
    z_in,
    bc_in,
    conv_x_weight,
    conv_x_bias,
    conv_bc_weight,
    conv_bc_bias,
    dt_raw,
    dt_bias,
    decay,
    skip_d,
    norm_gain,
    lengths,
):
    rows, chan = x_in.shape
    heads = dt_raw.shape[1]
    peers = lax.axis_size("seq")
    shard = lax.axis_index("seq").astype(jnp.int32)
    taps = conv_x_weight.shape[0]
    bcw = bc_in.shape[2]
    groups = bcw // STATE
    wide = chan // groups
    width = wide // QUAD
    reach = peers // 2 // QUAD

    bx = conv_x_bias.reshape(1, chan)
    scale = norm_gain.reshape(1, chan)
    owner = (shard % QUAD) ^ (shard // QUAD % 2 * 2)
    info = jnp.stack([shard, shard % QUAD, owner])

    def swap(values):
        routes = [[(i, i ^ k) for i in range(peers)] for k in range(QUAD)]
        swapped = {k: lax.ppermute(values[k], "seq", routes[k]) for k in (3, 1, 2)}
        return [values[0], swapped[1], swapped[2], swapped[3]]

    def ahead(value):
        return lax.ppermute(value, "seq", [(i, (i + QUAD) % peers ^ 2) for i in range(peers)])

    first_args = [
        lengths, x_in, bc_in, conv_x_weight, bx, dt_raw.T, dt_bias.reshape(1, heads), decay.reshape(1, heads),
        conv_bc_weight, conv_bc_bias, skip_d.reshape(1, heads), scale,
    ]
    sent = ((STATE + EXTRA, width), BF16)
    held = pltpu.VMEM((STATE + EXTRA, wide), BF16)
    x, bc, moves, shift, mask, factors, factor, carry, wx, bx, wbc, bbc, skip, scale, xc, *msg = call(
        first_kernel,
        [info],
        first_args,
        [
            ((rows, chan), BF16),
            ((rows, 2 * bcw), BF16),
            (((taps - 1) * (BLOCK + TILE), BLOCK), BF16),
            (((taps - 1) * BLOCK, HALO + BLOCK), BF16),
            ((BLOCK, BLOCK), F32),
            ((rows, 6 * heads), BF16),
            ((rows, 2 * heads), BF16),
            ((TILE, 2 * heads), BF16),
            ((taps, chan), BF16),
            ((1, chan), F32),
            ((taps, 2, bcw), BF16),
            ((2, bcw), F32),
            ((1, heads), F32),
            ((1, chan), F32),
            ((rows, wide), BF16),
            *[sent] * QUAD,
        ],
        600_000_000,
        specs=[HBM] * len(first_args),
        scratch_shapes=[
            pltpu.SMEM(lengths.shape, jnp.int32),
            pltpu.VMEM((rows, 2, bcw), BF16),
            pltpu.VMEM((heads, rows), BF16),
            pltpu.VMEM((1, heads), F32),
            pltpu.VMEM((1, heads), F32),
            held,
            pltpu.SemaphoreType.DMA((13,)),
        ],
    )
    xcs, msgs = [xc], [swap(msg)]
    for g in range(1, groups):
        xc, edge, *msg = call(
            functools.partial(other_kernel, g),
            [info],
            [x, bc, wx, bx, wbc, bbc, moves, factor, carry],
            [((rows, wide), BF16), ((HALO, chan + 2 * bcw), BF16), *[sent] * QUAD],
            300_000_000,
            scratch_shapes=[held],
        )
        xcs.append(xc)
        msgs.append(swap(msg))
    halo = lax.ppermute(edge, "seq", [(i, (i + 1) % peers) for i in range(peers)])

    local = []
    for g in range(groups):
        args = [xcs[g], x, z_in, bc, halo, wx, bx, wbc, bbc, shift, mask, factors, skip]
        outs = [((rows, wide), F32), ((rows, wide), F32), ((rows, STATE), BF16)]
        near = call(
            functools.partial(inner_kernel, g),
            [],
            args,
            outs,
            300_000_000,
            specs=[HBM if arg is z_in else VMEM for arg in args],
            scratch_shapes=[pltpu.VMEM((rows, wide), BF16), pltpu.SemaphoreType.DMA],
        )
        local.append(list(near))

    entering, fixes = [], []
    for g in range(groups):
        outs = [sent, (((QUAD - 2) * STATE, width), BF16)]
        args = list(msgs[g])
        if reach > 1:
            outs.append(((8, width), F32))
            args.append(ahead(lax.dynamic_index_in_dim(jnp.stack(args), shard % QUAD ^ (QUAD - 1), 0, False)))
        total, fixed, *through = call(
            functools.partial(fold_kernel, taps, len(args) - QUAD), (info,), args, outs, 1_000_000
        )
        state = ahead(total)
        for _ in range(reach - 1):
            own = total[0:STATE].astype(F32) + through[0][0:1] * state[0:STATE].astype(F32)
            state = ahead(jnp.concatenate([own.astype(BF16), total[STATE:]], axis=0))
        entering.append(state)
        fixes.append(fixed)

    blocks = []
    for g in range(groups):
        outs = [((STATE, width), BF16)] * QUAD
        kernel = functools.partial(enter_kernel, taps)
        blocks.append(swap(call(kernel, (info,), [entering[g], fixes[g], *msgs[g]], outs, 1_000_000)))

    out = None
    for g in range(groups):
        near, gain, cmat = local[g]
        args = [near, gain, *blocks[g], cmat, scale]
        specs = [VMEM] * len(args)
        aliases = {}
        if out is not None:
            aliases = {1 + len(args): 0}
            args.append(out)
            specs.append(ANY)
        (out,) = call(
            functools.partial(finish_kernel, g),
            (info,),
            args,
            [((rows, chan), BF16)],
            100_000_000,
            specs=specs,
            out_specs=[ANY],
            scratch_shapes=[
                pltpu.VMEM((rows, wide), BF16),
                pltpu.VMEM((rows, wide), F32),
                pltpu.SemaphoreType.DMA((4,)),
            ],
            input_output_aliases=aliases,
        )
    return out


def solution(mesh):
    return jax.shard_map(
        shards,
        mesh=mesh,
        in_specs=(
            P(("groups", "seq"), "heads"),
            P(("groups", "seq"), "heads"),
            P(("groups", "seq"), None, "heads"),
            P(None, "heads"),
            P("heads"),
            P(None, None, "heads"),
            P(None, "heads"),
            P(("groups", "seq"), "heads"),
            P("heads"),
            P("heads"),
            P("heads"),
            P("heads"),
            P("groups"),
        ),
        out_specs=P(("groups", "seq"), "heads"),
        check_vma=False,
    )
```

```python
import functools

import jax
import jax.numpy as jnp
from jax import lax
from jax.experimental import pallas as pl
from jax.experimental.pallas import tpu as pltpu
from jax.sharding import PartitionSpec as P

HEAD_DIM = 64
STATE = 128
BLOCK = 128
QUAD = 4
TILE = 8
EXTRA = 16
F32 = jnp.float32
BF16 = jnp.bfloat16


def mm(left, right):
    return jnp.dot(left, right, preferred_element_type=F32)


def ends_of(lens_ref):
    total = 0
    ends = []
    for i in range(lens_ref.shape[0]):
        total = total + lens_ref[i]
        ends.append(total)
    return ends


def seg_of(pos, ends):
    count = 0
    for end in ends:
        count = count + jnp.where(end <= pos, 1, 0)
    return jnp.where(pos >= 0, count, -1)


def tokens(start, shape, dim):
    return start + lax.broadcasted_iota(jnp.int32, shape, dim)


def shift_matrix(start, ends, rows, before, taps):
    shape = (rows, before + rows)
    row = lax.broadcasted_iota(jnp.int32, shape, 0)
    col = lax.broadcasted_iota(jnp.int32, shape, 1)
    same = seg_of(start + row, ends) == seg_of(start - before + col, ends)
    parts = []
    for k in range(taps - 1):
        parts.append(jnp.where((col == row + (before - taps + 1 + k)) & same, 1.0, 0.0))
    return jnp.concatenate(parts, axis=0).astype(BF16)


def conv_half(shift, extended, block, weight, bias):
    rows = block.shape[0]
    taps = weight.shape[0]
    half = weight.astype(F32) * 0.5
    moved = mm(shift, extended)
    total = bias * 0.5 + block.astype(F32) * half[taps - 1 : taps]
    for k in range(taps - 1):
        total = total + moved[k * rows : (k + 1) * rows] * half[k : k + 1]
    return total


def silu_of_half(half):
    return half + half * jnp.tanh(half)


def rates_of(dt_ref, dtb_ref, dec_ref):
    raw = jnp.transpose(dt_ref[...].astype(F32)) + dtb_ref[...]
    rate = jnp.maximum(raw, 0.0) + jnp.log1p(jnp.exp(-jnp.abs(raw)))
    shape = (BLOCK, BLOCK)
    lower = lax.broadcasted_iota(jnp.int32, shape, 0) >= lax.broadcasted_iota(jnp.int32, shape, 1)
    cum = jnp.dot(
        jnp.where(lower, 1.0, 0.0),
        -rate * dec_ref[...],
        precision=lax.Precision.HIGHEST,
        preferred_element_type=F32,
    )
    return rate, cum


def head_map(heads, first, width):
    shape = (heads, width)
    row = lax.broadcasted_iota(jnp.int32, shape, 0)
    col = lax.broadcasted_iota(jnp.int32, shape, 1)
    return jnp.where(row == first + col // HEAD_DIM, 1.0, 0.0).astype(BF16)


def pair_of(value):
    high = value.astype(BF16)
    low = (value - high.astype(F32)).astype(BF16)
    return jnp.concatenate([high, low], axis=1)


def twice(onehot):
    return jnp.concatenate([onehot, onehot], axis=0)


def next_matrix(start, ends, taps):
    shape = (TILE, BLOCK)
    row = lax.broadcasted_iota(jnp.int32, shape, 0)
    col = lax.broadcasted_iota(jnp.int32, shape, 1)
    same = seg_of(start + BLOCK + row, ends) == seg_of(start + col, ends)
    parts = []
    for k in range(taps - 1):
        parts.append(jnp.where((col == row + (BLOCK - taps + 1 + k)) & same, 1.0, 0.0))
    return jnp.concatenate(parts, axis=0).astype(BF16)


def conv_both(moves, block, weight, bias):
    taps = weight.shape[0]
    half = weight.astype(F32) * 0.5
    moved = mm(moves, block)
    total = bias * 0.5 + block.astype(F32) * half[taps - 1 : taps]
    after = 0.0
    base = (taps - 1) * BLOCK
    for k in range(taps - 1):
        total = total + moved[k * BLOCK : (k + 1) * BLOCK] * half[k : k + 1]
        after = after + moved[base + k * TILE : base + (k + 1) * TILE] * half[k : k + 1]
    return total, after


def bc_weight(which, lane, wbc):
    return jnp.concatenate([wbc[k].astype(F32)[which : which + 1, lane] for k in range(wbc.shape[0])], axis=0)


def send_states(g, mine, x, bc, wx, bx, wbc, bbc, moves, factor, carry, xc_out, msgs, held):
    taps = wx.shape[0]
    chan = x.shape[1]
    wide = xc_out.shape[1]
    heads = carry.shape[1] // 2
    width = wide // QUAD
    lane = slice(g * STATE, (g + 1) * STATE)
    inner = wbc.shape[2]
    btotal, bafter = conv_both(moves[...], bc[:, lane], bc_weight(0, lane, wbc), bbc[0:1, lane])
    cblock = bc[:, inner + g * STATE : inner + (g + 1) * STATE]
    ctotal, cafter = conv_both(moves[...], cblock, bc_weight(1, lane, wbc), bbc[1:2, lane])
    bmat = silu_of_half(btotal)
    bmat = jnp.where(tokens(0, bmat.shape, 0) >= taps - 1, bmat, 0.0)
    bmat_t = jnp.transpose(bmat).astype(BF16)
    bparts = jnp.concatenate([btotal[0:TILE], bafter, ctotal[0:TILE], cafter], axis=1)
    bparts = pltpu.roll(bparts, taps - 1, 0)
    step = 1024
    for at in range(0, wide, step):
        here = slice(at, at + step)
        deep = slice(g * wide + at, g * wide + at + step)
        onehot2 = twice(head_map(heads, (g * wide + at) // HEAD_DIM, step))
        total, after = conv_both(moves[...], x[:, deep], wx[:, deep], bx[:, deep])
        xc = silu_of_half(total).astype(BF16)
        xc_out[:, here] = xc
        spread = mm(factor[...], onehot2)
        held[0:STATE, here] = mm(bmat_t, (xc.astype(F32) * spread).astype(BF16)).astype(BF16)
        row = lax.broadcasted_iota(jnp.int32, (TILE, step), 0)
        passed = mm(carry[...], onehot2[0 : 2 * heads])
        high = passed.astype(BF16).astype(F32)
        upper = jnp.where(row < 2 + taps - 1, pltpu.roll(total[0:TILE], 2, 0), pltpu.roll(after, 1 + taps, 0))
        upper = jnp.where(row == 0, high, jnp.where(row == 1, passed - high, upper))
        lower = jnp.where(row < taps - 1, spread[0:TILE], jnp.concatenate([bparts] * (step // width), axis=1))
        held[STATE : STATE + EXTRA, here] = jnp.concatenate([upper, lower], axis=0).astype(BF16)
    for k, msg in enumerate(msgs):
        msg[...] = held[:, pl.ds(pl.multiple_of((mine ^ k) * width, width), width)]


def first_kernel(
    info, lens_in, x_in, bc_in, wx_in, bx_in, dt_in, dtb_in, dec_in, wbc_in, bbc_in, skip_in, scale_in,
    x, bc, moves, mask, live, factors, factor, carry, wx, bx, wbc, bbc, skip, scale, xc_out, m0, m1, m2, m3,
    lens, raw, dt, dtb, dec, held, sems,
):
    heads = dt.shape[0]
    wide = xc_out.shape[1]
    inner = bc.shape[1] // 2
    pairs = [
        (lens_in, lens), (dt_in, dt), (dtb_in, dtb), (dec_in, dec), (bc_in, raw), (wx_in, wx), (bx_in, bx),
        (wbc_in, wbc), (bbc_in, bbc), (x_in.at[:, 0:wide], x.at[:, 0:wide]), (x_in.at[:, wide:], x.at[:, wide:]),
        (skip_in, skip), (scale_in, scale),
    ]
    copies = [pltpu.make_async_copy(src, dst, sems.at[i]) for i, (src, dst) in enumerate(pairs)]
    for copy in copies:
        copy.start()
    for copy in copies[0:4]:
        copy.wait()
    start = info[0] * BLOCK
    taps = wx.shape[0]
    ends = ends_of(lens)
    moves[0 : (taps - 1) * BLOCK, :] = shift_matrix(start, ends, BLOCK, 0, taps)
    moves[(taps - 1) * BLOCK :, :] = next_matrix(start, ends, taps)
    shape = (BLOCK, BLOCK)
    row = lax.broadcasted_iota(jnp.int32, shape, 0)
    col = lax.broadcasted_iota(jnp.int32, shape, 1)
    seg_row = seg_of(start + row, ends)
    mask[...] = jnp.where((row >= col) & (seg_row == seg_of(start + col, ends)), 1.0, 0.0)
    rate, cum = rates_of(dt, dtb, dec)
    last = cum[BLOCK - 1 : BLOCK]
    seg_last = seg_of(start + BLOCK - 1, ends)
    seg_head = seg_row[:, 0:heads]
    factor[...] = pair_of(jnp.where(seg_head == seg_last, jnp.exp(last - cum), 0.0) * rate)
    grown = jnp.exp(cum)
    before = seg_of(start - 1, ends)
    factors[:, 0 : 2 * heads] = pair_of(rate * jnp.exp(-cum))
    factors[:, 2 * heads : 4 * heads] = pair_of(grown)
    live[...] = jnp.where(seg_row == before, 1.0, 0.0)
    passed = jnp.where(seg_last == before, jnp.exp(last), 0.0)
    carry[...] = pair_of(jnp.broadcast_to(passed, (TILE, heads)))
    for copy in copies[4:9]:
        copy.wait()
    value = raw[...].astype(F32)
    for i in range(2):
        bc[:, i * inner : (i + 1) * inner] = value[:, i, :].astype(BF16)
    copies[9].wait()
    send_states(0, info[2], x, bc, wx, bx, wbc, bbc, moves, factor, carry, xc_out, (m0, m1, m2, m3), held)
    for copy in copies[10:]:
        copy.wait()


def other_kernel(g, info, x, bc, wx, bx, wbc, bbc, moves, factor, carry, xc_out, m0, m1, m2, m3, held):
    send_states(g, info[2], x, bc, wx, bx, wbc, bbc, moves, factor, carry, xc_out, (m0, m1, m2, m3), held)


def extra_of(msg):
    value = msg[STATE : STATE + EXTRA, :].astype(F32)
    return value[0:TILE], value[TILE:EXTRA]


def top_state(taps, here, prior):
    upper, lower = here
    total = pltpu.roll(upper, TILE - 2, 0)
    parts = pltpu.roll(lower, TILE - taps + 1, 0)
    btotal, ctotal = parts[:, 0:STATE], parts[:, 2 * STATE : 3 * STATE]
    if prior is not None:
        total = total + pltpu.roll(prior[0], TILE - 1 - taps, 0)
        parts = pltpu.roll(prior[1], TILE - taps + 1, 0)
        btotal, ctotal = btotal + parts[:, STATE : 2 * STATE], ctotal + parts[:, 3 * STATE : 4 * STATE]
    xc = silu_of_half(total).astype(BF16).astype(F32)
    xc = jnp.where(tokens(0, xc.shape, 0) < taps - 1, xc, 0.0)
    both = silu_of_half(jnp.concatenate([btotal, ctotal], axis=1))
    both = jnp.where(tokens(0, both.shape, 0) < taps - 1, both, 0.0)
    rows = jnp.concatenate([xc, jnp.concatenate([both, jnp.zeros_like(both)], axis=1)], axis=0).astype(BF16)
    scaled, bmat = xc * lower, both[:, 0:STATE]
    scaled = jnp.concatenate([scaled, jnp.zeros_like(scaled)], axis=0).astype(BF16)
    bmat = jnp.concatenate([bmat, jnp.zeros_like(bmat)], axis=0).astype(BF16)
    return lax.dot_general(bmat, scaled, (((0,), (0,)), ((), ())), preferred_element_type=F32), rows


def carry_row(extra):
    return extra[0][0:1] + extra[0][1:2]


def fold_kernel(taps, more, info, *refs):
    msgs, rest = refs[0:QUAD], refs[QUAD:]
    total, fixed = rest[more], rest[more + 1]
    for mine in range(QUAD):

        @pl.when(info[1] == mine)
        def _():
            block = [msgs[mine ^ b] for b in range(QUAD)]
            extra = [extra_of(msg) for msg in block]
            add, _ = top_state(taps, extra[0], extra_of(rest[0]) if more else None)
            state = block[0][0:STATE, :].astype(F32) + add
            through = carry_row(extra[0])
            for b in range(1, QUAD):
                add, rows = top_state(taps, extra[b], extra[b - 1])
                own = block[b][0:STATE, :].astype(F32) + add
                fixed[b - 1, 0:STATE, :] = own.astype(BF16)
                fixed[b - 1, STATE : STATE + EXTRA, :] = rows
                state = own + carry_row(extra[b]) * state
                through = through * carry_row(extra[b])
            total[0:STATE, :] = state.astype(BF16)
            total[STATE : STATE + EXTRA, :] = block[QUAD - 1][STATE : STATE + EXTRA, :]
            for out in rest[more + 2 :]:
                out[...] = jnp.broadcast_to(through, out.shape)


def enter_kernel(taps, info, start, fixed, m0, m1, m2, m3, o0, o1, o2, o3):
    msgs = (m0, m1, m2, m3)
    outs = (o0, o1, o2, o3)
    lower = slice(STATE, STATE + EXTRA)
    prior = extra_of(start)
    for mine in range(QUAD):

        @pl.when(info[1] == mine)
        def _():
            head = extra_of(msgs[mine])
            add, rows = top_state(taps, head, prior)
            outs[mine][0:STATE, :] = start[0:STATE, :]
            outs[mine][lower, :] = rows
            state = msgs[mine][0:STATE, :].astype(F32) + add
            state = state + carry_row(head) * start[0:STATE, :].astype(F32)
            for b in range(1, QUAD):
                outs[mine ^ b][0:STATE, :] = state.astype(BF16)
                outs[mine ^ b][lower, :] = fixed[b - 1, lower, :]
                if b < QUAD - 1:
                    own = fixed[b - 1, 0:STATE, :].astype(F32)
                    state = own + carry_row(extra_of(msgs[mine ^ b])) * state


def inner_kernel(g, xc_in, z_in, bc, wbc, bbc, moves, mask, factors, skip, near, gain, c_out, rate_top, kept_top, z, sem):
    wide = xc_in.shape[1]
    copy = pltpu.make_async_copy(z_in.at[:, g * wide : (g + 1) * wide], z, sem)
    copy.start()
    heads = skip.shape[1]
    taps = wbc.shape[0]
    lane = slice(g * STATE, (g + 1) * STATE)
    shift = moves[0 : (taps - 1) * BLOCK, :]

    def conv(which):
        base = which * wbc.shape[2] + g * STATE
        block = bc[:, base : base + STATE]
        half = conv_half(shift, block, block, bc_weight(which, lane, wbc), bbc[which : which + 1, lane])
        return silu_of_half(half).astype(BF16)

    cmat = conv(1)
    c_out[...] = cmat
    scores = lax.dot_general(cmat, conv(0), (((1,), (1,)), ((), ())), preferred_element_type=F32)
    scores = jnp.where(tokens(0, scores.shape, 1) < taps - 1, 0.0, scores * mask[...]).astype(BF16)
    skips = pair_of(jnp.broadcast_to(skip[...], (8, heads)))
    step = 1024
    copy.wait()
    for at in range(0, wide, step):
        lane = slice(at, at + step)
        onehot2 = twice(head_map(heads, (g * wide + at) // HEAD_DIM, step))
        xf = xc_in[:, lane].astype(F32)
        xf = jnp.where(tokens(0, xf.shape, 0) < taps - 1, 0.0, xf)
        rates = mm(factors[:, 0 : 2 * heads], onehot2)
        rate_top[:, lane] = rates[0:TILE]
        scaled = (xf * rates).astype(BF16)
        grown = mm(factors[:, 2 * heads : 4 * heads], onehot2)
        skip_c = mm(skips, onehot2)[0:1]
        gate = silu_of_half(z[:, lane].astype(F32) * 0.5)
        kept_top[:, lane] = skip_c * gate[0:TILE]
        near[:, lane] = (mm(scores, scaled) * grown + skip_c * xf) * gate
        gain[:, lane] = grown * gate


def finish_kernel(g, taps, info, near, gain, cmat, rate_top, kept_top, mask, live, scale, *rest):
    out, ready, held, sems = rest[-4:]
    mine = info[2]
    rows, wide = near.shape
    width = wide // QUAD
    steps = sems.shape[0]
    part = rows // steps
    square = [0.0] * steps
    ats = [pl.ds(pl.multiple_of((mine ^ k) * width, width), width) for k in range(QUAD)]
    first = rest[0][STATE : STATE + EXTRA, 0 : 2 * STATE].astype(F32)[TILE:EXTRA]
    c = cmat[...].astype(F32)
    top = jnp.where(tokens(0, (TILE, STATE), 0) < taps - 1, first[:, STATE:], c[0:TILE])
    c = jnp.concatenate([top, c[TILE:]], axis=0)
    bmat = jnp.concatenate([first[:, 0:STATE], jnp.zeros((TILE, STATE), F32)], axis=0).astype(BF16)
    scores = lax.dot_general(c.astype(BF16), bmat, (((1,), (1,)), ((), ())), preferred_element_type=F32)
    left = jnp.concatenate([c * live[...], scores * mask[:, 0 : 2 * TILE]], axis=1).astype(BF16)
    for at, e in zip(ats, rest):
        xc = e[STATE : STATE + EXTRA, :].astype(F32)[0:TILE]
        sent = jnp.concatenate([xc * rate_top[:, at], jnp.zeros_like(xc)], axis=0).astype(BF16)
        far = mm(left, jnp.concatenate([e[0:STATE, :], sent], axis=0))
        for i in range(steps):
            these = slice(i * part, (i + 1) * part)
            value = near[these, at] + gain[these, at] * far[these]
            if i == 0:
                value = value + jnp.concatenate([xc * kept_top[:, at], jnp.zeros((part - TILE, width), F32)], axis=0)
            square[i] = square[i] + jnp.sum(value * value, axis=1, keepdims=True)
            held[these, at] = value
    copies = []
    for i in range(steps):
        these = slice(i * part, (i + 1) * part)
        inv = lax.rsqrt(square[i] * (1.0 / wide) + 1e-05)
        ready[these, :] = (held[these, :] * inv * scale[:, g * wide : (g + 1) * wide]).astype(BF16)
        copy = pltpu.make_async_copy(ready.at[these, :], out.at[these, g * wide : (g + 1) * wide], sems.at[i])
        copy.start()
        copies.append(copy)
    for copy in copies:
        copy.wait()


SMEM = pl.BlockSpec(memory_space=pltpu.SMEM)
VMEM = pl.BlockSpec(memory_space=pltpu.VMEM)
ANY = pl.BlockSpec(memory_space=pl.ANY)
HBM = pl.BlockSpec(memory_space=pltpu.HBM)


def call(kernel, scalars, args, outs, flops, limit=32 << 20, **more):
    pinned = more.get("specs", ())
    args = [
        pltpu.with_memory_space_constraint(arg, pltpu.HBM) if i < len(pinned) and pinned[i] is HBM else arg
        for i, arg in enumerate(args)
    ]
    return pl.pallas_call(
        kernel,
        in_specs=[SMEM] * len(scalars) + more.pop("specs", [VMEM] * len(args)),
        out_specs=more.pop("out_specs", [VMEM] * len(outs)),
        out_shape=[jax.ShapeDtypeStruct(*out) for out in outs],
        cost_estimate=pl.CostEstimate(flops=flops, bytes_accessed=4 << 20, transcendentals=0),
        compiler_params=pltpu.CompilerParams(vmem_limit_bytes=limit),
        **more,
    )(*scalars, *args)


def tie(first, second):
    return lax.optimization_barrier((first, second))


def shards(
    x_in,
    z_in,
    bc_in,
    conv_x_weight,
    conv_x_bias,
    conv_bc_weight,
    conv_bc_bias,
    dt_raw,
    dt_bias,
    decay,
    skip_d,
    norm_gain,
    lengths,
):
    rows, chan = x_in.shape
    heads = dt_raw.shape[1]
    peers = lax.axis_size("seq")
    shard = lax.axis_index("seq").astype(jnp.int32)
    taps = conv_x_weight.shape[0]
    bcw = bc_in.shape[2]
    groups = bcw // STATE
    wide = chan // groups
    width = wide // QUAD
    reach = peers // 2 // QUAD

    bx = conv_x_bias.reshape(1, chan)
    scale = norm_gain.reshape(1, chan)
    owner = (shard % QUAD) ^ (shard // QUAD % 2 * 2)
    info = jnp.stack([shard, shard % QUAD, owner])

    def swap(values):
        routes = [[(i, i ^ k) for i in range(peers)] for k in range(QUAD)]
        swapped = {k: lax.ppermute(values[k], "seq", routes[k]) for k in (3, 1, 2)}
        return [values[0], swapped[1], swapped[2], swapped[3]]

    def ahead(value):
        return lax.ppermute(value, "seq", [(i, (i + QUAD) % peers ^ 2) for i in range(peers)])

    first_args = [
        lengths, x_in, bc_in, conv_x_weight, bx, dt_raw.T, dt_bias.reshape(1, heads), decay.reshape(1, heads),
        conv_bc_weight, conv_bc_bias, skip_d.reshape(1, heads), scale,
    ]
    sent = ((STATE + EXTRA, width), BF16)
    held = pltpu.VMEM((STATE + EXTRA, wide), BF16)
    x, bc, moves, mask, live, factors, factor, carry, wx, bx, wbc, bbc, skip, scale, xc, *msg = call(
        first_kernel,
        [info],
        first_args,
        [
            ((rows, chan), BF16),
            ((rows, 2 * bcw), BF16),
            (((taps - 1) * (BLOCK + TILE), BLOCK), BF16),
            ((BLOCK, BLOCK), F32),
            ((BLOCK, BLOCK), F32),
            ((rows, 4 * heads), BF16),
            ((rows, 2 * heads), BF16),
            ((TILE, 2 * heads), BF16),
            ((taps, chan), BF16),
            ((1, chan), F32),
            ((taps, 2, bcw), BF16),
            ((2, bcw), F32),
            ((1, heads), F32),
            ((1, chan), F32),
            ((rows, wide), BF16),
            *[sent] * QUAD,
        ],
        600_000_000,
        specs=[HBM] * len(first_args),
        scratch_shapes=[
            pltpu.SMEM(lengths.shape, jnp.int32),
            pltpu.VMEM((rows, 2, bcw), BF16),
            pltpu.VMEM((heads, rows), BF16),
            pltpu.VMEM((1, heads), F32),
            pltpu.VMEM((1, heads), F32),
            held,
            pltpu.SemaphoreType.DMA((13,)),
        ],
    )
    xcs, msgs = [xc], [swap(msg)]
    for g in range(1, groups):
        xc, *msg = call(
            functools.partial(other_kernel, g),
            [info],
            [x, bc, wx, bx, wbc, bbc, moves, factor, carry],
            [((rows, wide), BF16), *[sent] * QUAD],
            300_000_000,
            scratch_shapes=[held],
        )
        xcs.append(xc)
        msgs.append(swap(msg))

    local = []
    for g in range(groups):
        args = [xcs[g], z_in, bc, wbc, bbc, moves, mask, factors, skip]
        outs = [((rows, wide), F32)] * 2 + [((rows, STATE), BF16)] + [((TILE, wide), F32)] * 2
        near = call(
            functools.partial(inner_kernel, g),
            [],
            args,
            outs,
            300_000_000,
            specs=[HBM if arg is z_in else VMEM for arg in args],
            scratch_shapes=[pltpu.VMEM((rows, wide), BF16), pltpu.SemaphoreType.DMA],
        )
        local.append(list(near))
    msgs[-1][0], local[0][0] = tie(msgs[-1][0], local[0][0])

    entering, fixes = [], []
    for g in range(groups):
        outs = [sent, ((QUAD - 1, STATE + EXTRA, width), BF16)]
        args = list(msgs[g])
        if reach > 1:
            outs.append(((8, width), F32))
            args.append(ahead(lax.dynamic_index_in_dim(jnp.stack(args), shard % QUAD ^ (QUAD - 1), 0, False)))
        total, fixed, *through = call(
            functools.partial(fold_kernel, taps, len(args) - QUAD), (info,), args, outs, 1_000_000
        )
        state = ahead(total)
        for _ in range(reach - 1):
            own = total[0:STATE].astype(F32) + through[0][0:1] * state[0:STATE].astype(F32)
            state = ahead(jnp.concatenate([own.astype(BF16), total[STATE:]], axis=0))
        entering.append(state)
        fixes.append(fixed)

    blocks = []
    for g in range(groups):
        outs = [sent] * QUAD
        kernel = functools.partial(enter_kernel, taps)
        blocks.append(swap(call(kernel, (info,), [entering[g], fixes[g], *msgs[g]], outs, 1_000_000)))

    blocks[0][1], local[-1][0] = tie(blocks[0][1], local[-1][0])

    out = None
    for g in range(groups):
        args = [*local[g], mask, live, scale, *blocks[g]]
        specs = [VMEM] * len(args)
        aliases = {}
        if out is not None:
            aliases = {1 + len(args): 0}
            args.append(out)
            specs.append(ANY)
        (out,) = call(
            functools.partial(finish_kernel, g, taps),
            (info,),
            args,
            [((rows, chan), BF16)],
            100_000_000,
            specs=specs,
            out_specs=[ANY],
            scratch_shapes=[
                pltpu.VMEM((rows, wide), BF16),
                pltpu.VMEM((rows, wide), F32),
                pltpu.SemaphoreType.DMA((4,)),
            ],
            input_output_aliases=aliases,
        )
    return out


def solution(mesh):
    return jax.shard_map(
        shards,
        mesh=mesh,
        in_specs=(
            P(("groups", "seq"), "heads"),
            P(("groups", "seq"), "heads"),
            P(("groups", "seq"), None, "heads"),
            P(None, "heads"),
            P("heads"),
            P(None, None, "heads"),
            P(None, "heads"),
            P(("groups", "seq"), "heads"),
            P("heads"),
            P("heads"),
            P("heads"),
            P("heads"),
            P("groups"),
        ),
        out_specs=P(("groups", "seq"), "heads"),
        check_vma=False,
    )
```

```python
import functools

import jax
import jax.numpy as jnp
from jax import lax
from jax.experimental import pallas as pl
from jax.experimental.pallas import tpu as pltpu
from jax.sharding import PartitionSpec as P

HEAD_DIM = 64
STATE = 128
BLOCK = 128
QUAD = 4
TILE = 8
EXTRA = 16
F32 = jnp.float32
BF16 = jnp.bfloat16


def mm(left, right):
    return jnp.dot(left, right, preferred_element_type=F32)


def ends_of(lens_ref):
    total = 0
    ends = []
    for i in range(lens_ref.shape[0]):
        total = total + lens_ref[i]
        ends.append(total)
    return ends


def seg_of(pos, ends):
    count = 0
    for end in ends:
        count = count + jnp.where(end <= pos, 1, 0)
    return jnp.where(pos >= 0, count, -1)


def tokens(start, shape, dim):
    return start + lax.broadcasted_iota(jnp.int32, shape, dim)


def shift_matrix(start, ends, rows, before, taps):
    shape = (rows, before + rows)
    row = lax.broadcasted_iota(jnp.int32, shape, 0)
    col = lax.broadcasted_iota(jnp.int32, shape, 1)
    same = seg_of(start + row, ends) == seg_of(start - before + col, ends)
    parts = []
    for k in range(taps - 1):
        parts.append(jnp.where((col == row + (before - taps + 1 + k)) & same, 1.0, 0.0))
    return jnp.concatenate(parts, axis=0).astype(BF16)


def conv_half(shift, extended, block, weight, bias):
    rows = block.shape[0]
    taps = weight.shape[0]
    half = weight.astype(F32) * 0.5
    moved = mm(shift, extended)
    total = bias * 0.5 + block.astype(F32) * half[taps - 1 : taps]
    for k in range(taps - 1):
        total = total + moved[k * rows : (k + 1) * rows] * half[k : k + 1]
    return total


def silu_of_half(half):
    return half + half * jnp.tanh(half)


def rates_of(dt_ref, dtb_ref, dec_ref):
    raw = jnp.transpose(dt_ref[...].astype(F32)) + dtb_ref[...]
    rate = jnp.maximum(raw, 0.0) + jnp.log1p(jnp.exp(-jnp.abs(raw)))
    shape = (BLOCK, BLOCK)
    lower = lax.broadcasted_iota(jnp.int32, shape, 0) >= lax.broadcasted_iota(jnp.int32, shape, 1)
    cum = jnp.dot(
        jnp.where(lower, 1.0, 0.0),
        -rate * dec_ref[...],
        precision=lax.Precision.HIGHEST,
        preferred_element_type=F32,
    )
    return rate, cum


def head_map(heads, first, width):
    shape = (heads, width)
    row = lax.broadcasted_iota(jnp.int32, shape, 0)
    col = lax.broadcasted_iota(jnp.int32, shape, 1)
    return jnp.where(row == first + col // HEAD_DIM, 1.0, 0.0).astype(BF16)


def pair_of(value):
    high = value.astype(BF16)
    low = (value - high.astype(F32)).astype(BF16)
    return jnp.concatenate([high, low], axis=1)


def twice(onehot):
    return jnp.concatenate([onehot, onehot], axis=0)


def next_matrix(start, ends, taps):
    shape = (TILE, BLOCK)
    row = lax.broadcasted_iota(jnp.int32, shape, 0)
    col = lax.broadcasted_iota(jnp.int32, shape, 1)
    same = seg_of(start + BLOCK + row, ends) == seg_of(start + col, ends)
    parts = []
    for k in range(taps - 1):
        parts.append(jnp.where((col == row + (BLOCK - taps + 1 + k)) & same, 1.0, 0.0))
    return jnp.concatenate(parts, axis=0).astype(BF16)


def conv_both(moves, block, weight, bias):
    taps = weight.shape[0]
    half = weight.astype(F32) * 0.5
    moved = mm(moves, block)
    total = bias * 0.5 + block.astype(F32) * half[taps - 1 : taps]
    after = 0.0
    base = (taps - 1) * BLOCK
    for k in range(taps - 1):
        total = total + moved[k * BLOCK : (k + 1) * BLOCK] * half[k : k + 1]
        after = after + moved[base + k * TILE : base + (k + 1) * TILE] * half[k : k + 1]
    return total, after


def bc_weight(which, lane, wbc):
    return jnp.concatenate([wbc[k].astype(F32)[which : which + 1, lane] for k in range(wbc.shape[0])], axis=0)


def send_states(g, mine, x, bc, wx, bx, wbc, bbc, moves, factor, carry, xc_out, msgs, held):
    taps = wx.shape[0]
    chan = x.shape[1]
    wide = xc_out.shape[1]
    heads = carry.shape[1] // 2
    width = wide // QUAD
    lane = slice(g * STATE, (g + 1) * STATE)
    inner = wbc.shape[2]
    btotal, bafter = conv_both(moves[...], bc[:, lane], bc_weight(0, lane, wbc), bbc[0:1, lane])
    cblock = bc[:, inner + g * STATE : inner + (g + 1) * STATE]
    ctotal, cafter = conv_both(moves[...], cblock, bc_weight(1, lane, wbc), bbc[1:2, lane])
    bmat = silu_of_half(btotal)
    bmat = jnp.where(tokens(0, bmat.shape, 0) >= taps - 1, bmat, 0.0)
    bmat_t = jnp.transpose(bmat).astype(BF16)
    bparts = jnp.concatenate([btotal[0:TILE], bafter, ctotal[0:TILE], cafter], axis=1)
    bparts = pltpu.roll(bparts, taps - 1, 0)
    step = 1024
    for at in range(0, wide, step):
        here = slice(at, at + step)
        deep = slice(g * wide + at, g * wide + at + step)
        onehot2 = twice(head_map(heads, (g * wide + at) // HEAD_DIM, step))
        total, after = conv_both(moves[...], x[:, deep], wx[:, deep], bx[:, deep])
        xc = silu_of_half(total).astype(BF16)
        xc_out[:, here] = xc
        spread = mm(factor[...], onehot2)
        held[0:STATE, here] = mm(bmat_t, (xc.astype(F32) * spread).astype(BF16)).astype(BF16)
        row = lax.broadcasted_iota(jnp.int32, (TILE, step), 0)
        passed = mm(carry[...], onehot2[0 : 2 * heads])
        high = passed.astype(BF16).astype(F32)
        upper = jnp.where(row < 2 + taps - 1, pltpu.roll(total[0:TILE], 2, 0), pltpu.roll(after, 1 + taps, 0))
        upper = jnp.where(row == 0, high, jnp.where(row == 1, passed - high, upper))
        lower = jnp.where(row < taps - 1, spread[0:TILE], jnp.concatenate([bparts] * (step // width), axis=1))
        held[STATE : STATE + EXTRA, here] = jnp.concatenate([upper, lower], axis=0).astype(BF16)
    for k, msg in enumerate(msgs):
        msg[...] = held[:, pl.ds(pl.multiple_of((mine ^ k) * width, width), width)]


def first_kernel(
    info, lens_in, x_in, bc_in, wx_in, bx_in, dt_in, dtb_in, dec_in, wbc_in, bbc_in, skip_in, scale_in,
    x, bc, moves, mask, live, factors, factor, carry, wx, bx, wbc, bbc, skip, scale, xc_out, m0, m1, m2, m3,
    lens, raw, dt, dtb, dec, held, sems,
):
    heads = dt.shape[0]
    wide = xc_out.shape[1]
    inner = bc.shape[1] // 2
    pairs = [
        (lens_in, lens), (dt_in, dt), (dtb_in, dtb), (dec_in, dec), (bc_in, raw), (wx_in, wx), (bx_in, bx),
        (wbc_in, wbc), (bbc_in, bbc), (x_in.at[:, 0:wide], x.at[:, 0:wide]), (x_in.at[:, wide:], x.at[:, wide:]),
        (skip_in, skip), (scale_in, scale),
    ]
    copies = [pltpu.make_async_copy(src, dst, sems.at[i]) for i, (src, dst) in enumerate(pairs)]
    for copy in copies:
        copy.start()
    for copy in copies[0:4]:
        copy.wait()
    start = info[0] * BLOCK
    taps = wx.shape[0]
    ends = ends_of(lens)
    moves[0 : (taps - 1) * BLOCK, :] = shift_matrix(start, ends, BLOCK, 0, taps)
    moves[(taps - 1) * BLOCK :, :] = next_matrix(start, ends, taps)
    shape = (BLOCK, BLOCK)
    row = lax.broadcasted_iota(jnp.int32, shape, 0)
    col = lax.broadcasted_iota(jnp.int32, shape, 1)
    seg_row = seg_of(start + row, ends)
    mask[...] = jnp.where((row >= col) & (seg_row == seg_of(start + col, ends)), 1.0, 0.0)
    rate, cum = rates_of(dt, dtb, dec)
    last = cum[BLOCK - 1 : BLOCK]
    seg_last = seg_of(start + BLOCK - 1, ends)
    seg_head = seg_row[:, 0:heads]
    factor[...] = pair_of(jnp.where(seg_head == seg_last, jnp.exp(last - cum), 0.0) * rate)
    grown = jnp.exp(cum)
    before = seg_of(start - 1, ends)
    factors[:, 0 : 2 * heads] = pair_of(rate * jnp.exp(-cum))
    factors[:, 2 * heads : 4 * heads] = pair_of(grown)
    live[...] = jnp.where(seg_row == before, 1.0, 0.0)
    passed = jnp.where(seg_last == before, jnp.exp(last), 0.0)
    carry[...] = pair_of(jnp.broadcast_to(passed, (TILE, heads)))
    for copy in copies[4:9]:
        copy.wait()
    value = raw[...].astype(F32)
    for i in range(2):
        bc[:, i * inner : (i + 1) * inner] = value[:, i, :].astype(BF16)
    copies[9].wait()
    send_states(0, info[2], x, bc, wx, bx, wbc, bbc, moves, factor, carry, xc_out, (m0, m1, m2, m3), held)
    for copy in copies[10:]:
        copy.wait()


def other_kernel(g, info, x, bc, wx, bx, wbc, bbc, moves, factor, carry, xc_out, m0, m1, m2, m3, held):
    send_states(g, info[2], x, bc, wx, bx, wbc, bbc, moves, factor, carry, xc_out, (m0, m1, m2, m3), held)


def extra_of(msg):
    value = msg[STATE : STATE + EXTRA, :].astype(F32)
    return value[0:TILE], value[TILE:EXTRA]


def top_state(taps, here, prior):
    upper, lower = here
    total = pltpu.roll(upper, TILE - 2, 0)
    parts = pltpu.roll(lower, TILE - taps + 1, 0)
    btotal, ctotal = parts[:, 0:STATE], parts[:, 2 * STATE : 3 * STATE]
    if prior is not None:
        total = total + pltpu.roll(prior[0], TILE - 1 - taps, 0)
        parts = pltpu.roll(prior[1], TILE - taps + 1, 0)
        btotal, ctotal = btotal + parts[:, STATE : 2 * STATE], ctotal + parts[:, 3 * STATE : 4 * STATE]
    xc = silu_of_half(total).astype(BF16).astype(F32)
    xc = jnp.where(tokens(0, xc.shape, 0) < taps - 1, xc, 0.0)
    both = silu_of_half(jnp.concatenate([btotal, ctotal], axis=1))
    both = jnp.where(tokens(0, both.shape, 0) < taps - 1, both, 0.0)
    rows = pltpu.roll(jnp.concatenate([both, jnp.zeros_like(both)], axis=1), taps - 1, 0)
    rows = jnp.where(tokens(0, rows.shape, 0) < taps - 1, xc, rows).astype(BF16)
    scaled, bmat = xc * lower, both[:, 0:STATE]
    scaled = jnp.concatenate([scaled, jnp.zeros_like(scaled)], axis=0).astype(BF16)
    bmat = jnp.concatenate([bmat, jnp.zeros_like(bmat)], axis=0).astype(BF16)
    return lax.dot_general(bmat, scaled, (((0,), (0,)), ((), ())), preferred_element_type=F32), rows


def carry_row(extra):
    return extra[0][0:1] + extra[0][1:2]


def fold_kernel(taps, more, info, *refs):
    msgs, rest = refs[0:QUAD], refs[QUAD:]
    total, fixed = rest[more], rest[more + 1]
    for mine in range(QUAD):

        @pl.when(info[1] == mine)
        def _():
            block = [msgs[mine ^ b] for b in range(QUAD)]
            extra = [extra_of(msg) for msg in block]
            add, _ = top_state(taps, extra[0], extra_of(rest[0]) if more else None)
            state = block[0][0:STATE, :].astype(F32) + add
            through = carry_row(extra[0])
            for b in range(1, QUAD):
                add, rows = top_state(taps, extra[b], extra[b - 1])
                own = block[b][0:STATE, :].astype(F32) + add
                fixed[b - 1, 0:STATE, :] = own.astype(BF16)
                fixed[b - 1, STATE : STATE + TILE, :] = rows
                state = own + carry_row(extra[b]) * state
                through = through * carry_row(extra[b])
            total[0:STATE, :] = state.astype(BF16)
            total[STATE : STATE + EXTRA, :] = block[QUAD - 1][STATE : STATE + EXTRA, :]
            for out in rest[more + 2 :]:
                out[...] = jnp.broadcast_to(through, out.shape)


def enter_kernel(taps, info, start, fixed, m0, m1, m2, m3, o0, o1, o2, o3):
    msgs = (m0, m1, m2, m3)
    outs = (o0, o1, o2, o3)
    lower = slice(STATE, STATE + TILE)
    prior = extra_of(start)
    for mine in range(QUAD):

        @pl.when(info[1] == mine)
        def _():
            head = extra_of(msgs[mine])
            add, rows = top_state(taps, head, prior)
            outs[mine][0:STATE, :] = start[0:STATE, :]
            outs[mine][lower, :] = rows
            state = msgs[mine][0:STATE, :].astype(F32) + add
            state = state + carry_row(head) * start[0:STATE, :].astype(F32)
            for b in range(1, QUAD):
                outs[mine ^ b][0:STATE, :] = state.astype(BF16)
                outs[mine ^ b][lower, :] = fixed[b - 1, lower, :]
                if b < QUAD - 1:
                    own = fixed[b - 1, 0:STATE, :].astype(F32)
                    state = own + carry_row(extra_of(msgs[mine ^ b])) * state


def inner_kernel(g, xc_in, z_in, bc, wbc, bbc, moves, mask, factors, skip, near, gain, c_out, rate_top, kept_top, z, sem):
    wide = xc_in.shape[1]
    copy = pltpu.make_async_copy(z_in.at[:, g * wide : (g + 1) * wide], z, sem)
    copy.start()
    heads = skip.shape[1]
    taps = wbc.shape[0]
    lane = slice(g * STATE, (g + 1) * STATE)
    shift = moves[0 : (taps - 1) * BLOCK, :]

    def conv(which):
        base = which * wbc.shape[2] + g * STATE
        block = bc[:, base : base + STATE]
        half = conv_half(shift, block, block, bc_weight(which, lane, wbc), bbc[which : which + 1, lane])
        return silu_of_half(half).astype(BF16)

    cmat = conv(1)
    c_out[...] = cmat
    scores = lax.dot_general(cmat, conv(0), (((1,), (1,)), ((), ())), preferred_element_type=F32)
    scores = jnp.where(tokens(0, scores.shape, 1) < taps - 1, 0.0, scores * mask[...]).astype(BF16)
    skips = pair_of(jnp.broadcast_to(skip[...], (8, heads)))
    step = 1024
    copy.wait()
    for at in range(0, wide, step):
        lane = slice(at, at + step)
        onehot2 = twice(head_map(heads, (g * wide + at) // HEAD_DIM, step))
        xf = xc_in[:, lane].astype(F32)
        xf = jnp.where(tokens(0, xf.shape, 0) < taps - 1, 0.0, xf)
        rates = mm(factors[:, 0 : 2 * heads], onehot2)
        rate_top[:, lane] = rates[0:TILE]
        scaled = (xf * rates).astype(BF16)
        grown = mm(factors[:, 2 * heads : 4 * heads], onehot2)
        skip_c = mm(skips, onehot2)[0:1]
        gate = silu_of_half(z[:, lane].astype(F32) * 0.5)
        kept_top[:, lane] = skip_c * gate[0:TILE]
        near[:, lane] = (mm(scores, scaled) * grown + skip_c * xf) * gate
        gain[:, lane] = grown * gate


def finish_kernel(g, taps, info, near, gain, cmat, rate_top, kept_top, mask, live, scale, *rest):
    out, ready, held, sems = rest[-4:]
    mine = info[2]
    rows, wide = near.shape
    width = wide // QUAD
    steps = sems.shape[0]
    part = rows // steps
    square = [0.0] * steps
    ats = [pl.ds(pl.multiple_of((mine ^ k) * width, width), width) for k in range(QUAD)]
    first = pltpu.roll(rest[0][STATE : STATE + TILE, 0 : 2 * STATE].astype(F32), TILE - taps + 1, 0)
    first = jnp.where(tokens(0, first.shape, 0) < taps - 1, first, 0.0)
    c = cmat[...].astype(F32)
    top = jnp.where(tokens(0, (TILE, STATE), 0) < taps - 1, first[:, STATE:], c[0:TILE])
    c = jnp.concatenate([top, c[TILE:]], axis=0)
    bmat = jnp.concatenate([first[:, 0:STATE], jnp.zeros((TILE, STATE), F32)], axis=0).astype(BF16)
    scores = lax.dot_general(c.astype(BF16), bmat, (((1,), (1,)), ((), ())), preferred_element_type=F32)
    left = jnp.concatenate([c * live[...], scores * mask[:, 0 : 2 * TILE]], axis=1).astype(BF16)
    for at, e in zip(ats, rest):
        xc = e[STATE : STATE + TILE, :].astype(F32)
        xc = jnp.where(tokens(0, xc.shape, 0) < taps - 1, xc, 0.0)
        sent = jnp.concatenate([xc * rate_top[:, at], jnp.zeros_like(xc)], axis=0).astype(BF16)
        far = mm(left, jnp.concatenate([e[0:STATE, :], sent], axis=0))
        for i in range(steps):
            these = slice(i * part, (i + 1) * part)
            value = near[these, at] + gain[these, at] * far[these]
            if i == 0:
                value = value + jnp.concatenate([xc * kept_top[:, at], jnp.zeros((part - TILE, width), F32)], axis=0)
            square[i] = square[i] + jnp.sum(value * value, axis=1, keepdims=True)
            held[these, at] = value
    copies = []
    for i in range(steps):
        these = slice(i * part, (i + 1) * part)
        inv = lax.rsqrt(square[i] * (1.0 / wide) + 1e-05)
        ready[these, :] = (held[these, :] * inv * scale[:, g * wide : (g + 1) * wide]).astype(BF16)
        copy = pltpu.make_async_copy(ready.at[these, :], out.at[these, g * wide : (g + 1) * wide], sems.at[i])
        copy.start()
        copies.append(copy)
    for copy in copies:
        copy.wait()


SMEM = pl.BlockSpec(memory_space=pltpu.SMEM)
VMEM = pl.BlockSpec(memory_space=pltpu.VMEM)
ANY = pl.BlockSpec(memory_space=pl.ANY)
HBM = pl.BlockSpec(memory_space=pltpu.HBM)


def call(kernel, scalars, args, outs, flops, limit=32 << 20, **more):
    pinned = more.get("specs", ())
    args = [
        pltpu.with_memory_space_constraint(arg, pltpu.HBM) if i < len(pinned) and pinned[i] is HBM else arg
        for i, arg in enumerate(args)
    ]
    return pl.pallas_call(
        kernel,
        in_specs=[SMEM] * len(scalars) + more.pop("specs", [VMEM] * len(args)),
        out_specs=more.pop("out_specs", [VMEM] * len(outs)),
        out_shape=[jax.ShapeDtypeStruct(*out) for out in outs],
        cost_estimate=pl.CostEstimate(flops=flops, bytes_accessed=4 << 20, transcendentals=0),
        compiler_params=pltpu.CompilerParams(vmem_limit_bytes=limit),
        **more,
    )(*scalars, *args)


def tie(first, second):
    return lax.optimization_barrier((first, second))


def shards(
    x_in,
    z_in,
    bc_in,
    conv_x_weight,
    conv_x_bias,
    conv_bc_weight,
    conv_bc_bias,
    dt_raw,
    dt_bias,
    decay,
    skip_d,
    norm_gain,
    lengths,
):
    rows, chan = x_in.shape
    heads = dt_raw.shape[1]
    peers = lax.axis_size("seq")
    shard = lax.axis_index("seq").astype(jnp.int32)
    taps = conv_x_weight.shape[0]
    bcw = bc_in.shape[2]
    groups = bcw // STATE
    wide = chan // groups
    width = wide // QUAD
    reach = peers // 2 // QUAD

    bx = conv_x_bias.reshape(1, chan)
    scale = norm_gain.reshape(1, chan)
    owner = (shard % QUAD) ^ (shard // QUAD % 2 * 2)
    info = jnp.stack([shard, shard % QUAD, owner])

    def swap(values):
        routes = [[(i, i ^ k) for i in range(peers)] for k in range(QUAD)]
        swapped = {k: lax.ppermute(values[k], "seq", routes[k]) for k in (3, 1, 2)}
        return [values[0], swapped[1], swapped[2], swapped[3]]

    def ahead(value):
        return lax.ppermute(value, "seq", [(i, i + QUAD ^ 2) for i in range(peers - QUAD)])

    first_args = [
        lengths, x_in, bc_in, conv_x_weight, bx, dt_raw.T, dt_bias.reshape(1, heads), decay.reshape(1, heads),
        conv_bc_weight, conv_bc_bias, skip_d.reshape(1, heads), scale,
    ]
    sent = ((STATE + EXTRA, width), BF16)
    held = pltpu.VMEM((STATE + EXTRA, wide), BF16)
    x, bc, moves, mask, live, factors, factor, carry, wx, bx, wbc, bbc, skip, scale, xc, *msg = call(
        first_kernel,
        [info],
        first_args,
        [
            ((rows, chan), BF16),
            ((rows, 2 * bcw), BF16),
            (((taps - 1) * (BLOCK + TILE), BLOCK), BF16),
            ((BLOCK, BLOCK), F32),
            ((BLOCK, BLOCK), F32),
            ((rows, 4 * heads), BF16),
            ((rows, 2 * heads), BF16),
            ((TILE, 2 * heads), BF16),
            ((taps, chan), BF16),
            ((1, chan), F32),
            ((taps, 2, bcw), BF16),
            ((2, bcw), F32),
            ((1, heads), F32),
            ((1, chan), F32),
            ((rows, wide), BF16),
            *[sent] * QUAD,
        ],
        600_000_000,
        specs=[HBM] * len(first_args),
        scratch_shapes=[
            pltpu.SMEM(lengths.shape, jnp.int32),
            pltpu.VMEM((rows, 2, bcw), BF16),
            pltpu.VMEM((heads, rows), BF16),
            pltpu.VMEM((1, heads), F32),
            pltpu.VMEM((1, heads), F32),
            held,
            pltpu.SemaphoreType.DMA((13,)),
        ],
    )
    xcs, msgs = [xc], [swap(msg)]
    for g in range(1, groups):
        xc, *msg = call(
            functools.partial(other_kernel, g),
            [info],
            [x, bc, wx, bx, wbc, bbc, moves, factor, carry],
            [((rows, wide), BF16), *[sent] * QUAD],
            300_000_000,
            scratch_shapes=[held],
        )
        xcs.append(xc)
        msgs.append(swap(msg))

    local = []
    for g in range(groups):
        args = [xcs[g], z_in, bc, wbc, bbc, moves, mask, factors, skip]
        outs = [((rows, wide), F32)] * 2 + [((rows, STATE), BF16)] + [((TILE, wide), F32)] * 2
        near = call(
            functools.partial(inner_kernel, g),
            [],
            args,
            outs,
            300_000_000,
            specs=[HBM if arg is z_in else VMEM for arg in args],
            scratch_shapes=[pltpu.VMEM((rows, wide), BF16), pltpu.SemaphoreType.DMA],
        )
        local.append(list(near))
    msgs[-1][0], local[0][0] = tie(msgs[-1][0], local[0][0])

    entering, fixes = [], []
    for g in range(groups):
        outs = [sent, ((QUAD - 1, STATE + TILE, width), BF16)]
        args = list(msgs[g])
        if reach > 1:
            outs.append(((8, width), F32))
            args.append(ahead(lax.dynamic_index_in_dim(jnp.stack(args), shard % QUAD ^ (QUAD - 1), 0, False)))
        total, fixed, *through = call(
            functools.partial(fold_kernel, taps, len(args) - QUAD), (info,), args, outs, 1_000_000
        )
        state = ahead(total)
        for _ in range(reach - 1):
            own = total[0:STATE].astype(F32) + through[0][0:1] * state[0:STATE].astype(F32)
            state = ahead(jnp.concatenate([own.astype(BF16), total[STATE:]], axis=0))
        entering.append(state)
        fixes.append(fixed)

    blocks = []
    for g in range(groups):
        outs = [((STATE + TILE, width), BF16)] * QUAD
        kernel = functools.partial(enter_kernel, taps)
        blocks.append(swap(call(kernel, (info,), [entering[g], fixes[g], *msgs[g]], outs, 1_000_000)))

    blocks[0][1], local[-1][0] = tie(blocks[0][1], local[-1][0])

    out = None
    for g in range(groups):
        args = [*local[g], mask, live, scale, *blocks[g]]
        specs = [VMEM] * len(args)
        aliases = {}
        if out is not None:
            aliases = {1 + len(args): 0}
            args.append(out)
            specs.append(ANY)
        (out,) = call(
            functools.partial(finish_kernel, g, taps),
            (info,),
            args,
            [((rows, chan), BF16)],
            100_000_000,
            specs=specs,
            out_specs=[ANY],
            scratch_shapes=[
                pltpu.VMEM((rows, wide), BF16),
                pltpu.VMEM((rows, wide), F32),
                pltpu.SemaphoreType.DMA((2,)),
            ],
            input_output_aliases=aliases,
        )
    return out


def solution(mesh):
    return jax.shard_map(
        shards,
        mesh=mesh,
        in_specs=(
            P(("groups", "seq"), "heads"),
            P(("groups", "seq"), "heads"),
            P(("groups", "seq"), None, "heads"),
            P(None, "heads"),
            P("heads"),
            P(None, None, "heads"),
            P(None, "heads"),
            P(("groups", "seq"), "heads"),
            P("heads"),
            P("heads"),
            P("heads"),
            P("heads"),
            P("groups"),
        ),
        out_specs=P(("groups", "seq"), "heads"),
        check_vma=False,
    )
```

```python
import functools

import jax
import jax.numpy as jnp
from jax import lax
from jax.experimental import pallas as pl
from jax.experimental.pallas import tpu as pltpu
from jax.sharding import PartitionSpec as P

HEAD_DIM = 64
STATE = 128
BLOCK = 128
QUAD = 4
TILE = 8
EXTRA = 16
F32 = jnp.float32
BF16 = jnp.bfloat16


def mm(left, right):
    return jnp.dot(left, right, preferred_element_type=F32)


def ends_of(lens_ref):
    total = 0
    ends = []
    for i in range(lens_ref.shape[0]):
        total = total + lens_ref[i]
        ends.append(total)
    return ends


def seg_of(pos, ends):
    count = 0
    for end in ends:
        count = count + jnp.where(end <= pos, 1, 0)
    return jnp.where(pos >= 0, count, -1)


def tokens(start, shape, dim):
    return start + lax.broadcasted_iota(jnp.int32, shape, dim)


def shift_matrix(start, ends, rows, before, taps):
    shape = (rows, before + rows)
    row = lax.broadcasted_iota(jnp.int32, shape, 0)
    col = lax.broadcasted_iota(jnp.int32, shape, 1)
    same = seg_of(start + row, ends) == seg_of(start - before + col, ends)
    parts = []
    for k in range(taps - 1):
        parts.append(jnp.where((col == row + (before - taps + 1 + k)) & same, 1.0, 0.0))
    return jnp.concatenate(parts, axis=0).astype(BF16)


def conv_half(shift, extended, block, weight, bias):
    rows = block.shape[0]
    taps = weight.shape[0]
    half = weight.astype(F32) * 0.5
    moved = mm(shift, extended)
    total = bias * 0.5 + block.astype(F32) * half[taps - 1 : taps]
    for k in range(taps - 1):
        total = total + moved[k * rows : (k + 1) * rows] * half[k : k + 1]
    return total


def silu_of_half(half):
    return half + half * jnp.tanh(half)


def rates_of(dt_ref, dtb_ref, dec_ref):
    raw = jnp.transpose(dt_ref[...].astype(F32)) + dtb_ref[...]
    rate = jnp.maximum(raw, 0.0) + jnp.log1p(jnp.exp(-jnp.abs(raw)))
    shape = (BLOCK, BLOCK)
    lower = lax.broadcasted_iota(jnp.int32, shape, 0) >= lax.broadcasted_iota(jnp.int32, shape, 1)
    cum = jnp.dot(
        jnp.where(lower, 1.0, 0.0),
        -rate * dec_ref[...],
        precision=lax.Precision.HIGHEST,
        preferred_element_type=F32,
    )
    return rate, cum


def head_map(heads, first, width):
    shape = (heads, width)
    row = lax.broadcasted_iota(jnp.int32, shape, 0)
    col = lax.broadcasted_iota(jnp.int32, shape, 1)
    return jnp.where(row == first + col // HEAD_DIM, 1.0, 0.0).astype(BF16)


def pair_of(value):
    high = value.astype(BF16)
    low = (value - high.astype(F32)).astype(BF16)
    return jnp.concatenate([high, low], axis=1)


def twice(onehot):
    return jnp.concatenate([onehot, onehot], axis=0)


def next_matrix(start, ends, taps):
    shape = (2 * TILE, BLOCK)
    row = lax.broadcasted_iota(jnp.int32, shape, 0)
    col = lax.broadcasted_iota(jnp.int32, shape, 1)
    same = seg_of(start + BLOCK + row, ends) == seg_of(start + col, ends)
    parts = []
    for k in range(taps - 1):
        parts.append(jnp.where((col == row + (BLOCK - taps + 1 + k)) & same, 1.0, 0.0))
    return jnp.concatenate(parts, axis=0).astype(BF16)


def conv_both(moves, block, weight, bias):
    taps = weight.shape[0]
    half = weight.astype(F32) * 0.5
    moved = mm(moves, block)
    total = bias * 0.5 + block.astype(F32) * half[taps - 1 : taps]
    after = 0.0
    base = (taps - 1) * BLOCK
    for k in range(taps - 1):
        total = total + moved[k * BLOCK : (k + 1) * BLOCK] * half[k : k + 1]
        after = after + moved[base + 2 * k * TILE : base + (2 * k + 1) * TILE] * half[k : k + 1]
    return total, after


def bc_weight(which, lane, wbc):
    return jnp.concatenate([wbc[k].astype(F32)[which : which + 1, lane] for k in range(wbc.shape[0])], axis=0)


def send_states(g, mine, x, bc, wx, bx, wbc, bbc, moves, factor, carry, xc_out, msgs, held):
    taps = wx.shape[0]
    chan = x.shape[1]
    wide = xc_out.shape[1]
    heads = carry.shape[1] // 2
    width = wide // QUAD
    lane = slice(g * STATE, (g + 1) * STATE)
    inner = wbc.shape[2]
    btotal, bafter = conv_both(moves[...], bc[:, lane], bc_weight(0, lane, wbc), bbc[0:1, lane])
    cblock = bc[:, inner + g * STATE : inner + (g + 1) * STATE]
    ctotal, cafter = conv_both(moves[...], cblock, bc_weight(1, lane, wbc), bbc[1:2, lane])
    bmat = silu_of_half(btotal)
    bmat = jnp.where(tokens(0, bmat.shape, 0) >= taps - 1, bmat, 0.0)
    bmat_t = jnp.transpose(bmat).astype(BF16)
    bparts = jnp.concatenate([btotal[0:TILE], bafter, ctotal[0:TILE], cafter], axis=1)
    bparts = pltpu.roll(bparts, taps - 1, 0)
    step = 1024
    for at in range(0, wide, step):
        here = slice(at, at + step)
        deep = slice(g * wide + at, g * wide + at + step)
        onehot2 = twice(head_map(heads, (g * wide + at) // HEAD_DIM, step))
        total, after = conv_both(moves[...], x[:, deep], wx[:, deep], bx[:, deep])
        xc = silu_of_half(total).astype(BF16)
        xc_out[:, here] = xc
        spread = mm(factor[...], onehot2)
        held[0:STATE, here] = mm(bmat_t, (xc.astype(F32) * spread).astype(BF16)).astype(BF16)
        row = lax.broadcasted_iota(jnp.int32, (TILE, step), 0)
        passed = mm(carry[...], onehot2[0 : 2 * heads])[0:TILE]
        high = passed.astype(BF16).astype(F32)
        upper = jnp.where(row < 2 + taps - 1, pltpu.roll(total[0:TILE], 2, 0), pltpu.roll(after, 1 + taps, 0))
        upper = jnp.where(row == 0, high, jnp.where(row == 1, passed - high, upper))
        lower = jnp.where(row < taps - 1, spread[0:TILE], jnp.concatenate([bparts] * (step // width), axis=1))
        held[STATE : STATE + EXTRA, here] = jnp.concatenate([upper, lower], axis=0).astype(BF16)
    for k, msg in enumerate(msgs):
        msg[...] = held[:, pl.ds(pl.multiple_of((mine ^ k) * width, width), width)]


def first_kernel(
    info, lens_in, x_in, bc_in, wx_in, bx_in, dt_in, dtb_in, dec_in, wbc_in, bbc_in, skip_in, scale_in,
    x, bc, moves, mask, live, factors, factor, carry, wx, bx, wbc, bbc, skip, scale, xc_out, m0, m1, m2, m3,
    lens, raw, dt, dtb, dec, held, sems,
):
    heads = dt.shape[0]
    wide = xc_out.shape[1]
    inner = bc.shape[1] // 2
    pairs = [
        (lens_in, lens), (dt_in, dt), (dtb_in, dtb), (dec_in, dec), (bc_in, raw), (wx_in, wx), (bx_in, bx),
        (wbc_in, wbc), (bbc_in, bbc), (x_in.at[:, 0:wide], x.at[:, 0:wide]), (x_in.at[:, wide:], x.at[:, wide:]),
        (skip_in, skip), (scale_in, scale),
    ]
    copies = [pltpu.make_async_copy(src, dst, sems.at[i]) for i, (src, dst) in enumerate(pairs)]
    for copy in copies:
        copy.start()
    for copy in copies[0:4]:
        copy.wait()
    start = info[0] * BLOCK
    taps = wx.shape[0]
    ends = ends_of(lens)
    moves[0 : (taps - 1) * BLOCK, :] = shift_matrix(start, ends, BLOCK, 0, taps)
    moves[(taps - 1) * BLOCK :, :] = next_matrix(start, ends, taps)
    shape = (BLOCK, BLOCK)
    row = lax.broadcasted_iota(jnp.int32, shape, 0)
    col = lax.broadcasted_iota(jnp.int32, shape, 1)
    seg_row = seg_of(start + row, ends)
    mask[...] = jnp.where((row >= col) & (seg_row == seg_of(start + col, ends)), 1.0, 0.0)
    rate, cum = rates_of(dt, dtb, dec)
    last = cum[BLOCK - 1 : BLOCK]
    seg_last = seg_of(start + BLOCK - 1, ends)
    seg_head = seg_row[:, 0:heads]
    factor[...] = pair_of(jnp.where(seg_head == seg_last, jnp.exp(last - cum), 0.0) * rate)
    grown = jnp.exp(cum)
    before = seg_of(start - 1, ends)
    factors[:, 0 : 2 * heads] = pair_of(rate * jnp.exp(-cum))
    factors[:, 2 * heads : 4 * heads] = pair_of(grown)
    live[...] = jnp.where(seg_row == before, 1.0, 0.0)
    passed = jnp.where(seg_last == before, jnp.exp(last), 0.0)
    carry[...] = pair_of(jnp.broadcast_to(passed, (2 * TILE, heads)))
    for copy in copies[4:9]:
        copy.wait()
    value = raw[...].astype(F32)
    for i in range(2):
        bc[:, i * inner : (i + 1) * inner] = value[:, i, :].astype(BF16)
    copies[9].wait()
    send_states(0, info[2], x, bc, wx, bx, wbc, bbc, moves, factor, carry, xc_out, (m0, m1, m2, m3), held)
    for copy in copies[10:]:
        copy.wait()


def other_kernel(g, info, x, bc, wx, bx, wbc, bbc, moves, factor, carry, xc_out, m0, m1, m2, m3, held):
    send_states(g, info[2], x, bc, wx, bx, wbc, bbc, moves, factor, carry, xc_out, (m0, m1, m2, m3), held)


def extra_of(msg):
    value = msg[STATE : STATE + EXTRA, :].astype(F32)
    return value[0:TILE], value[TILE:EXTRA]


def top_state(taps, here, prior):
    upper, lower = here
    total = pltpu.roll(upper, TILE - 2, 0)
    parts = pltpu.roll(lower, TILE - taps + 1, 0)
    btotal, ctotal = parts[:, 0:STATE], parts[:, 2 * STATE : 3 * STATE]
    if prior is not None:
        total = total + pltpu.roll(prior[0], TILE - 1 - taps, 0)
        parts = pltpu.roll(prior[1], TILE - taps + 1, 0)
        btotal, ctotal = btotal + parts[:, STATE : 2 * STATE], ctotal + parts[:, 3 * STATE : 4 * STATE]
    xc = silu_of_half(total).astype(BF16).astype(F32)
    xc = jnp.where(tokens(0, xc.shape, 0) < taps - 1, xc, 0.0)
    both = silu_of_half(jnp.concatenate([btotal, ctotal], axis=1))
    both = jnp.where(tokens(0, both.shape, 0) < taps - 1, both, 0.0)
    rows = jnp.concatenate([xc, jnp.concatenate([both, jnp.zeros_like(both)], axis=1)], axis=0).astype(BF16)
    scaled, bmat = xc * lower, both[:, 0:STATE]
    scaled = jnp.concatenate([scaled, jnp.zeros_like(scaled)], axis=0).astype(BF16)
    bmat = jnp.concatenate([bmat, jnp.zeros_like(bmat)], axis=0).astype(BF16)
    return lax.dot_general(bmat, scaled, (((0,), (0,)), ((), ())), preferred_element_type=F32), rows


def carry_row(extra):
    return extra[0][0:1] + extra[0][1:2]


def fold_kernel(taps, more, info, *refs):
    msgs, rest = refs[0:QUAD], refs[QUAD:]
    total, fixed = rest[more], rest[more + 1]
    for mine in range(QUAD):

        @pl.when(info[1] == mine)
        def _():
            block = [msgs[mine ^ b] for b in range(QUAD)]
            extra = [extra_of(msg) for msg in block]
            add, _ = top_state(taps, extra[0], extra_of(rest[0]) if more else None)
            state = block[0][0:STATE, :].astype(F32) + add
            through = carry_row(extra[0])
            for b in range(1, QUAD):
                add, rows = top_state(taps, extra[b], extra[b - 1])
                own = block[b][0:STATE, :].astype(F32) + add
                fixed[b - 1, 0:STATE, :] = own.astype(BF16)
                fixed[b - 1, STATE : STATE + EXTRA, :] = rows
                state = own + carry_row(extra[b]) * state
                through = through * carry_row(extra[b])
            total[0:STATE, :] = state.astype(BF16)
            total[STATE : STATE + EXTRA, :] = block[QUAD - 1][STATE : STATE + EXTRA, :]
            for out in rest[more + 2 :]:
                out[...] = jnp.broadcast_to(through, out.shape)


def enter_kernel(taps, info, start, fixed, m0, m1, m2, m3, o0, o1, o2, o3):
    msgs = (m0, m1, m2, m3)
    outs = (o0, o1, o2, o3)
    lower = slice(STATE, STATE + EXTRA)
    prior = extra_of(start)
    for mine in range(QUAD):

        @pl.when(info[1] == mine)
        def _():
            head = extra_of(msgs[mine])
            add, rows = top_state(taps, head, prior)
            outs[mine][0:STATE, :] = start[0:STATE, :]
            outs[mine][lower, :] = rows
            state = msgs[mine][0:STATE, :].astype(F32) + add
            state = state + carry_row(head) * start[0:STATE, :].astype(F32)
            for b in range(1, QUAD):
                outs[mine ^ b][0:STATE, :] = state.astype(BF16)
                outs[mine ^ b][lower, :] = fixed[b - 1, lower, :]
                if b < QUAD - 1:
                    own = fixed[b - 1, 0:STATE, :].astype(F32)
                    state = own + carry_row(extra_of(msgs[mine ^ b])) * state


def inner_kernel(g, xc_in, z_in, bc, wbc, bbc, moves, mask, factors, skip, near, gain, c_out, rate_top, kept_top, z, sem):
    wide = xc_in.shape[1]
    copy = pltpu.make_async_copy(z_in.at[:, g * wide : (g + 1) * wide], z, sem)
    copy.start()
    heads = skip.shape[1]
    taps = wbc.shape[0]
    lane = slice(g * STATE, (g + 1) * STATE)
    shift = moves[0 : (taps - 1) * BLOCK, :]

    def conv(which):
        base = which * wbc.shape[2] + g * STATE
        block = bc[:, base : base + STATE]
        half = conv_half(shift, block, block, bc_weight(which, lane, wbc), bbc[which : which + 1, lane])
        return silu_of_half(half).astype(BF16)

    cmat = conv(1)
    c_out[...] = cmat
    scores = lax.dot_general(cmat, conv(0), (((1,), (1,)), ((), ())), preferred_element_type=F32)
    scores = jnp.where(tokens(0, scores.shape, 1) < taps - 1, 0.0, scores * mask[...]).astype(BF16)
    skips = pair_of(jnp.broadcast_to(skip[...], (8, heads)))
    step = 1024
    copy.wait()
    for at in range(0, wide, step):
        lane = slice(at, at + step)
        onehot2 = twice(head_map(heads, (g * wide + at) // HEAD_DIM, step))
        xf = xc_in[:, lane].astype(F32)
        xf = jnp.where(tokens(0, xf.shape, 0) < taps - 1, 0.0, xf)
        rates = mm(factors[:, 0 : 2 * heads], onehot2)
        rate_top[:, lane] = rates[0:TILE]
        scaled = (xf * rates).astype(BF16)
        grown = mm(factors[:, 2 * heads : 4 * heads], onehot2)
        skip_c = mm(skips, onehot2)[0:1]
        gate = silu_of_half(z[:, lane].astype(F32) * 0.5)
        kept_top[:, lane] = skip_c * gate[0:TILE]
        near[:, lane] = (mm(scores, scaled) * grown + skip_c * xf) * gate
        gain[:, lane] = grown * gate


def finish_kernel(g, taps, info, near, gain, cmat, rate_top, kept_top, mask, live, scale, *rest):
    out, ready, held, sems = rest[-4:]
    mine = info[2]
    rows, wide = near.shape
    width = wide // QUAD
    steps = sems.shape[0]
    part = rows // steps
    square = [0.0] * steps
    ats = [pl.ds(pl.multiple_of((mine ^ k) * width, width), width) for k in range(QUAD)]
    first = rest[0][STATE : STATE + EXTRA, 0 : 2 * STATE].astype(F32)[TILE:EXTRA]
    c = cmat[...].astype(F32)
    top = jnp.where(tokens(0, (TILE, STATE), 0) < taps - 1, first[:, STATE:], c[0:TILE])
    c = jnp.concatenate([top, c[TILE:]], axis=0)
    bmat = jnp.concatenate([first[:, 0:STATE], jnp.zeros((TILE, STATE), F32)], axis=0).astype(BF16)
    scores = lax.dot_general(c.astype(BF16), bmat, (((1,), (1,)), ((), ())), preferred_element_type=F32)
    left = jnp.concatenate([c * live[...], scores * mask[:, 0 : 2 * TILE]], axis=1).astype(BF16)
    for at, e in zip(ats, rest):
        xc = e[STATE : STATE + EXTRA, :].astype(F32)[0:TILE]
        sent = jnp.concatenate([xc * rate_top[:, at], jnp.zeros_like(xc)], axis=0).astype(BF16)
        far = mm(left, jnp.concatenate([e[0:STATE, :], sent], axis=0))
        for i in range(steps):
            these = slice(i * part, (i + 1) * part)
            value = near[these, at] + gain[these, at] * far[these]
            if i == 0:
                value = value + jnp.concatenate([xc * kept_top[:, at], jnp.zeros((part - TILE, width), F32)], axis=0)
            square[i] = square[i] + jnp.sum(value * value, axis=1, keepdims=True)
            held[these, at] = value
    copies = []
    for i in range(steps):
        these = slice(i * part, (i + 1) * part)
        inv = lax.rsqrt(square[i] * (1.0 / wide) + 1e-05)
        ready[these, :] = (held[these, :] * inv * scale[:, g * wide : (g + 1) * wide]).astype(BF16)
        copy = pltpu.make_async_copy(ready.at[these, :], out.at[these, g * wide : (g + 1) * wide], sems.at[i])
        copy.start()
        copies.append(copy)
    for copy in copies:
        copy.wait()


SMEM = pl.BlockSpec(memory_space=pltpu.SMEM)
VMEM = pl.BlockSpec(memory_space=pltpu.VMEM)
ANY = pl.BlockSpec(memory_space=pl.ANY)
HBM = pl.BlockSpec(memory_space=pltpu.HBM)


def call(kernel, scalars, args, outs, flops, limit=32 << 20, **more):
    pinned = more.get("specs", ())
    args = [
        pltpu.with_memory_space_constraint(arg, pltpu.HBM) if i < len(pinned) and pinned[i] is HBM else arg
        for i, arg in enumerate(args)
    ]
    return pl.pallas_call(
        kernel,
        in_specs=[SMEM] * len(scalars) + more.pop("specs", [VMEM] * len(args)),
        out_specs=more.pop("out_specs", [VMEM] * len(outs)),
        out_shape=[jax.ShapeDtypeStruct(*out) for out in outs],
        cost_estimate=pl.CostEstimate(flops=flops, bytes_accessed=4 << 20, transcendentals=0),
        compiler_params=pltpu.CompilerParams(vmem_limit_bytes=limit),
        **more,
    )(*scalars, *args)


def tie(first, second):
    return lax.optimization_barrier((first, second))


def shards(
    x_in,
    z_in,
    bc_in,
    conv_x_weight,
    conv_x_bias,
    conv_bc_weight,
    conv_bc_bias,
    dt_raw,
    dt_bias,
    decay,
    skip_d,
    norm_gain,
    lengths,
):
    rows, chan = x_in.shape
    heads = dt_raw.shape[1]
    peers = lax.axis_size("seq")
    shard = lax.axis_index("seq").astype(jnp.int32)
    taps = conv_x_weight.shape[0]
    bcw = bc_in.shape[2]
    groups = bcw // STATE
    wide = chan // groups
    width = wide // QUAD
    reach = peers // 2 // QUAD

    bx = conv_x_bias.reshape(1, chan)
    scale = norm_gain.reshape(1, chan)
    owner = (shard % QUAD) ^ (shard // QUAD % 2 * 2)
    info = jnp.stack([shard, shard % QUAD, owner])

    def swap(values):
        routes = [[(i, i ^ k) for i in range(peers)] for k in range(QUAD)]
        swapped = {k: lax.ppermute(values[k], "seq", routes[k]) for k in (3, 1, 2)}
        return [values[0], swapped[1], swapped[2], swapped[3]]

    def ahead(value):
        return lax.ppermute(value, "seq", [(i, i + QUAD ^ 2) for i in range(peers - QUAD)])

    first_args = [
        lengths, x_in, bc_in, conv_x_weight, bx, dt_raw.T, dt_bias.reshape(1, heads), decay.reshape(1, heads),
        conv_bc_weight, conv_bc_bias, skip_d.reshape(1, heads), scale,
    ]
    sent = ((STATE + EXTRA, width), BF16)
    held = pltpu.VMEM((STATE + EXTRA, wide), BF16)
    x, bc, moves, mask, live, factors, factor, carry, wx, bx, wbc, bbc, skip, scale, xc, *msg = call(
        first_kernel,
        [info],
        first_args,
        [
            ((rows, chan), BF16),
            ((rows, 2 * bcw), BF16),
            (((taps - 1) * (BLOCK + 2 * TILE), BLOCK), BF16),
            ((BLOCK, BLOCK), F32),
            ((BLOCK, BLOCK), F32),
            ((rows, 4 * heads), BF16),
            ((rows, 2 * heads), BF16),
            ((2 * TILE, 2 * heads), BF16),
            ((taps, chan), BF16),
            ((1, chan), F32),
            ((taps, 2, bcw), BF16),
            ((2, bcw), F32),
            ((1, heads), F32),
            ((1, chan), F32),
            ((rows, wide), BF16),
            *[sent] * QUAD,
        ],
        600_000_000,
        specs=[HBM] * len(first_args),
        scratch_shapes=[
            pltpu.SMEM(lengths.shape, jnp.int32),
            pltpu.VMEM((rows, 2, bcw), BF16),
            pltpu.VMEM((heads, rows), BF16),
            pltpu.VMEM((1, heads), F32),
            pltpu.VMEM((1, heads), F32),
            held,
            pltpu.SemaphoreType.DMA((13,)),
        ],
    )
    xcs, msgs = [xc], [swap(msg)]
    for g in range(1, groups):
        xc, *msg = call(
            functools.partial(other_kernel, g),
            [info],
            [x, bc, wx, bx, wbc, bbc, moves, factor, carry],
            [((rows, wide), BF16), *[sent] * QUAD],
            300_000_000,
            scratch_shapes=[held],
        )
        xcs.append(xc)
        msgs.append(swap(msg))

    local = []
    for g in range(groups):
        args = [xcs[g], z_in, bc, wbc, bbc, moves, mask, factors, skip]
        outs = [((rows, wide), F32)] * 2 + [((rows, STATE), BF16)] + [((TILE, wide), F32)] * 2
        near = call(
            functools.partial(inner_kernel, g),
            [],
            args,
            outs,
            300_000_000,
            specs=[HBM if arg is z_in else VMEM for arg in args],
            scratch_shapes=[pltpu.VMEM((rows, wide), BF16), pltpu.SemaphoreType.DMA],
        )
        local.append(list(near))
    msgs[-1][0], local[0][0] = tie(msgs[-1][0], local[0][0])

    entering, fixes = [], []
    for g in range(groups):
        outs = [sent, ((QUAD - 1, STATE + EXTRA, width), BF16)]
        args = list(msgs[g])
        if reach > 1:
            outs.append(((8, width), F32))
            args.append(ahead(lax.dynamic_index_in_dim(jnp.stack(args), shard % QUAD ^ (QUAD - 1), 0, False)))
        total, fixed, *through = call(
            functools.partial(fold_kernel, taps, len(args) - QUAD), (info,), args, outs, 1_000_000
        )
        state = ahead(total)
        for _ in range(reach - 1):
            own = total[0:STATE].astype(F32) + through[0][0:1] * state[0:STATE].astype(F32)
            state = ahead(jnp.concatenate([own.astype(BF16), total[STATE:]], axis=0))
        entering.append(state)
        fixes.append(fixed)

    blocks = []
    for g in range(groups):
        outs = [sent] * QUAD
        kernel = functools.partial(enter_kernel, taps)
        blocks.append(swap(call(kernel, (info,), [entering[g], fixes[g], *msgs[g]], outs, 1_000_000)))

    blocks[0][1], local[-1][0] = tie(blocks[0][1], local[-1][0])

    out = None
    for g in range(groups):
        args = [*local[g], mask, live, scale, *blocks[g]]
        specs = [VMEM] * len(args)
        aliases = {}
        if out is not None:
            aliases = {1 + len(args): 0}
            args.append(out)
            specs.append(ANY)
        (out,) = call(
            functools.partial(finish_kernel, g, taps),
            (info,),
            args,
            [((rows, chan), BF16)],
            100_000_000,
            specs=specs,
            out_specs=[ANY],
            scratch_shapes=[
                pltpu.VMEM((rows, wide), BF16),
                pltpu.VMEM((rows, wide), F32),
                pltpu.SemaphoreType.DMA((4,)),
            ],
            input_output_aliases=aliases,
        )
    return out


def solution(mesh):
    return jax.shard_map(
        shards,
        mesh=mesh,
        in_specs=(
            P(("groups", "seq"), "heads"),
            P(("groups", "seq"), "heads"),
            P(("groups", "seq"), None, "heads"),
            P(None, "heads"),
            P("heads"),
            P(None, None, "heads"),
            P(None, "heads"),
            P(("groups", "seq"), "heads"),
            P("heads"),
            P("heads"),
            P("heads"),
            P("heads"),
            P("groups"),
        ),
        out_specs=P(("groups", "seq"), "heads"),
        check_vma=False,
    )
```
